32 devices in a mesh: segment: 4 (over y, x), dp: 2 (over core), tensor: 4 (over z).
Axes of the slice: x: 2, y: 2, z: 4, core: 2. Of those that a mesh axis runs over, the one named last changes fastest.
Arguments:
- text_embed: bfloat16 [2, 2048, 8192], P('dp', 'segment', 'tensor'), may hold values from -6 to 6
- crop_feats: bfloat16 [4, 2, 1, 256, 1280], P('segment', 'dp'), may hold values from -6 to 6
- crop_dest: int32 [4, 2, 1], P('segment'), may hold values from 0 to 1, as said below
- vision_gain: bfloat16 [1280], replicated, may hold values from 0.5 to 1.5
- proj_weight: bfloat16 [1280, 8192], P(None, 'tensor'), may hold values from -0.15625 to 0.15625
- newline: bfloat16 [8192], P('tensor'), may hold values from -6 to 6
- norm_gain: bfloat16 [8192], P('tensor'), may hold values from 0.5 to 1.5
- xz_weight: bfloat16 [8192, 2048], P('tensor', 'dp'), may hold values from -0.0625 to 0.0625
- dt_weight: bfloat16 [8192, 8], P('tensor', 'dp'), may hold values from -0.0625 to 0.0625
- bc_weight: bfloat16 [8192, 512], P('tensor', 'dp'), may hold values from -0.0625 to 0.0625
- conv_x: bfloat16 [4, 1024], P(None, ('dp', 'tensor')), may hold values from -3 to 3
- conv_bc: bfloat16 [4, 512], P(None, 'dp'), may hold values from -3 to 3
- dt_bias: float32 [8], P(('dp', 'tensor')), may hold values from -6 to -2
- a_log: float32 [8], P(('dp', 'tensor')), may hold values from -4 to 1
- skip: float32 [8], P(('dp', 'tensor')), may hold values from 0.5 to 1.5
- out_gain: bfloat16 [1024], P(('dp', 'tensor')), may hold values from 0.5 to 1.5
- out_weight: bfloat16 [1024, 8192], P('dp', 'tensor'), may hold values from -0.1875 to 0.1875
Outputs:
- hidden_out: bfloat16 [2, 2048, 8192], P('dp', 'segment', 'tensor')
The draws below stay inside these ranges and needn't reach their ends.
Inputs may be any that keep to these rules, and one draw needn't show every extreme that they name: `crop_dest`: in each section, the 1 crops of one encoder rank go to different sequences, at most 1 crops go to one sequence, and in every section some sequence receives exactly 1.
All inputs are finite; a program needn't handle non-finite values.
Results may differ from the reference program's by a relative error of at most 0.015.
Values may be sent and summed in bfloat16 or wider, within the bound.
No kernel may reach another device: no remote copies, remote signals or barrier semaphores. Data moves between devices by JAX's collectives and lax.ppermute only.
A program may use at most 128 MiB of HBM per device.

```python
import jax
import jax.numpy as jnp
from jax import lax

D = 8192
VD = 1280
HEAD_DIM = 128
STATE = 128
CONV = 4
CROP_ROWS = 256
CROPS_DEV = 1
MAXC = 1
SEC = 512
GROUP_HEADS = 4
HEADS = 8
INNER = 1024
SEQ = 2048
N_SEGMENT = 4
N_DP = 2
N_TENSOR = 4


def draw_crop_dest(key, part):
    slot_total = N_DP * MAXC
    chosen_total = N_DP * CROPS_DEV

    def one_segment(segment_key):
        key_busy, key_scores, key_labels = jax.random.split(segment_key, 3)
        busy = jax.random.randint(key_busy, (), 0, N_DP, dtype=jnp.int32)
        scores = jax.random.permutation(key_scores, slot_total).astype(jnp.int32)
        slot_owner = jnp.arange(slot_total, dtype=jnp.int32) // MAXC
        scores = scores + jnp.where(slot_owner == busy, slot_total, 0).astype(jnp.int32)
        _, chosen = lax.top_k(scores, chosen_total)
        chosen = jnp.sort(chosen.astype(jnp.int32))
        owners = chosen // MAXC
        labels = jax.random.permutation(key_labels, N_DP).astype(jnp.int32)
        owners = labels[owners]
        return owners.reshape(CROPS_DEV, N_DP).T
    segment_keys = jax.random.split(key, N_SEGMENT)
    return jax.vmap(one_segment)(segment_keys).astype(jnp.int32)


def levels(stream_key, dims, cuts, low, largest):
    loudness, own = 1.0, jax.random.fold_in(stream_key, 6)
    for position, parts in cuts:
        heights = jnp.exp(jax.random.uniform(jax.random.fold_in(own, position), (parts,), jnp.float32, low / len(cuts), largest / len(cuts)))
        loudness = loudness * jnp.repeat(heights, dims[position] // parts).reshape([-1 if axis == position else 1 for axis in range(len(dims))])
    return loudness


def bell_draw(key, extent, width, limit, cuts=(), kind=jnp.bfloat16):
    values = jax.random.normal(key, extent, jnp.float32) * width
    if len(cuts) > 0:
        values = levels(key, extent, cuts, -0.22, 0.18) * values
    return jnp.clip(values, min=-limit, max=limit).astype(kind)


def setup_inputs(seed: int = 0) -> dict:
    seeds = jax.random.split(jax.random.key(seed), 18)
    text_embed = bell_draw(seeds[0], (N_DP, SEQ, D), 1.0, 6.0, ((0, 2), (1, 4), (2, 4)))
    crop_feats = bell_draw(seeds[1], (N_SEGMENT, N_DP, CROPS_DEV, CROP_ROWS, VD), 1.0, 6.0, ((0, 4), (1, 2)))
    crop_dest = draw_crop_dest(jax.random.fold_in(seeds[17], 71), 0)
    vision_gain = jnp.clip(1.0 + 0.1 * jax.random.normal(seeds[3], (VD,), jnp.float32), 0.5, 1.5).astype(jnp.bfloat16)
    proj_weight = bell_draw(seeds[4], (VD, D), VD ** -0.5, 0.15625, ((1, 4),))
    newline = bell_draw(seeds[5], (D,), 1.0, 6.0, ((0, 4),))
    norm_gain = jnp.clip(1.0 + 0.1 * jax.random.normal(seeds[6], (D,), jnp.float32), 0.5, 1.5).astype(jnp.bfloat16)
    xz_weight = bell_draw(seeds[7], (D, 2 * INNER), D ** -0.5, 0.0625, ((0, 4), (1, 2)))
    dt_weight = bell_draw(seeds[8], (D, HEADS), D ** -0.5, 0.0625, ((0, 4), (1, 2)))
    bc_weight = bell_draw(seeds[9], (D, 2 * N_DP * STATE), D ** -0.5, 0.0625, ((0, 4), (1, 2)))
    conv_x = bell_draw(seeds[10], (CONV, INNER), CONV ** -0.5, 3.0, ((1, 8),))
    conv_bc = bell_draw(seeds[11], (CONV, 2 * N_DP * STATE), CONV ** -0.5, 3.0, ((1, 2),))
    dt_bias = jnp.clip(-6.0 + 4.0 * jax.random.uniform(seeds[12], (HEADS,), jnp.float32) ** levels(seeds[12], (HEADS,), ((0, 8),), -0.2, 0.2), -6.0, -2.0)
    a_log = jnp.clip(-4.0 + 5.0 * jax.random.uniform(seeds[13], (HEADS,), jnp.float32) ** levels(seeds[13], (HEADS,), ((0, 8),), -0.2, 0.2), -4.0, 1.0)
    skip = jnp.clip(0.5 + 1.0 * jax.random.uniform(seeds[14], (HEADS,), jnp.float32) ** levels(seeds[14], (HEADS,), ((0, 8),), -0.2, 0.2), 0.5, 1.5)
    out_gain = jnp.clip(1.0 + 0.1 * jax.random.normal(seeds[15], (INNER,), jnp.float32), 0.5, 1.5).astype(jnp.bfloat16)
    out_weight = bell_draw(seeds[16], (INNER, D), INNER ** -0.5, 0.1875, ((0, 2), (1, 4)))
    return dict(text_embed=text_embed, crop_feats=crop_feats, crop_dest=crop_dest, vision_gain=vision_gain, proj_weight=proj_weight, newline=newline, norm_gain=norm_gain, xz_weight=xz_weight, dt_weight=dt_weight, bc_weight=bc_weight, conv_x=conv_x, conv_bc=conv_bc, dt_bias=dt_bias, a_log=a_log, skip=skip, out_gain=out_gain, out_weight=out_weight)


def causal_filter(signal, kernel):
    widths = ((0, 0), (CONV - 1, 0)) + ((0, 0),) * (signal.ndim - 2)
    padded = jnp.pad(signal, widths)
    result = kernel[0] * padded[:, 0:SEQ]
    for offset in range(1, CONV):
        result = result + kernel[offset] * padded[:, offset:offset + SEQ]
    return result

def project_blocks(normed, weight):
    quarter = D // N_TENSOR
    total = jnp.zeros((normed.shape[0], weight.shape[1]), jnp.float32)
    for block_id in range(N_TENSOR):
        partial_term = jnp.dot(normed[:, block_id * quarter:(block_id + 1) * quarter], weight[block_id * quarter:(block_id + 1) * quarter], preferred_element_type=jnp.float32)
        total = total + lax.optimization_barrier(partial_term.astype(jnp.bfloat16)).astype(jnp.float32)
    return total

def reference(text_embed, crop_feats, crop_dest, vision_gain, proj_weight, newline, norm_gain, xz_weight, dt_weight, bc_weight, conv_x, conv_bc, dt_bias, a_log, skip, out_gain, out_weight):
    highest = lax.Precision.HIGHEST
    eps = 1e-05
    crop_span = CROP_ROWS + 1
    feats = crop_feats.astype(jnp.float32)
    vision = (feats * lax.rsqrt(lax.optimization_barrier(jnp.mean(feats * feats, -1, keepdims=True)) + eps) * vision_gain.astype(jnp.float32)).astype(jnp.bfloat16)
    encoded = jnp.dot(vision.reshape(-1, VD), proj_weight, preferred_element_type=jnp.float32)
    encoded = encoded.astype(jnp.bfloat16).reshape(N_SEGMENT, N_DP, CROPS_DEV, CROP_ROWS, D)
    targets = jnp.arange(N_DP, dtype=jnp.int32)
    hits = crop_dest[:, :, :, None] == targets[None, None, None, :]
    valid = jnp.any(hits, axis=2).astype(jnp.int32)
    crop_of = lax.optimization_barrier(jnp.sum(jnp.where(hits, jnp.arange(CROPS_DEV, dtype=jnp.int32)[None, None, :, None], 0), axis=2))
    order = jnp.cumsum(valid, axis=1) - valid
    counted = lax.optimization_barrier(jnp.sum(valid, axis=1))
    positions = jnp.arange(SEC, dtype=jnp.int32)
    block = positions // crop_span
    within = positions % crop_span
    matched = (valid[:, :, :, None] == 1) & (order[:, :, :, None] == block[None, None, None, :])
    source = lax.optimization_barrier(jnp.sum(jnp.where(matched, targets[None, :, None, None], 0), axis=1))
    which_crop = lax.optimization_barrier(jnp.sum(jnp.where(matched, crop_of[:, :, :, None], 0), axis=1))
    segment_ids = jnp.arange(N_SEGMENT, dtype=jnp.int32)[:, None, None]
    crop_row = jnp.minimum(within, CROP_ROWS - 1)[None, None, :]
    picked = encoded[segment_ids, source, which_crop, crop_row]
    image = block[None, None, :] < counted[:, :, None]
    crop_pos = image & (within[None, None, :] < CROP_ROWS)
    line_pos = image & (within[None, None, :] == CROP_ROWS)
    text = text_embed.reshape(N_DP, N_SEGMENT, SEC, D).transpose(1, 0, 2, 3)
    sections = jnp.where(crop_pos[..., None], picked, jnp.where(line_pos[..., None], newline[None, None, None, :], text))
    hidden = sections.transpose(1, 0, 2, 3).reshape(N_DP, SEQ, D)
    wide = hidden.astype(jnp.float32)
    normed = (wide * lax.rsqrt(lax.optimization_barrier(jnp.mean(wide * wide, -1, keepdims=True)) + eps) * norm_gain.astype(jnp.float32)).astype(jnp.bfloat16).reshape(N_DP * SEQ, D)
    pairs = project_blocks(normed, xz_weight).reshape(N_DP, SEQ, HEADS, 2, HEAD_DIM)
    step_raw = project_blocks(normed, dt_weight).reshape(N_DP, SEQ, HEADS)
    maps_raw = project_blocks(normed, bc_weight).reshape(N_DP, SEQ, N_DP, 2 * STATE)
    values = pairs[:, :, :, 0, :]
    gates = pairs[:, :, :, 1, :]
    kernel_x = conv_x.astype(jnp.float32).reshape(CONV, HEADS, HEAD_DIM)
    kernel_b = conv_bc.astype(jnp.float32).reshape(CONV, N_DP, 2 * STATE)
    streams = jax.nn.silu(causal_filter(values, kernel_x))
    maps = jax.nn.silu(causal_filter(maps_raw, kernel_b))
    b_map = maps[..., :STATE]
    c_map = maps[..., STATE:]
    step = jax.nn.softplus(step_raw + dt_bias.astype(jnp.float32))
    log_decay = -jnp.exp(a_log.astype(jnp.float32)) * step

    def split_sections(array):
        shaped = array.reshape((N_DP, N_SEGMENT, SEC) + array.shape[2:])
        return jnp.moveaxis(shaped, 1, 0)
    lower = positions[:, None] >= positions[None, :]

    def section_step(prior, inputs):
        x_sec, b_sec, c_sec, s_sec, l_sec = inputs
        cumulative = jnp.cumsum(l_sec, axis=1)
        b_head = jnp.repeat(b_sec, GROUP_HEADS, axis=2)
        c_head = jnp.repeat(c_sec, GROUP_HEADS, axis=2)
        scores = jnp.einsum('nlhs,nmhs->nlmh', c_head, b_head, precision=highest)
        gaps = cumulative[:, :, None, :] - cumulative[:, None, :, :]
        mask = lower[None, :, :, None]
        weights = jnp.where(mask, jnp.exp(jnp.where(mask, gaps, 0.0)), 0.0) * scores * s_sec[:, None, :, :]
        inside = jnp.einsum('nlmh,nmhp->nlhp', weights, x_sec, precision=highest)
        across = jnp.exp(cumulative)[..., None] * jnp.einsum('nlhs,nhsp->nlhp', c_head, prior, precision=highest)
        final = cumulative[:, -1, :]
        carry_weight = jnp.exp(final[:, None, :] - cumulative) * s_sec
        local_state = jnp.einsum('nlh,nlhs,nlhp->nhsp', carry_weight, b_head, x_sec, precision=highest)
        following = jnp.exp(final)[:, :, None, None] * prior + local_state
        return (following, inside + across)
    start_state = jnp.zeros((N_DP, HEADS, STATE, HEAD_DIM), jnp.float32)
    _, pieces = lax.scan(section_step, start_state, (split_sections(streams), split_sections(b_map), split_sections(c_map), split_sections(step), split_sections(log_decay)))
    mixer_y = jnp.moveaxis(pieces, 0, 1).reshape(N_DP, SEQ, HEADS, HEAD_DIM)
    outputs = mixer_y + skip.astype(jnp.float32)[None, None, :, None] * streams
    gated = outputs * jax.nn.silu(gates)
    group_width = GROUP_HEADS * HEAD_DIM
    grouped = gated.reshape(N_DP, SEQ, N_DP, group_width)
    normed_out = (grouped * lax.rsqrt(lax.optimization_barrier(jnp.mean(grouped * grouped, -1, keepdims=True)) + eps) * out_gain.astype(jnp.float32).reshape(N_DP, group_width)).astype(jnp.bfloat16)
    normed_out = normed_out.reshape(N_DP * SEQ, N_DP, group_width)
    mixed = jnp.zeros((N_DP * SEQ, D), jnp.float32)
    for group in range(N_DP):
        partial_term = jnp.dot(normed_out[:, group], out_weight[group * group_width:(group + 1) * group_width], preferred_element_type=jnp.float32)
        mixed = mixed + lax.optimization_barrier(partial_term.astype(jnp.bfloat16)).astype(jnp.float32)
    result = wide.reshape(N_DP * SEQ, D) + mixed
    return result.astype(jnp.bfloat16).reshape(N_DP, SEQ, D)
```

```python
import jax
import jax.numpy as jnp
from jax import lax
from jax.experimental import pallas as pl
from jax.experimental.pallas import tpu as pltpu
from jax.sharding import PartitionSpec as P

EPS = 1e-05
F32 = jnp.float32
BF16 = jnp.bfloat16
HIGHEST = lax.Precision.HIGHEST


def passed_along(block, axis, distance):
    devices = range(lax.axis_size(axis))
    route = [(i - distance, i) for i in devices if i - distance in devices]
    return lax.ppermute(block, axis, route)


def swapped(block, axis, bits):
    return lax.ppermute(block, axis, [(i, i ^ bits) for i in range(lax.axis_size(axis))])


def per_device_any(
    text_embed,
    crop_feats,
    crop_dest,
    vision_gain,
    proj_weight,
    newline,
    norm_gain,
    xz_weight,
    dt_weight,
    bc_weight,
    conv_x,
    conv_bc,
    dt_bias,
    a_log,
    skip,
    out_gain,
    out_weight,
):
    highest = lax.Precision.HIGHEST
    eps = 1e-05
    dp_count = lax.axis_size("dp")
    tp_count = lax.axis_size("tensor")
    segment_count = lax.axis_size("segment")
    my_rank = lax.axis_index("dp")
    section = text_embed.shape[1]
    columns = text_embed.shape[2]
    crop_count = crop_feats.shape[2]
    crop_rows = crop_feats.shape[3]
    crop_span = crop_rows + 1
    heads_dev = dt_bias.shape[0]
    head_width = out_gain.shape[0] // heads_dev
    state_size = bc_weight.shape[1] // 2
    feats = crop_feats[0, 0].astype(jnp.float32)
    vision = (
        feats
        * lax.rsqrt(jnp.mean(feats * feats, -1, keepdims=True) + eps)
        * vision_gain.astype(jnp.float32)
    ).astype(jnp.bfloat16)
    encoded = jnp.dot(
        vision.reshape(crop_count * crop_rows, -1), proj_weight, preferred_element_type=jnp.float32
    )
    encoded = encoded.astype(jnp.bfloat16).reshape(crop_count, crop_rows, columns)
    table = crop_dest[0]
    sources = jnp.arange(dp_count, dtype=jnp.int32)
    mine = jnp.sum(jnp.where(sources[:, None] == my_rank, table, 0), axis=0)
    chosen = mine[None, :] == sources[:, None]
    outgoing = jnp.einsum(
        "dc,crq->drq", chosen.astype(jnp.bfloat16), encoded, preferred_element_type=jnp.float32
    ).astype(jnp.bfloat16)
    incoming = lax.all_to_all(outgoing, "dp", split_axis=0, concat_axis=0, tiled=True)
    sent_rows = incoming.shape[1]
    valid = jnp.any(table == my_rank, axis=1).astype(jnp.int32)
    order = jnp.cumsum(valid) - valid
    counted = jnp.sum(valid)
    positions = jnp.arange(section, dtype=jnp.int32)
    block = positions // crop_span
    within = positions % crop_span
    slot_ids = jnp.arange(section // crop_span + 1, dtype=jnp.int32)
    matched = (valid[None, :] == 1) & (order[None, :] == slot_ids[:, None])
    slot_source = jnp.sum(jnp.where(matched, sources[None, :], 0), axis=1)
    row_source = jnp.sum(
        jnp.where(block[:, None] == slot_ids[None, :], slot_source[None, :], 0), axis=1
    )
    row_index = row_source * sent_rows + jnp.minimum(within, sent_rows - 1)
    picked = jnp.take(incoming.reshape(dp_count * sent_rows, columns), row_index, axis=0)
    image = block < counted
    text = text_embed[0]
    crop_pos = image & (within < crop_rows)
    line_pos = image & (within == crop_rows)
    hidden = jnp.where(
        crop_pos[:, None], picked, jnp.where(line_pos[:, None], newline[None, :], text)
    )
    wide = hidden.astype(jnp.float32)
    row_total = lax.psum(jnp.sum(wide * wide, -1), "tensor")
    normed = (
        wide
        * lax.rsqrt(row_total / (columns * tp_count) + eps)[:, None]
        * norm_gain.astype(jnp.float32)
    ).astype(jnp.bfloat16)
    pair_cols = xz_weight.shape[1]
    step_cols = dt_weight.shape[1]
    piece = lax.all_gather(normed, "dp", axis=0, tiled=True)
    terms = jnp.concatenate(
        [
            jnp.dot(piece, xz_weight, preferred_element_type=jnp.float32),
            jnp.dot(piece, dt_weight, preferred_element_type=jnp.float32),
            jnp.dot(piece, bc_weight, preferred_element_type=jnp.float32),
        ],
        axis=1,
    )
    pair_mine, step_mine = (
        lax.psum_scatter(
            terms[:, :pair_cols].astype(jnp.bfloat16), "tensor", scatter_dimension=1, tiled=True
        ).astype(jnp.float32),
        lax.psum_scatter(
            terms[:, pair_cols : pair_cols + step_cols].astype(jnp.bfloat16),
            "tensor",
            scatter_dimension=1,
            tiled=True,
        ).astype(jnp.float32),
    )
    map_terms = terms[:, pair_cols + step_cols :]
    maps_all = lax.psum(map_terms.astype(jnp.bfloat16), "tensor").astype(jnp.float32)
    pairs = pair_mine.reshape(dp_count, section, heads_dev, 2, head_width)
    values = pairs[:, :, :, 0, :].reshape(dp_count, section, heads_dev * head_width)
    gates = pairs[:, :, :, 1, :]
    fresh = jnp.concatenate([values, maps_all.reshape(dp_count, section, 2 * state_size)], axis=2)
    kernel = jnp.concatenate([conv_x, conv_bc], axis=1).astype(jnp.float32)
    taps = kernel.shape[0]
    edge = passed_along(fresh[:, section - (taps - 1) :, :], "segment", 1)
    padded = jnp.concatenate([edge, fresh], axis=1)
    filtered = kernel[0] * padded[:, 0:section]
    for offset in range(1, taps):
        filtered = filtered + kernel[offset] * padded[:, offset : offset + section]
    activated = jax.nn.silu(filtered)
    inner_cols = heads_dev * head_width
    streams = activated[..., :inner_cols].reshape(dp_count, section, heads_dev, head_width)
    b_rows = activated[..., inner_cols : inner_cols + state_size]
    c_rows = activated[..., inner_cols + state_size :]
    step = jax.nn.softplus(step_mine.reshape(dp_count, section, heads_dev) + dt_bias)
    cumulative = jnp.cumsum(-jnp.exp(a_log) * step, axis=1)
    scores = jnp.einsum("nls,nms->nlm", c_rows, b_rows, precision=highest)
    mask = (positions[:, None] >= positions[None, :])[None, :, :, None]
    gaps = cumulative[:, :, None, :] - cumulative[:, None, :, :]
    weights = (
        jnp.where(mask, jnp.exp(jnp.where(mask, gaps, 0.0)), 0.0)
        * scores[..., None]
        * step[:, None, :, :]
    )
    inside = jnp.einsum("nlmh,nmhp->nlhp", weights, streams, precision=highest)
    final = cumulative[:, -1, :]
    carry_weight = jnp.exp(final[:, None, :] - cumulative) * step
    local_state = jnp.einsum("nlh,nls,nlhp->nhsp", carry_weight, b_rows, streams, precision=highest)
    decay = jnp.exp(final)
    prior = jnp.zeros_like(local_state)
    for turn in range(segment_count - 1):
        prior = passed_along(
            (decay[:, :, None, None] * prior + local_state).astype(jnp.bfloat16), "segment", 1
        ).astype(jnp.float32)
    across = jnp.exp(cumulative)[..., None] * jnp.einsum(
        "nls,nhsp->nlhp", c_rows, prior, precision=highest
    )
    outputs = inside + across + skip[None, None, :, None] * streams
    gated = outputs * jax.nn.silu(gates)
    group_total = lax.psum(jnp.sum(gated * gated, axis=(2, 3)), "tensor")
    scale = lax.rsqrt(group_total / (inner_cols * tp_count) + eps)
    normed_out = (
        gated * scale[..., None, None] * out_gain.astype(jnp.float32).reshape(heads_dev, head_width)
    ).astype(jnp.bfloat16)
    normed_out = normed_out.reshape(dp_count * section, inner_cols)
    term = jnp.dot(
        lax.all_gather(normed_out, "tensor", axis=1, tiled=True),
        out_weight,
        preferred_element_type=jnp.float32,
    )
    mixed = lax.psum_scatter(
        term.astype(jnp.bfloat16), "dp", scatter_dimension=0, tiled=True
    ).astype(jnp.float32)
    return (wide + mixed).astype(jnp.bfloat16)[None]


def contract(a, b, dims, precision=None):
    return lax.dot_general(
        a, b, (dims, ((), ())), precision=precision, preferred_element_type=F32
    )


def eye(n):
    return (
        lax.broadcasted_iota(jnp.int32, (n, n), 0) == lax.broadcasted_iota(jnp.int32, (n, n), 1)
    ).astype(F32)


def columns_of(rows):
    return contract(eye(rows.shape[1]), rows, ((1,), (1,)), HIGHEST)


def silu(a):
    return a / (1.0 + jnp.exp(-a))


def encode_body(place, mine, other, gain, weight, out, normed):
    rows = mine.shape[0]

    @pl.when(pl.program_id(0) == 0)
    def _():
        stays = place[0] == 1
        for index, (a, b) in enumerate(((mine, other), (other, mine))):
            feats = jnp.where(stays, a[...], b[...]).astype(F32)
            scale = lax.rsqrt(jnp.mean(feats * feats, -1, keepdims=True) + EPS)
            normed[index * rows : (index + 1) * rows, :] = (
                feats * scale * gain[...].astype(F32)
            ).astype(BF16)

    out[...] = jnp.dot(normed[...], weight[...], preferred_element_type=F32).astype(BF16)


def encode(place, mine, other, gain, weight):
    rows, width = mine.shape
    columns = weight.shape[1]
    tile = columns // 4
    return pl.pallas_call(
        encode_body,
        grid=(4,),
        in_specs=[
            pl.BlockSpec(memory_space=pltpu.SMEM),
            pl.BlockSpec((rows, width), lambda i: (0, 0)),
            pl.BlockSpec((rows, width), lambda i: (0, 0)),
            pl.BlockSpec((1, width), lambda i: (0, 0)),
            pl.BlockSpec((width, tile), lambda i: (0, i)),
        ],
        out_specs=pl.BlockSpec((2 * rows, tile), lambda i: (0, i)),
        out_shape=jax.ShapeDtypeStruct((2 * rows, columns), BF16),
        scratch_shapes=[pltpu.VMEM((2 * rows, width), BF16)],
        name="encode",
    )(place, mine, other, gain, weight)


def project_body(
    crops, text_mine, text_other, edge_mine, edge_other, newline, gain, xz, bc, dt, first, second,
    rows, meta,
):
    half = text_mine.shape[0]
    step = pl.program_id(0)

    @pl.when(step == 0)
    def _():
        scale = gain[...].astype(F32)
        top = lax.broadcasted_iota(jnp.int32, (half, 1), 0) == 0
        line = newline[...].astype(F32)
        pick = (
            lax.broadcasted_iota(jnp.int32, (8, 128), 0)
            == lax.broadcasted_iota(jnp.int32, (8, 128), 1)
        ).astype(F32)
        lane = lax.broadcasted_iota(jnp.int32, (half + 16, 128), 1)
        for part in range(4):
            base = (part // 2) * half
            if part % 2 == 0:
                main = crops[base : base + half, :].astype(F32)
                edge = (edge_mine, edge_other)[part // 2][...].astype(F32)
            else:
                main = (text_mine, text_other)[part // 2][...].astype(F32)
                main = jnp.where(top, line, main)
                edge = crops[base + half - 16 : base + half, :].astype(F32)[8:]
            rows[part, 0:half, :] = (main * scale).astype(BF16)
            rows[part, half : half + 16, :] = jnp.concatenate(
                [edge * scale, jnp.zeros_like(edge)], 0
            ).astype(BF16)
            squares = jnp.concatenate(
                [
                    jnp.sum(main * main, -1, keepdims=True),
                    jnp.sum(edge * edge, -1, keepdims=True),
                    jnp.zeros((8, 1), F32),
                ],
                0,
            )
            steps = jnp.dot(rows[part], dt[...], preferred_element_type=F32)
            both = jnp.where(lane == 4, squares, steps)
            across = contract(pick, both, ((1,), (1,)), HIGHEST).astype(BF16)
            meta[part, 0] = across[:, 0:128]
            meta[part, 1] = across[:, 128:256]
            meta[part, 2] = jnp.concatenate(
                [across[:, half : half + 16], jnp.zeros((8, 112), BF16)], 1
            )
            meta[part, 3] = jnp.zeros((8, 128), BF16)
            meta[part, 4] = jnp.zeros((8, 128), BF16)

    def write(weight):
        for part in range(4):
            result = jnp.dot(rows[part], weight, preferred_element_type=F32).astype(BF16)
            first[part, 0 : half + 8, :] = result[0 : half + 8, 0:128]
            first[part, half + 8 : half + 16, :] = meta[part, step]
            second[part] = result[0 : half + 8, 128:256]

    @pl.when(step < 4)
    def _():
        write(xz[...])

    @pl.when(step == 4)
    def _():
        write(bc[...])


def project(crops, text, text_other, edge_mine, edge_other, newline, gain, xz, bc, dt):
    section, columns = text.shape
    half = section // 2
    return pl.pallas_call(
        project_body,
        grid=(5,),
        in_specs=[
            pl.BlockSpec((2 * half, columns), lambda i: (0, 0)),
            pl.BlockSpec((half, columns), lambda i: (1, 0)),
            pl.BlockSpec((half, columns), lambda i: (0, 0)),
            pl.BlockSpec((8, columns), lambda i: (0, 0)),
            pl.BlockSpec((8, columns), lambda i: (0, 0)),
            pl.BlockSpec((1, columns), lambda i: (0, 0)),
            pl.BlockSpec((1, columns), lambda i: (0, 0)),
            pl.BlockSpec((columns, 256), lambda i: (0, jnp.minimum(i, 3))),
            pl.BlockSpec((columns, 256), lambda i: (0, 0)),
            pl.BlockSpec((columns, 128), lambda i: (0, 0)),
        ],
        out_specs=[
            pl.BlockSpec((4, half + 16, 128), lambda i: (0, 0, i)),
            pl.BlockSpec((4, half + 8, 128), lambda i: (0, 0, i)),
        ],
        out_shape=[
            jax.ShapeDtypeStruct((4, half + 16, 640), BF16),
            jax.ShapeDtypeStruct((4, half + 8, 640), BF16),
        ],
        scratch_shapes=[
            pltpu.VMEM((4, half + 16, columns), BF16),
            pltpu.VMEM((4, 5, 8, 128), BF16),
        ],
        name="project",
    )(crops, text, text_other, edge_mine, edge_other, newline, gain, xz, bc, dt)


def filtered(main, edge, taps):
    rows = main.shape[0]
    padded = jnp.concatenate([edge, main], 0)
    count = taps.shape[0]
    total = taps[count - 1 : count] * main
    for back in range(1, count):
        total = total + taps[count - 1 - back : count - back] * padded[8 - back : 8 - back + rows]
    return total


def scan_body(width, first, params, taps_b, streams, maps, meta, state):
    half = first.shape[0] - 16
    sums = first[half : half + 16, 0 : half + 128].astype(F32)[8:16]
    scale = lax.rsqrt(sums[4:5] / width + EPS)
    head = lax.broadcasted_iota(jnp.int32, (8, 512), 1) // 128
    owner = (head == lax.broadcasted_iota(jnp.int32, (8, 512), 0)).astype(F32)
    scalars = params[5:8, :]
    bias = jnp.sum(owner * scalars[0:1], 1, keepdims=True) * (1.0 / 128)
    rate = jnp.sum(owner * scalars[1:2], 1, keepdims=True) * (1.0 / 128)
    raw = sums[:, 0:half] * scale[:, 0:half] + bias
    step = jnp.maximum(raw, 0.0) + jnp.log1p(jnp.exp(-jnp.abs(raw)))
    decays = -jnp.exp(rate) * step
    upper = (
        lax.broadcasted_iota(jnp.int32, (half, half), 0)
        <= lax.broadcasted_iota(jnp.int32, (half, half), 1)
    ).astype(F32)
    cumulative = contract(decays, upper, ((1,), (0,)), HIGHEST)
    final = cumulative[:, half - 1 : half]
    carry = jnp.exp(final - cumulative) * step
    scale_main = columns_of(jnp.broadcast_to(scale[:, 0:half], (8, half)))[:, 0:1]
    scale_edge = columns_of(jnp.broadcast_to(scale[:, half : half + 128], (8, 128)))[0:8, 0:1]
    taps_x = params[0:4, :]
    edge = first[half : half + 16, :].astype(F32)[0:8] * scale_edge
    x = silu(filtered(first[0:half, 0:512].astype(F32) * scale_main, edge[:, 0:512], taps_x))
    b = silu(
        filtered(
            first[0:half, 512:640].astype(F32) * scale_main, edge[:, 512:640], taps_b[...].astype(F32)
        )
    )
    carried = contract(columns_of(carry), owner, ((1,), (0,)), HIGHEST)
    b16 = b.astype(BF16)
    state[0:128, :] = contract(b16, (x * carried).astype(BF16), ((0,), (0,))).astype(BF16)
    total = jnp.sum(jnp.exp(final) * owner, 0, keepdims=True)
    state[128:144, :] = jnp.broadcast_to(total, (16, 512)).astype(BF16)
    streams[...] = x.astype(BF16)
    maps[...] = b16
    meta[0:8, 0:half] = cumulative
    meta[8:16, 0:half] = step
    meta[16:24, 0:half] = jnp.broadcast_to(scale[:, 0:half], (8, half))
    meta[0:8, half : half + 128] = jnp.broadcast_to(scale[:, half : half + 128], (8, 128))


def scan(width, first, params, taps_b):
    half = first.shape[0] - 16
    return pl.pallas_call(
        lambda *refs: scan_body(width, *refs),
        out_shape=[
            jax.ShapeDtypeStruct((half, 512), BF16),
            jax.ShapeDtypeStruct((half, 128), BF16),
            jax.ShapeDtypeStruct((24, half + 128), F32),
            jax.ShapeDtypeStruct((144, 512), BF16),
        ],
        name="scan",
    )(first, params, taps_b)


def mix_body(second, streams, maps, meta, prior, params, taps_c, out):
    half = streams.shape[0]
    cumulative = meta[0:8, 0:half]
    step = meta[8:16, 0:half]
    cum_cols = columns_of(cumulative)
    scale_main = columns_of(meta[16:24, 0:half])[:, 0:1]
    scale_edge = columns_of(meta[0:8, half : half + 128])[0:8, 0:1]
    both = second[half - 8 : half + 8, 512:640].astype(F32)[8:16] * scale_edge
    c = silu(
        filtered(second[0:half, 512:640].astype(F32) * scale_main, both, taps_c[...].astype(F32))
    ).astype(BF16)
    scores = contract(c, maps[...], ((1,), (1,)))
    lower = lax.broadcasted_iota(jnp.int32, (half, half), 0) >= lax.broadcasted_iota(
        jnp.int32, (half, half), 1
    )
    across = jnp.dot(c, prior[...].astype(BF16), preferred_element_type=F32)
    gated = []
    squares = jnp.zeros((half, 1), F32)
    for head in range(4):
        cols = slice(128 * head, 128 * head + 128)
        x = streams[:, cols]
        gaps = cum_cols[:, head : head + 1] - cumulative[head : head + 1]
        weights = (
            jnp.where(lower, jnp.exp(jnp.where(lower, gaps, 0.0)), 0.0)
            * scores
            * step[head : head + 1]
        )
        y = jnp.dot(weights.astype(BF16), x, preferred_element_type=F32)
        y = y + jnp.exp(cum_cols[:, head : head + 1]) * across[:, cols]
        y = y + params[7:8, cols] * x.astype(F32)
        value = y * silu(second[0:half, cols].astype(F32) * scale_main)
        squares = squares + jnp.sum(value * value, -1, keepdims=True)
        gated.append(value)
    norm = lax.rsqrt(squares / 512 + EPS)
    for head in range(4):
        cols = slice(128 * head, 128 * head + 128)
        out[:, cols] = (gated[head] * norm * params[4:5, cols]).astype(BF16)


def mix(second, streams, maps, meta, prior, params, taps_c):
    return pl.pallas_call(
        mix_body,
        out_shape=jax.ShapeDtypeStruct(streams.shape, BF16),
        name="mix",
    )(second, streams, maps, meta, prior, params, taps_c)


def output_body(gathered, weight_mine, weight_other, crops, text, newline, out):
    half = crops.shape[0]
    top = lax.broadcasted_iota(jnp.int32, (half, 1), 0) == 0
    tail = jnp.where(top, newline[...].astype(F32), text[...].astype(F32))
    for index, hidden in enumerate((crops[...].astype(F32), tail)):
        mixed = jnp.dot(gathered[index], weight_mine[...], preferred_element_type=F32)
        mixed = mixed + jnp.dot(
            gathered[2 + index], weight_other[...], preferred_element_type=F32
        )
        out[index * half : (index + 1) * half, :] = (hidden + mixed).astype(BF16)


def output(gathered, weight_mine, weight_other, crops, text, newline):
    section, columns = text.shape
    half = section // 2
    tile = columns // 4
    inner = gathered.shape[2]
    return pl.pallas_call(
        output_body,
        grid=(4,),
        in_specs=[
            pl.BlockSpec((4, half, inner), lambda i: (0, 0, 0)),
            pl.BlockSpec((inner, tile), lambda i: (0, i)),
            pl.BlockSpec((inner, tile), lambda i: (0, i)),
            pl.BlockSpec((half, tile), lambda i: (0, i)),
            pl.BlockSpec((half, tile), lambda i: (1, i)),
            pl.BlockSpec((1, tile), lambda i: (0, i)),
        ],
        out_specs=pl.BlockSpec((section, tile), lambda i: (0, i)),
        out_shape=jax.ShapeDtypeStruct((section, columns), BF16),
        name="output",
    )(gathered, weight_mine, weight_other, crops, text, newline)


def per_device_halves(
    text_embed, crop_feats, crop_dest, vision_gain, proj_weight, newline, norm_gain, xz_weight,
    dt_weight, bc_weight, conv_x, conv_bc, dt_bias, a_log, skip, out_gain, out_weight,
):
    my_rank = lax.axis_index("dp")
    my_chip = lax.axis_index("tensor")
    my_segment = lax.axis_index("segment")
    segment_count = lax.axis_size("segment")
    text = text_embed[0]
    section, columns = text.shape
    half = section // 2
    width = columns * lax.axis_size("tensor")
    state_size = bc_weight.shape[1] // 2
    feats = crop_feats[0, 0, 0]
    feats_other = swapped(feats, "dp", 1)
    text_other = swapped(text[half:], "dp", 1)
    edge_mine = passed_along(text[section - 8 :], "segment", 1)
    edge_other = swapped(edge_mine, "dp", 1)
    weight_other = swapped(out_weight, "dp", 1)
    stays = jnp.where(my_rank == 0, crop_dest[0, 0, 0] == 0, crop_dest[0, 1, 0] == 1)
    crops = encode(
        stays.astype(jnp.int32).reshape(1), feats, feats_other, vision_gain[None], proj_weight
    )
    dt_wide = jnp.pad(dt_weight, ((0, 0), (0, 128 - dt_weight.shape[1])))
    first, second = project(
        crops, text, text_other, edge_mine, edge_other, newline[None], norm_gain[None], xz_weight,
        bc_weight, dt_wide,
    )
    own = jnp.concatenate(
        [conv_x.astype(F32), out_gain.astype(F32)[None]]
        + [jnp.broadcast_to(value[:, None], (1, 128)) for value in (dt_bias, a_log, skip)],
        0,
    )
    own, first = lax.optimization_barrier((own, first))
    params = lax.all_gather(own, "tensor", axis=1, tiled=True)
    first = lax.psum_scatter(first, "tensor", scatter_dimension=0, tiled=False)
    second = lax.psum_scatter(second, "tensor", scatter_dimension=0, tiled=False)
    streams, maps, meta, state = scan(width, first, params, conv_bc[:, :state_size])
    partner = swapped(state, "tensor", 1).astype(F32)
    state = state.astype(F32)
    late = my_chip % 2 == 1
    early_state = jnp.where(late, partner, state)[:128]
    late_state = jnp.where(late, state, partner)[:128]
    early_decay = jnp.where(late, partner, state)[128:129]
    late_decay = jnp.where(late, state, partner)[128:129]
    whole = jnp.concatenate(
        [
            late_decay * early_state + late_state,
            jnp.broadcast_to(early_decay * late_decay, (16, 512)),
        ],
        0,
    ).astype(BF16)
    others = [None] + [swapped(whole, "segment", bits) for bits in range(1, segment_count)]
    prior = jnp.zeros((128, 512), F32)
    for source in range(segment_count - 1):
        bits = my_segment ^ source
        piece = others[1]
        for index in range(2, segment_count):
            piece = jnp.where(bits == index, others[index], piece)
        piece = piece.astype(F32)
        prior = jnp.where(source < my_segment, piece[128:129] * prior + piece[:128], prior)
    prior = jnp.where(late, early_decay * prior + early_state, prior)
    normed = mix(second, streams, maps, meta, prior, params, conv_bc[:, state_size:])
    normed = jnp.where(my_chip < 2, normed, swapped(normed, "dp", 1))
    gathered = lax.all_gather(normed, "tensor", axis=0, tiled=False)
    return output(gathered, out_weight, weight_other, crops, text, newline[None])[None]


def per_device(*args):
    text_embed, crop_feats = args[0], args[1]
    sizes = tuple(lax.axis_size(axis) for axis in ("segment", "dp", "tensor"))
    heads_dev = args[12].shape[0]
    head_width = args[15].shape[0] // heads_dev
    state_size = args[9].shape[1] // 2
    fits = (
        sizes == (4, 2, 4)
        and heads_dev == 1
        and (head_width, state_size) == (128, 128)
        and crop_feats.shape[2:4] == (1, 256)
        and text_embed.shape[1] == 512
    )
    return (per_device_halves if fits else per_device_any)(*args)


def solution(mesh):
    return jax.shard_map(
        per_device,
        mesh=mesh,
        in_specs=(
            P("dp", "segment", "tensor"),
            P("segment", "dp", None, None, None),
            P("segment", None, None),
            P(),
            P(None, "tensor"),
            P("tensor"),
            P("tensor"),
            P("tensor", "dp"),
            P("tensor", "dp"),
            P("tensor", "dp"),
            P(None, ("dp", "tensor")),
            P(None, "dp"),
            P(("dp", "tensor")),
            P(("dp", "tensor")),
            P(("dp", "tensor")),
            P(("dp", "tensor")),
            P("dp", "tensor"),
        ),
        out_specs=P("dp", "segment", "tensor"),
        check_vma=False,
    )
```

```python
import jax
import jax.numpy as jnp
from jax import lax
from jax.experimental import pallas as pl
from jax.experimental.pallas import tpu as pltpu
from jax.sharding import PartitionSpec as P

EPS = 1e-05
F32 = jnp.float32
BF16 = jnp.bfloat16
HIGHEST = lax.Precision.HIGHEST


def passed_along(block, axis, distance):
    devices = range(lax.axis_size(axis))
    route = [(i - distance, i) for i in devices if i - distance in devices]
    return lax.ppermute(block, axis, route)


def swapped(block, axis, bits):
    return lax.ppermute(block, axis, [(i, i ^ bits) for i in range(lax.axis_size(axis))])


def per_device_any(
    text_embed,
    crop_feats,
    crop_dest,
    vision_gain,
    proj_weight,
    newline,
    norm_gain,
    xz_weight,
    dt_weight,
    bc_weight,
    conv_x,
    conv_bc,
    dt_bias,
    a_log,
    skip,
    out_gain,
    out_weight,
):
    highest = lax.Precision.HIGHEST
    eps = 1e-05
    dp_count = lax.axis_size("dp")
    tp_count = lax.axis_size("tensor")
    segment_count = lax.axis_size("segment")
    my_rank = lax.axis_index("dp")
    section = text_embed.shape[1]
    columns = text_embed.shape[2]
    crop_count = crop_feats.shape[2]
    crop_rows = crop_feats.shape[3]
    crop_span = crop_rows + 1
    heads_dev = dt_bias.shape[0]
    head_width = out_gain.shape[0] // heads_dev
    state_size = bc_weight.shape[1] // 2
    feats = crop_feats[0, 0].astype(jnp.float32)
    vision = (
        feats
        * lax.rsqrt(jnp.mean(feats * feats, -1, keepdims=True) + eps)
        * vision_gain.astype(jnp.float32)
    ).astype(jnp.bfloat16)
    encoded = jnp.dot(
        vision.reshape(crop_count * crop_rows, -1), proj_weight, preferred_element_type=jnp.float32
    )
    encoded = encoded.astype(jnp.bfloat16).reshape(crop_count, crop_rows, columns)
    table = crop_dest[0]
    sources = jnp.arange(dp_count, dtype=jnp.int32)
    mine = jnp.sum(jnp.where(sources[:, None] == my_rank, table, 0), axis=0)
    chosen = mine[None, :] == sources[:, None]
    outgoing = jnp.einsum(
        "dc,crq->drq", chosen.astype(jnp.bfloat16), encoded, preferred_element_type=jnp.float32
    ).astype(jnp.bfloat16)
    incoming = lax.all_to_all(outgoing, "dp", split_axis=0, concat_axis=0, tiled=True)
    sent_rows = incoming.shape[1]
    valid = jnp.any(table == my_rank, axis=1).astype(jnp.int32)
    order = jnp.cumsum(valid) - valid
    counted = jnp.sum(valid)
    positions = jnp.arange(section, dtype=jnp.int32)
    block = positions // crop_span
    within = positions % crop_span
    slot_ids = jnp.arange(section // crop_span + 1, dtype=jnp.int32)
    matched = (valid[None, :] == 1) & (order[None, :] == slot_ids[:, None])
    slot_source = jnp.sum(jnp.where(matched, sources[None, :], 0), axis=1)
    row_source = jnp.sum(
        jnp.where(block[:, None] == slot_ids[None, :], slot_source[None, :], 0), axis=1
    )
    row_index = row_source * sent_rows + jnp.minimum(within, sent_rows - 1)
    picked = jnp.take(incoming.reshape(dp_count * sent_rows, columns), row_index, axis=0)
    image = block < counted
    text = text_embed[0]
    crop_pos = image & (within < crop_rows)
    line_pos = image & (within == crop_rows)
    hidden = jnp.where(
        crop_pos[:, None], picked, jnp.where(line_pos[:, None], newline[None, :], text)
    )
    wide = hidden.astype(jnp.float32)
    row_total = lax.psum(jnp.sum(wide * wide, -1), "tensor")
    normed = (
        wide
        * lax.rsqrt(row_total / (columns * tp_count) + eps)[:, None]
        * norm_gain.astype(jnp.float32)
    ).astype(jnp.bfloat16)
    pair_cols = xz_weight.shape[1]
    step_cols = dt_weight.shape[1]
    piece = lax.all_gather(normed, "dp", axis=0, tiled=True)
    terms = jnp.concatenate(
        [
            jnp.dot(piece, xz_weight, preferred_element_type=jnp.float32),
            jnp.dot(piece, dt_weight, preferred_element_type=jnp.float32),
            jnp.dot(piece, bc_weight, preferred_element_type=jnp.float32),
        ],
        axis=1,
    )
    pair_mine, step_mine = (
        lax.psum_scatter(
            terms[:, :pair_cols].astype(jnp.bfloat16), "tensor", scatter_dimension=1, tiled=True
        ).astype(jnp.float32),
        lax.psum_scatter(
            terms[:, pair_cols : pair_cols + step_cols].astype(jnp.bfloat16),
            "tensor",
            scatter_dimension=1,
            tiled=True,
        ).astype(jnp.float32),
    )
    map_terms = terms[:, pair_cols + step_cols :]
    maps_all = lax.psum(map_terms.astype(jnp.bfloat16), "tensor").astype(jnp.float32)
    pairs = pair_mine.reshape(dp_count, section, heads_dev, 2, head_width)
    values = pairs[:, :, :, 0, :].reshape(dp_count, section, heads_dev * head_width)
    gates = pairs[:, :, :, 1, :]
    fresh = jnp.concatenate([values, maps_all.reshape(dp_count, section, 2 * state_size)], axis=2)
    kernel = jnp.concatenate([conv_x, conv_bc], axis=1).astype(jnp.float32)
    taps = kernel.shape[0]
    edge = passed_along(fresh[:, section - (taps - 1) :, :], "segment", 1)
    padded = jnp.concatenate([edge, fresh], axis=1)
    filtered = kernel[0] * padded[:, 0:section]
    for offset in range(1, taps):
        filtered = filtered + kernel[offset] * padded[:, offset : offset + section]
    activated = jax.nn.silu(filtered)
    inner_cols = heads_dev * head_width
    streams = activated[..., :inner_cols].reshape(dp_count, section, heads_dev, head_width)
    b_rows = activated[..., inner_cols : inner_cols + state_size]
    c_rows = activated[..., inner_cols + state_size :]
    step = jax.nn.softplus(step_mine.reshape(dp_count, section, heads_dev) + dt_bias)
    cumulative = jnp.cumsum(-jnp.exp(a_log) * step, axis=1)
    scores = jnp.einsum("nls,nms->nlm", c_rows, b_rows, precision=highest)
    mask = (positions[:, None] >= positions[None, :])[None, :, :, None]
    gaps = cumulative[:, :, None, :] - cumulative[:, None, :, :]
    weights = (
        jnp.where(mask, jnp.exp(jnp.where(mask, gaps, 0.0)), 0.0)
        * scores[..., None]
        * step[:, None, :, :]
    )
    inside = jnp.einsum("nlmh,nmhp->nlhp", weights, streams, precision=highest)
    final = cumulative[:, -1, :]
    carry_weight = jnp.exp(final[:, None, :] - cumulative) * step
    local_state = jnp.einsum("nlh,nls,nlhp->nhsp", carry_weight, b_rows, streams, precision=highest)
    decay = jnp.exp(final)
    prior = jnp.zeros_like(local_state)
    for turn in range(segment_count - 1):
        prior = passed_along(
            (decay[:, :, None, None] * prior + local_state).astype(jnp.bfloat16), "segment", 1
        ).astype(jnp.float32)
    across = jnp.exp(cumulative)[..., None] * jnp.einsum(
        "nls,nhsp->nlhp", c_rows, prior, precision=highest
    )
    outputs = inside + across + skip[None, None, :, None] * streams
    gated = outputs * jax.nn.silu(gates)
    group_total = lax.psum(jnp.sum(gated * gated, axis=(2, 3)), "tensor")
    scale = lax.rsqrt(group_total / (inner_cols * tp_count) + eps)
    normed_out = (
        gated * scale[..., None, None] * out_gain.astype(jnp.float32).reshape(heads_dev, head_width)
    ).astype(jnp.bfloat16)
    normed_out = normed_out.reshape(dp_count * section, inner_cols)
    term = jnp.dot(
        lax.all_gather(normed_out, "tensor", axis=1, tiled=True),
        out_weight,
        preferred_element_type=jnp.float32,
    )
    mixed = lax.psum_scatter(
        term.astype(jnp.bfloat16), "dp", scatter_dimension=0, tiled=True
    ).astype(jnp.float32)
    return (wide + mixed).astype(jnp.bfloat16)[None]


def contract(a, b, dims, precision=None):
    return lax.dot_general(
        a, b, (dims, ((), ())), precision=precision, preferred_element_type=F32
    )


def eye(n):
    return (
        lax.broadcasted_iota(jnp.int32, (n, n), 0) == lax.broadcasted_iota(jnp.int32, (n, n), 1)
    ).astype(F32)


def columns_of(rows):
    return contract(eye(rows.shape[1]), rows, ((1,), (1,)), HIGHEST)


def silu(a):
    return a / (1.0 + jnp.exp(-a))


def enter_body(
    table, feats_mine, feats_other, vision_gain, proj, text, text_other, edge_mine, edge_other,
    newline, gain, xz, bc, dt, crops_out, first_out, second_out,
    feats, normed, proj_tiles, tails, weights, crops, rows, first, second, sems, out_sems,
):
    half = tails.shape[1]
    span = half + 16
    tiles, _, tile = proj_tiles.shape
    arrivals = [
        pltpu.make_async_copy(feats_mine, feats.at[0], sems.at[0]),
        pltpu.make_async_copy(feats_other, feats.at[1], sems.at[1]),
    ]
    arrivals += [
        pltpu.make_async_copy(proj.at[:, pl.ds(i * tile, tile)], proj_tiles.at[i], sems.at[2 + i])
        for i in range(tiles)
    ]
    arrivals += [
        pltpu.make_async_copy(text.at[pl.ds(half, half), :], tails.at[0], sems.at[2 + tiles]),
        pltpu.make_async_copy(text_other, tails.at[1], sems.at[3 + tiles]),
        pltpu.make_async_copy(bc, weights.at[4], sems.at[4 + tiles]),
    ]
    arrivals += [
        pltpu.make_async_copy(
            xz.at[:, pl.ds(i * 256, 256)], weights.at[i], sems.at[5 + tiles + i]
        )
        for i in range(4)
    ]
    for copy in arrivals:
        copy.start()
    gain_row = gain[...].reshape(1, -1)
    rank = lax.axis_index("dp")
    stays = table[0, rank, 0] == rank
    arrivals[0].wait()
    arrivals[1].wait()
    for index in range(2):
        block = jnp.where(stays, feats[index], feats[1 - index]).astype(F32)
        scale = lax.rsqrt(jnp.mean(block * block, -1, keepdims=True) + EPS)
        normed[index * half : (index + 1) * half, :] = (
            block * scale * vision_gain[...].reshape(1, -1).astype(F32)
        ).astype(BF16)
    departures = []
    for i in range(tiles):
        arrivals[2 + i].wait()
        cols = slice(i * tile, (i + 1) * tile)
        result = jnp.dot(normed[...], proj_tiles[i], preferred_element_type=F32).astype(BF16)
        crops[:, cols] = result
        scaled = result * gain_row[:, cols]
        rows[0:half, cols] = scaled[:half]
        rows[2 * span : 2 * span + half, cols] = scaled[half:]
    departures.append(pltpu.make_async_copy(crops, crops_out, out_sems.at[0]))
    departures[-1].start()
    top = lax.broadcasted_iota(jnp.int32, (8, 1), 0) == 0
    ones = jnp.ones((8, rows.shape[1]), BF16)
    sums = []
    for part in range(4):
        index = part // 2
        base = part * span
        if part % 2 == 0:
            main = crops[index * half : (index + 1) * half, :]
            edge = (edge_mine, edge_other)[index][...]
        else:
            arrivals[2 + tiles + index].wait()
            head = tails[index, 0:8, :].astype(F32)
            line = newline[...].reshape(1, -1).astype(F32)
            tails[index, 0:8, :] = jnp.where(top, line, head).astype(BF16)
            main = tails[index]
            rows[base : base + half, :] = main * gain_row
            edge = crops[(index + 1) * half - 8 : (index + 1) * half, :]
        wide = edge.astype(F32)
        last = jnp.concatenate([wide, jnp.zeros_like(wide)], 0).astype(BF16)
        rows[base + half : base + span, :] = last * gain_row
        sums.append(
            jnp.concatenate(
                [
                    contract(ones, main * main, ((1,), (1,))),
                    contract(ones, last * last, ((1,), (1,))),
                ],
                1,
            )
        )
    for i in (4, 0, 1, 2, 3):
        arrivals[5 + tiles + i if i < 4 else 4 + tiles].wait()
        result = jnp.dot(rows[...], weights[i], preferred_element_type=F32).astype(BF16)
        for part in range(4):
            block = result[part * span : (part + 1) * span]
            if i == 4:
                first[part, :, 512:768] = block
            else:
                cols = slice(128 * i, 128 * i + 128)
                first[part, :, cols] = block[:, 0:128]
                second[part, :, cols] = block[0:half, 128:256]
    for part in range(4):
        steps = contract(dt[...], rows[part * span : (part + 1) * span, :], ((1,), (1,)))
        both = jnp.concatenate([steps[0:4], sums[part][4:8]], 0)
        first[part, half + 8 : span, 0:span] = both.astype(BF16)
    for source, target, i in ((first, first_out, 1), (second, second_out, 2)):
        departures.append(pltpu.make_async_copy(source, target, out_sems.at[i]))
        departures[-1].start()
    for copy in departures:
        copy.wait()


def enter(
    table, feats_mine, feats_other, vision_gain, proj, text, text_other, edge_mine, edge_other,
    newline, gain, xz, bc, dt,
):
    half, vision = feats_mine.shape
    columns = text.shape[1]
    tiles = 4
    whole = pl.BlockSpec(memory_space=pl.ANY)
    near = pl.BlockSpec(memory_space=pltpu.VMEM)
    return pl.pallas_call(
        enter_body,
        in_specs=[pl.BlockSpec(memory_space=pltpu.SMEM), whole, whole, near, whole, whole, whole]
        + [near, near, near, near, whole, whole, near],
        out_specs=[whole, whole, whole],
        out_shape=[
            jax.ShapeDtypeStruct((2 * half, columns), BF16),
            jax.ShapeDtypeStruct((4, half + 16, 768), BF16),
            jax.ShapeDtypeStruct((4, half, 512), BF16),
        ],
        scratch_shapes=[
            pltpu.VMEM((2, half, vision), BF16),
            pltpu.VMEM((2 * half, vision), BF16),
            pltpu.VMEM((tiles, vision, columns // tiles), BF16),
            pltpu.VMEM((2, half, columns), BF16),
            pltpu.VMEM((5, columns, 256), BF16),
            pltpu.VMEM((2 * half, columns), BF16),
            pltpu.VMEM((4 * (half + 16), columns), BF16),
            pltpu.VMEM((4, half + 16, 768), BF16),
            pltpu.VMEM((4, half, 512), BF16),
            pltpu.SemaphoreType.DMA((9 + tiles,)),
            pltpu.SemaphoreType.DMA((3,)),
        ],
        name="enter",
    )(
        table, feats_mine, feats_other, vision_gain, proj, text, text_other, edge_mine, edge_other,
        newline, gain, xz, bc, dt,
    )


def filtered(main, edge, taps):
    rows = main.shape[0]
    padded = jnp.concatenate([edge, main], 0)
    count = taps.shape[0]
    total = taps[count - 1 : count] * main
    for back in range(1, count):
        total = total + taps[count - 1 - back : count - back] * padded[8 - back : 8 - back + rows]
    return total


def scan_body(width, first, params, taps_maps, streams, maps, meta, state):
    half = first.shape[0] - 16
    sums = first[half : half + 16, 0 : half + 128].astype(F32)[8:16]
    scale = lax.rsqrt(sums[4:5] / width + EPS)
    head = lax.broadcasted_iota(jnp.int32, (8, 512), 1) // 128
    owner = (head == lax.broadcasted_iota(jnp.int32, (8, 512), 0)).astype(F32)
    scalars = params[5:8, :]
    bias = jnp.sum(owner * scalars[0:1], 1, keepdims=True) * (1.0 / 128)
    rate = jnp.sum(owner * scalars[1:2], 1, keepdims=True) * (1.0 / 128)
    raw = sums[:, 0:half] * scale[:, 0:half] + bias
    step = jnp.maximum(raw, 0.0) + jnp.log1p(jnp.exp(-jnp.abs(raw)))
    decays = -jnp.exp(rate) * step
    upper = (
        lax.broadcasted_iota(jnp.int32, (half, half), 0)
        <= lax.broadcasted_iota(jnp.int32, (half, half), 1)
    ).astype(F32)
    cumulative = contract(decays, upper, ((1,), (0,)), HIGHEST)
    final = cumulative[:, half - 1 : half]
    carry = jnp.exp(final - cumulative) * step
    scale_main = columns_of(jnp.broadcast_to(scale[:, 0:half], (8, half)))[:, 0:1]
    scale_edge = columns_of(jnp.broadcast_to(scale[:, half : half + 128], (8, 128)))[0:8, 0:1]
    taps_x = params[0:4, :]
    edge = first[half : half + 16, :].astype(F32)[0:8] * scale_edge
    x = silu(filtered(first[0:half, 0:512].astype(F32) * scale_main, edge[:, 0:512], taps_x))
    both = silu(
        filtered(
            first[0:half, 512:768].astype(F32) * scale_main,
            edge[:, 512:768],
            taps_maps[...].astype(F32),
        )
    ).astype(BF16)
    carried = contract(columns_of(carry), owner, ((1,), (0,)), HIGHEST)
    state[0:128, :] = contract(both[:, 0:128], (x * carried).astype(BF16), ((0,), (0,))).astype(BF16)
    total = jnp.sum(jnp.exp(final) * owner, 0, keepdims=True)
    state[128:144, :] = jnp.broadcast_to(total, (16, 512)).astype(BF16)
    streams[...] = x.astype(BF16)
    maps[...] = both
    meta[0:8, :] = cumulative
    meta[8:16, :] = step
    meta[16:24, :] = jnp.broadcast_to(scale[:, 0:half], (8, half))


def scan(width, first, params, taps_maps):
    half = first.shape[0] - 16
    return pl.pallas_call(
        lambda *refs: scan_body(width, *refs),
        out_shape=[
            jax.ShapeDtypeStruct((half, 512), BF16),
            jax.ShapeDtypeStruct((half, 256), BF16),
            jax.ShapeDtypeStruct((24, half), F32),
            jax.ShapeDtypeStruct((144, 512), BF16),
        ],
        name="scan",
    )(first, params, taps_maps)


def inside_body(streams, maps, meta, params, out):
    half = streams.shape[0]
    cumulative = meta[0:8, :]
    step = meta[8:16, :]
    cum_cols = columns_of(cumulative)
    scores = contract(maps[:, 128:256], maps[:, 0:128], ((1,), (1,)))
    lower = lax.broadcasted_iota(jnp.int32, (half, half), 0) >= lax.broadcasted_iota(
        jnp.int32, (half, half), 1
    )
    scores = jnp.where(lower, scores, 0.0)
    for head in range(4):
        cols = slice(128 * head, 128 * head + 128)
        x = streams[:, cols]
        gaps = cum_cols[:, head : head + 1] - cumulative[head : head + 1]
        weights = jnp.exp(jnp.where(lower, gaps, 0.0)) * scores * step[head : head + 1]
        y = jnp.dot(weights.astype(BF16), x, preferred_element_type=F32)
        out[:, cols] = y + params[7:8, cols] * x.astype(F32)


def inside(streams, maps, meta, params):
    return pl.pallas_call(
        inside_body,
        out_shape=jax.ShapeDtypeStruct(streams.shape, F32),
        name="inside",
    )(streams, maps, meta, params)


def gate_body(second, local, maps, meta, prior, params, out):
    half = local.shape[0]
    scale = columns_of(meta[16:24, :])[:, 0:1]
    entry = jnp.exp(columns_of(meta[0:8, :]))
    across = jnp.dot(maps[:, 128:256], prior[...].astype(BF16), preferred_element_type=F32)
    gated = []
    squares = jnp.zeros((half, 1), F32)
    for head in range(4):
        cols = slice(128 * head, 128 * head + 128)
        y = local[:, cols] + entry[:, head : head + 1] * across[:, cols]
        value = y * silu(second[:, cols].astype(F32) * scale)
        squares = squares + jnp.sum(value * value, -1, keepdims=True)
        gated.append(value)
    norm = lax.rsqrt(squares / 512 + EPS)
    for head in range(4):
        cols = slice(128 * head, 128 * head + 128)
        out[:, cols] = (gated[head] * norm * params[4:5, cols]).astype(BF16)


def gate(second, local, maps, meta, prior, params):
    return pl.pallas_call(
        gate_body,
        out_shape=jax.ShapeDtypeStruct(local.shape, BF16),
        name="gate",
    )(second, local, maps, meta, prior, params)


def output_body(gathered, weight_mine, weight_other, crops, text, newline, out):
    half = crops.shape[0]
    top = lax.broadcasted_iota(jnp.int32, (half, 1), 0) == 0
    tail = jnp.where(top, newline[...].reshape(1, -1).astype(F32), text[...].astype(F32))
    for index, hidden in enumerate((crops[...].astype(F32), tail)):
        mixed = jnp.dot(gathered[index], weight_mine[...], preferred_element_type=F32)
        mixed = mixed + jnp.dot(
            gathered[2 + index], weight_other[...], preferred_element_type=F32
        )
        out[index * half : (index + 1) * half, :] = (hidden + mixed).astype(BF16)


def output(gathered, weight_mine, weight_other, crops, text, newline):
    section, columns = text.shape
    half = section // 2
    tile = columns // 4
    inner = gathered.shape[2]
    return pl.pallas_call(
        output_body,
        grid=(4,),
        in_specs=[
            pl.BlockSpec((4, half, inner), lambda i: (0, 0, 0)),
            pl.BlockSpec((inner, tile), lambda i: (0, i)),
            pl.BlockSpec((inner, tile), lambda i: (0, i)),
            pl.BlockSpec((half, tile), lambda i: (0, i)),
            pl.BlockSpec((half, tile), lambda i: (1, i)),
            pl.BlockSpec((tile,), lambda i: (i,)),
        ],
        out_specs=pl.BlockSpec((section, tile), lambda i: (0, i)),
        out_shape=jax.ShapeDtypeStruct((section, columns), BF16),
        name="output",
    )(gathered, weight_mine, weight_other, crops, text, newline)


def per_device_halves(
    text_embed, crop_feats, crop_dest, vision_gain, proj_weight, newline, norm_gain, xz_weight,
    dt_weight, bc_weight, conv_x, conv_bc, dt_bias, a_log, skip, out_gain, out_weight,
):
    my_chip = lax.axis_index("tensor")
    my_segment = lax.axis_index("segment")
    segment_count = lax.axis_size("segment")
    text = text_embed[0]
    section, columns = text.shape
    half = section // 2
    width = columns * lax.axis_size("tensor")
    feats = crop_feats[0, 0, 0]
    feats_other = swapped(feats, "dp", 1)
    text_other = swapped(text[half:], "dp", 1)
    edge_mine = passed_along(text[section - 8 :], "segment", 1)
    edge_other = swapped(edge_mine, "dp", 1)
    weight_other = swapped(out_weight, "dp", 1)
    crops, first, second = enter(
        crop_dest, feats, feats_other, vision_gain, proj_weight, text, text_other, edge_mine,
        edge_other, newline, norm_gain, xz_weight, bc_weight, dt_weight.T,
    )
    own = jnp.concatenate(
        [conv_x.astype(F32), out_gain.astype(F32)[None]]
        + [jnp.broadcast_to(value[:, None], (1, 128)) for value in (dt_bias, a_log, skip)],
        0,
    )
    own, first = lax.optimization_barrier((own, first))
    params = lax.all_gather(own, "tensor", axis=1, tiled=True)
    first = lax.psum_scatter(first, "tensor", scatter_dimension=0, tiled=False)
    second = lax.psum_scatter(second, "tensor", scatter_dimension=0, tiled=False)
    streams, maps, meta, state = scan(width, first, params, conv_bc)
    local = inside(streams, maps, meta, params)
    partner = swapped(state, "tensor", 1).astype(F32)
    state = state.astype(F32)
    late = my_chip % 2 == 1
    early_state = jnp.where(late, partner, state)[:128]
    late_state = jnp.where(late, state, partner)[:128]
    early_decay = jnp.where(late, partner, state)[128:129]
    late_decay = jnp.where(late, state, partner)[128:129]
    whole = jnp.concatenate(
        [
            late_decay * early_state + late_state,
            jnp.broadcast_to(early_decay * late_decay, (16, 512)),
        ],
        0,
    ).astype(BF16)
    others = [None] + [swapped(whole, "segment", bits) for bits in range(1, segment_count)]
    prior = jnp.zeros((128, 512), F32)
    for source in range(segment_count - 1):
        bits = my_segment ^ source
        piece = others[1]
        for index in range(2, segment_count):
            piece = jnp.where(bits == index, others[index], piece)
        piece = piece.astype(F32)
        prior = jnp.where(source < my_segment, piece[128:129] * prior + piece[:128], prior)
    prior = jnp.where(late, early_decay * prior + early_state, prior)
    normed = gate(second, local, maps, meta, prior, params)
    normed = lax.ppermute(
        normed, ("dp", "tensor"), [(i, i if i % 4 < 2 else i ^ 4) for i in range(8)]
    )
    gathered = lax.all_gather(normed, "tensor", axis=0, tiled=False)
    return output(gathered, out_weight, weight_other, crops, text, newline)[None]


def per_device(*args):
    text_embed, crop_feats = args[0], args[1]
    sizes = tuple(lax.axis_size(axis) for axis in ("segment", "dp", "tensor"))
    heads_dev = args[12].shape[0]
    head_width = args[15].shape[0] // heads_dev
    state_size = args[9].shape[1] // 2
    fits = (
        sizes == (4, 2, 4)
        and heads_dev == 1
        and (head_width, state_size) == (128, 128)
        and crop_feats.shape[2:4] == (1, 256)
        and text_embed.shape[1] == 512
    )
    return (per_device_halves if fits else per_device_any)(*args)


def solution(mesh):
    return jax.shard_map(
        per_device,
        mesh=mesh,
        in_specs=(
            P("dp", "segment", "tensor"),
            P("segment", "dp", None, None, None),
            P("segment", None, None),
            P(),
            P(None, "tensor"),
            P("tensor"),
            P("tensor"),
            P("tensor", "dp"),
            P("tensor", "dp"),
            P("tensor", "dp"),
            P(None, ("dp", "tensor")),
            P(None, "dp"),
            P(("dp", "tensor")),
            P(("dp", "tensor")),
            P(("dp", "tensor")),
            P(("dp", "tensor")),
            P("dp", "tensor"),
        ),
        out_specs=P("dp", "segment", "tensor"),
        check_vma=False,
    )
```

```python
import jax
import jax.numpy as jnp
from jax import lax
from jax.experimental import pallas as pl
from jax.experimental.pallas import tpu as pltpu
from jax.sharding import PartitionSpec as P

EPS = 1e-05
F32 = jnp.float32
BF16 = jnp.bfloat16
HIGHEST = lax.Precision.HIGHEST


def passed_along(block, axis, distance):
    devices = range(lax.axis_size(axis))
    route = [(i - distance, i) for i in devices if i - distance in devices]
    return lax.ppermute(block, axis, route)


def swapped(block, axis, bits):
    return lax.ppermute(block, axis, [(i, i ^ bits) for i in range(lax.axis_size(axis))])


def per_device_any(
    text_embed,
    crop_feats,
    crop_dest,
    vision_gain,
    proj_weight,
    newline,
    norm_gain,
    xz_weight,
    dt_weight,
    bc_weight,
    conv_x,
    conv_bc,
    dt_bias,
    a_log,
    skip,
    out_gain,
    out_weight,
):
    highest = lax.Precision.HIGHEST
    eps = 1e-05
    dp_count = lax.axis_size("dp")
    tp_count = lax.axis_size("tensor")
    segment_count = lax.axis_size("segment")
    my_rank = lax.axis_index("dp")
    section = text_embed.shape[1]
    columns = text_embed.shape[2]
    crop_count = crop_feats.shape[2]
    crop_rows = crop_feats.shape[3]
    crop_span = crop_rows + 1
    heads_dev = dt_bias.shape[0]
    head_width = out_gain.shape[0] // heads_dev
    state_size = bc_weight.shape[1] // 2
    feats = crop_feats[0, 0].astype(jnp.float32)
    vision = (
        feats
        * lax.rsqrt(jnp.mean(feats * feats, -1, keepdims=True) + eps)
        * vision_gain.astype(jnp.float32)
    ).astype(jnp.bfloat16)
    encoded = jnp.dot(
        vision.reshape(crop_count * crop_rows, -1), proj_weight, preferred_element_type=jnp.float32
    )
    encoded = encoded.astype(jnp.bfloat16).reshape(crop_count, crop_rows, columns)
    table = crop_dest[0]
    sources = jnp.arange(dp_count, dtype=jnp.int32)
    mine = jnp.sum(jnp.where(sources[:, None] == my_rank, table, 0), axis=0)
    chosen = mine[None, :] == sources[:, None]
    outgoing = jnp.einsum(
        "dc,crq->drq", chosen.astype(jnp.bfloat16), encoded, preferred_element_type=jnp.float32
    ).astype(jnp.bfloat16)
    incoming = lax.all_to_all(outgoing, "dp", split_axis=0, concat_axis=0, tiled=True)
    sent_rows = incoming.shape[1]
    valid = jnp.any(table == my_rank, axis=1).astype(jnp.int32)
    order = jnp.cumsum(valid) - valid
    counted = jnp.sum(valid)
    positions = jnp.arange(section, dtype=jnp.int32)
    block = positions // crop_span
    within = positions % crop_span
    slot_ids = jnp.arange(section // crop_span + 1, dtype=jnp.int32)
    matched = (valid[None, :] == 1) & (order[None, :] == slot_ids[:, None])
    slot_source = jnp.sum(jnp.where(matched, sources[None, :], 0), axis=1)
    row_source = jnp.sum(
        jnp.where(block[:, None] == slot_ids[None, :], slot_source[None, :], 0), axis=1
    )
    row_index = row_source * sent_rows + jnp.minimum(within, sent_rows - 1)
    picked = jnp.take(incoming.reshape(dp_count * sent_rows, columns), row_index, axis=0)
    image = block < counted
    text = text_embed[0]
    crop_pos = image & (within < crop_rows)
    line_pos = image & (within == crop_rows)
    hidden = jnp.where(
        crop_pos[:, None], picked, jnp.where(line_pos[:, None], newline[None, :], text)
    )
    wide = hidden.astype(jnp.float32)
    row_total = lax.psum(jnp.sum(wide * wide, -1), "tensor")
    normed = (
        wide
        * lax.rsqrt(row_total / (columns * tp_count) + eps)[:, None]
        * norm_gain.astype(jnp.float32)
    ).astype(jnp.bfloat16)
    pair_cols = xz_weight.shape[1]
    step_cols = dt_weight.shape[1]
    piece = lax.all_gather(normed, "dp", axis=0, tiled=True)
    terms = jnp.concatenate(
        [
            jnp.dot(piece, xz_weight, preferred_element_type=jnp.float32),
            jnp.dot(piece, dt_weight, preferred_element_type=jnp.float32),
            jnp.dot(piece, bc_weight, preferred_element_type=jnp.float32),
        ],
        axis=1,
    )
    pair_mine, step_mine = (
        lax.psum_scatter(
            terms[:, :pair_cols].astype(jnp.bfloat16), "tensor", scatter_dimension=1, tiled=True
        ).astype(jnp.float32),
        lax.psum_scatter(
            terms[:, pair_cols : pair_cols + step_cols].astype(jnp.bfloat16),
            "tensor",
            scatter_dimension=1,
            tiled=True,
        ).astype(jnp.float32),
    )
    map_terms = terms[:, pair_cols + step_cols :]
    maps_all = lax.psum(map_terms.astype(jnp.bfloat16), "tensor").astype(jnp.float32)
    pairs = pair_mine.reshape(dp_count, section, heads_dev, 2, head_width)
    values = pairs[:, :, :, 0, :].reshape(dp_count, section, heads_dev * head_width)
    gates = pairs[:, :, :, 1, :]
    fresh = jnp.concatenate([values, maps_all.reshape(dp_count, section, 2 * state_size)], axis=2)
    kernel = jnp.concatenate([conv_x, conv_bc], axis=1).astype(jnp.float32)
    taps = kernel.shape[0]
    edge = passed_along(fresh[:, section - (taps - 1) :, :], "segment", 1)
    padded = jnp.concatenate([edge, fresh], axis=1)
    filtered = kernel[0] * padded[:, 0:section]
    for offset in range(1, taps):
        filtered = filtered + kernel[offset] * padded[:, offset : offset + section]
    activated = jax.nn.silu(filtered)
    inner_cols = heads_dev * head_width
    streams = activated[..., :inner_cols].reshape(dp_count, section, heads_dev, head_width)
    b_rows = activated[..., inner_cols : inner_cols + state_size]
    c_rows = activated[..., inner_cols + state_size :]
    step = jax.nn.softplus(step_mine.reshape(dp_count, section, heads_dev) + dt_bias)
    cumulative = jnp.cumsum(-jnp.exp(a_log) * step, axis=1)
    scores = jnp.einsum("nls,nms->nlm", c_rows, b_rows, precision=highest)
    mask = (positions[:, None] >= positions[None, :])[None, :, :, None]
    gaps = cumulative[:, :, None, :] - cumulative[:, None, :, :]
    weights = (
        jnp.where(mask, jnp.exp(jnp.where(mask, gaps, 0.0)), 0.0)
        * scores[..., None]
        * step[:, None, :, :]
    )
    inside = jnp.einsum("nlmh,nmhp->nlhp", weights, streams, precision=highest)
    final = cumulative[:, -1, :]
    carry_weight = jnp.exp(final[:, None, :] - cumulative) * step
    local_state = jnp.einsum("nlh,nls,nlhp->nhsp", carry_weight, b_rows, streams, precision=highest)
    decay = jnp.exp(final)
    prior = jnp.zeros_like(local_state)
    for turn in range(segment_count - 1):
        prior = passed_along(
            (decay[:, :, None, None] * prior + local_state).astype(jnp.bfloat16), "segment", 1
        ).astype(jnp.float32)
    across = jnp.exp(cumulative)[..., None] * jnp.einsum(
        "nls,nhsp->nlhp", c_rows, prior, precision=highest
    )
    outputs = inside + across + skip[None, None, :, None] * streams
    gated = outputs * jax.nn.silu(gates)
    group_total = lax.psum(jnp.sum(gated * gated, axis=(2, 3)), "tensor")
    scale = lax.rsqrt(group_total / (inner_cols * tp_count) + eps)
    normed_out = (
        gated * scale[..., None, None] * out_gain.astype(jnp.float32).reshape(heads_dev, head_width)
    ).astype(jnp.bfloat16)
    normed_out = normed_out.reshape(dp_count * section, inner_cols)
    term = jnp.dot(
        lax.all_gather(normed_out, "tensor", axis=1, tiled=True),
        out_weight,
        preferred_element_type=jnp.float32,
    )
    mixed = lax.psum_scatter(
        term.astype(jnp.bfloat16), "dp", scatter_dimension=0, tiled=True
    ).astype(jnp.float32)
    return (wide + mixed).astype(jnp.bfloat16)[None]


def contract(a, b, dims, precision=None):
    return lax.dot_general(
        a, b, (dims, ((), ())), precision=precision, preferred_element_type=F32
    )


def eye(n):
    return (
        lax.broadcasted_iota(jnp.int32, (n, n), 0) == lax.broadcasted_iota(jnp.int32, (n, n), 1)
    ).astype(F32)


def columns_of(rows):
    return contract(eye(rows.shape[1]), rows, ((1,), (1,)), HIGHEST)


def silu(a):
    return a / (1.0 + jnp.exp(-a))


def enter_body(
    table, feats_mine, feats_other, vision_gain, proj, text, text_other, newline, gain, xz, bc, dt,
    crops_out, rows_out, first_out,
    feats, normed, proj_tiles, tails, weights, crops, rows, first, sems, out_sems,
):
    half = tails.shape[1]
    tiles, _, tile = proj_tiles.shape
    columns = rows.shape[1]
    load_feats = [
        pltpu.make_async_copy(feats_mine, feats.at[0], sems.at[0]),
        pltpu.make_async_copy(feats_other, feats.at[1], sems.at[1]),
    ]
    load_proj = [
        pltpu.make_async_copy(proj.at[:, pl.ds(i * tile, tile)], proj_tiles.at[i], sems.at[2 + i])
        for i in range(tiles)
    ]
    load_tails = [
        pltpu.make_async_copy(text.at[pl.ds(half, half), :], tails.at[0], sems.at[2 + tiles]),
        pltpu.make_async_copy(text_other, tails.at[1], sems.at[3 + tiles]),
    ]
    load_weights = [
        pltpu.make_async_copy(
            xz.at[:, pl.ds(i * 256, 128)],
            weights.at[i // 2, :, pl.ds(i % 2 * 128, 128)],
            sems.at[4 + tiles + i],
        )
        for i in range(4)
    ]
    load_weights.append(pltpu.make_async_copy(bc, weights.at[2], sems.at[8 + tiles]))
    for copy in load_feats + load_proj[:2] + load_tails + load_proj[2:] + load_weights:
        copy.start()
    gain_row = gain[...].reshape(1, -1)
    rank = lax.axis_index("dp")
    stays = table[0, rank, 0] == rank
    load_feats[0].wait()
    load_feats[1].wait()
    for index in range(2):
        block = jnp.where(stays, feats[index], feats[1 - index]).astype(F32)
        scale = lax.rsqrt(jnp.mean(block * block, -1, keepdims=True) + EPS)
        normed[index * half : (index + 1) * half, :] = (
            block * scale * vision_gain[...].reshape(1, -1).astype(F32)
        ).astype(BF16)
    ones = jnp.ones((8, 128), BF16)

    def folded(block):
        total = jnp.zeros((block.shape[0], 128), F32)
        for start in range(0, block.shape[1], 128):
            piece = block[:, start : start + 128].astype(F32)
            total = total + piece * piece
        return total

    squares = [None] * 4
    for i in range(tiles):
        load_proj[i].wait()
        cols = slice(i * tile, (i + 1) * tile)
        result = jnp.dot(normed[...], proj_tiles[i], preferred_element_type=F32).astype(BF16)
        crops[:, cols] = result
        scaled = result * gain_row[:, cols]
        rows[0:half, cols] = scaled[:half]
        rows[2 * half : 3 * half, cols] = scaled[half:]
        for index in range(2):
            more = folded(result[index * half : (index + 1) * half])
            squares[2 * index] = more if i == 0 else squares[2 * index] + more
        if i < 2:
            load_tails[i].wait()
            head = tails[i, 0:8, :].astype(F32)
            line = newline[...].reshape(1, -1).astype(F32)
            top = lax.broadcasted_iota(jnp.int32, (8, 1), 0) == 0
            tails[i, 0:8, :] = jnp.where(top, line, head).astype(BF16)
            main = tails[i]
            base = (2 * i + 1) * half
            rows[base : base + half, :] = main * gain_row
            squares[2 * i + 1] = folded(main)
    departures = [
        pltpu.make_async_copy(crops, crops_out, out_sems.at[0]),
        pltpu.make_async_copy(rows, rows_out, out_sems.at[1]),
    ]
    for copy in departures:
        copy.start()
    for copy in load_weights:
        copy.wait()
    for part in range(4):
        main = rows[part * half : (part + 1) * half, :]
        for i in range(3):
            first[part, 0:half, i * 256 : i * 256 + 256] = jnp.dot(
                main, weights[i], preferred_element_type=F32
            ).astype(BF16)
        steps = contract(dt[...], main, ((1,), (1,)))
        sums = contract(ones, squares[part].astype(BF16), ((1,), (1,)))
        first[part, half : half + 8, 0:half] = jnp.concatenate(
            [steps[0:4], sums[0:4]], 0
        ).astype(BF16)
        departures.append(
            pltpu.make_async_copy(first.at[part], first_out.at[part], out_sems.at[2 + part])
        )
        departures[-1].start()
    for copy in departures:
        copy.wait()


def enter(
    table, feats_mine, feats_other, vision_gain, proj, text, text_other, newline, gain, xz, bc, dt
):
    half, vision = feats_mine.shape
    columns = text.shape[1]
    tiles = 4
    whole = pl.BlockSpec(memory_space=pl.ANY)
    near = pl.BlockSpec(memory_space=pltpu.VMEM)
    return pl.pallas_call(
        enter_body,
        in_specs=[pl.BlockSpec(memory_space=pltpu.SMEM), whole, whole, near, whole, whole, whole]
        + [near, near, whole, whole, near],
        out_specs=[whole, whole, whole],
        out_shape=[
            jax.ShapeDtypeStruct((2 * half, columns), BF16),
            jax.ShapeDtypeStruct((4 * half, columns), BF16),
            jax.ShapeDtypeStruct((4, half + 8, 768), BF16),
        ],
        scratch_shapes=[
            pltpu.VMEM((2, half, vision), BF16),
            pltpu.VMEM((2 * half, vision), BF16),
            pltpu.VMEM((tiles, vision, columns // tiles), BF16),
            pltpu.VMEM((2, half, columns), BF16),
            pltpu.VMEM((3, columns, 256), BF16),
            pltpu.VMEM((2 * half, columns), BF16),
            pltpu.VMEM((4 * half, columns), BF16),
            pltpu.VMEM((4, half + 8, 768), BF16),
            pltpu.SemaphoreType.DMA((9 + tiles,)),
            pltpu.SemaphoreType.DMA((6,)),
        ],
        name="enter",
    )(table, feats_mine, feats_other, vision_gain, proj, text, text_other, newline, gain, xz, bc, dt)


def gates_body(rows, weight, out):
    for head in range(4):
        out[0, :, 128 * head : 128 * head + 128] = jnp.dot(
            rows[...],
            weight[:, 256 * head + 128 : 256 * head + 256],
            preferred_element_type=F32,
        ).astype(BF16)


def gates(rows, weight):
    half, columns = rows.shape[0] // 4, rows.shape[1]
    return pl.pallas_call(
        gates_body,
        grid=(4,),
        in_specs=[
            pl.BlockSpec((half, columns), lambda i: (i, 0)),
            pl.BlockSpec(weight.shape, lambda i: (0, 0)),
        ],
        out_specs=pl.BlockSpec((1, half, 512), lambda i: (i, 0, 0)),
        out_shape=jax.ShapeDtypeStruct((4, half, 512), BF16),
        name="gates",
    )(rows, weight)


def filtered(main, edge, taps):
    rows = main.shape[0]
    padded = jnp.concatenate([edge, main], 0)
    count = taps.shape[0]
    total = taps[count - 1 : count] * main
    for back in range(1, count):
        total = total + taps[count - 1 - back : count - back] * padded[8 - back : 8 - back + rows]
    return total


def scan_body(width, first, before, params, taps_maps, streams, maps, meta, state):
    half = first.shape[0] - 8
    sums = first[half : half + 8, 0:half].astype(F32)
    scale = lax.rsqrt(sums[4:5] / width + EPS)
    sums_before = before[8:16, half - 128 : half].astype(F32)
    scale_before = lax.rsqrt(sums_before[4:5] / width + EPS)
    head = lax.broadcasted_iota(jnp.int32, (8, 512), 1) // 128
    owner = (head == lax.broadcasted_iota(jnp.int32, (8, 512), 0)).astype(F32)
    scalars = params[5:8, :]
    bias = jnp.sum(owner * scalars[0:1], 1, keepdims=True) * (1.0 / 128)
    rate = jnp.sum(owner * scalars[1:2], 1, keepdims=True) * (1.0 / 128)
    raw = sums * scale + bias
    step = jnp.maximum(raw, 0.0) + jnp.log1p(jnp.exp(-jnp.abs(raw)))
    decays = -jnp.exp(rate) * step
    upper = (
        lax.broadcasted_iota(jnp.int32, (half, half), 0)
        <= lax.broadcasted_iota(jnp.int32, (half, half), 1)
    ).astype(F32)
    cumulative = contract(decays, upper, ((1,), (0,)), HIGHEST)
    final = cumulative[:, half - 1 : half]
    carry = jnp.exp(final - cumulative) * step
    scale_main = columns_of(jnp.broadcast_to(scale, (8, half)))[:, 0:1]
    scale_edge = columns_of(jnp.broadcast_to(scale_before, (8, 128)))[120:128, 0:1]
    taps_x = params[0:4, :]
    edge = before[0:8, :].astype(F32) * scale_edge
    x = silu(filtered(first[0:half, 0:512].astype(F32) * scale_main, edge[:, 0:512], taps_x))
    both = silu(
        filtered(
            first[0:half, 512:768].astype(F32) * scale_main,
            edge[:, 512:768],
            taps_maps[...].astype(F32),
        )
    ).astype(BF16)
    carried = contract(columns_of(carry), owner, ((1,), (0,)), HIGHEST)
    state[0:128, :] = contract(both[:, 0:128], (x * carried).astype(BF16), ((0,), (0,))).astype(BF16)
    total = jnp.sum(jnp.exp(final) * owner, 0, keepdims=True)
    state[128:144, :] = jnp.broadcast_to(total, (16, 512)).astype(BF16)
    streams[...] = x.astype(BF16)
    maps[...] = both
    meta[0:8, :] = cumulative
    meta[8:16, :] = step
    meta[16:24, :] = jnp.broadcast_to(scale, (8, half))


def scan(width, first, before, params, taps_maps):
    half = first.shape[0] - 8
    return pl.pallas_call(
        lambda *refs: scan_body(width, *refs),
        out_shape=[
            jax.ShapeDtypeStruct((half, 512), BF16),
            jax.ShapeDtypeStruct((half, 256), BF16),
            jax.ShapeDtypeStruct((24, half), F32),
            jax.ShapeDtypeStruct((144, 512), BF16),
        ],
        name="scan",
    )(first, before, params, taps_maps)


def inside_body(streams, maps, meta, params, out):
    half = streams.shape[0]
    cumulative = meta[0:8, :]
    step = meta[8:16, :]
    cum_cols = columns_of(cumulative)
    scores = contract(maps[:, 128:256], maps[:, 0:128], ((1,), (1,)))
    lower = lax.broadcasted_iota(jnp.int32, (half, half), 0) >= lax.broadcasted_iota(
        jnp.int32, (half, half), 1
    )
    scores = jnp.where(lower, scores, 0.0)
    for head in range(4):
        cols = slice(128 * head, 128 * head + 128)
        x = streams[:, cols]
        gaps = cum_cols[:, head : head + 1] - cumulative[head : head + 1]
        weights = jnp.exp(jnp.where(lower, gaps, 0.0)) * scores * step[head : head + 1]
        y = jnp.dot(weights.astype(BF16), x, preferred_element_type=F32)
        out[:, cols] = y + params[7:8, cols] * x.astype(F32)


def inside(streams, maps, meta, params):
    return pl.pallas_call(
        inside_body,
        out_shape=jax.ShapeDtypeStruct(streams.shape, F32),
        name="inside",
    )(streams, maps, meta, params)


def gate_body(second, local, maps, meta, prior, params, out):
    half = local.shape[0]
    scale = columns_of(meta[16:24, :])[:, 0:1]
    entry = jnp.exp(columns_of(meta[0:8, :]))
    across = jnp.dot(maps[:, 128:256], prior[...].astype(BF16), preferred_element_type=F32)
    gated = []
    squares = jnp.zeros((half, 1), F32)
    for head in range(4):
        cols = slice(128 * head, 128 * head + 128)
        y = local[:, cols] + entry[:, head : head + 1] * across[:, cols]
        value = y * silu(second[:, cols].astype(F32) * scale)
        squares = squares + jnp.sum(value * value, -1, keepdims=True)
        gated.append(value)
    norm = lax.rsqrt(squares / 512 + EPS)
    for head in range(4):
        cols = slice(128 * head, 128 * head + 128)
        out[:, cols] = (gated[head] * norm * params[4:5, cols]).astype(BF16)


def gate(second, local, maps, meta, prior, params):
    return pl.pallas_call(
        gate_body,
        out_shape=jax.ShapeDtypeStruct(local.shape, BF16),
        name="gate",
    )(second, local, maps, meta, prior, params)


def output_body(
    here, near, far, both, weight_mine, weight_other, crops, text, newline, out_hbm,
    blocks, weights, hidden, out, sems, out_sems,
):
    half = hidden.shape[1]
    tiles, _, _, tile = weights.shape
    chip = lax.axis_index("tensor")
    load_hidden = [
        pltpu.make_async_copy(crops.at[pl.ds(0, half), :], hidden.at[0], sems.at[0]),
        pltpu.make_async_copy(text.at[pl.ds(half, half), :], hidden.at[1], sems.at[1]),
    ]
    load_blocks = [
        pltpu.make_async_copy(source, blocks.at[jnp.bitwise_xor(chip, bits)], sems.at[2 + bits])
        for bits, source in enumerate((here, near, far, both))
    ]
    load_weights = [
        [
            pltpu.make_async_copy(
                source.at[:, pl.ds(i * tile, tile)], weights.at[i, index], sems.at[6 + 2 * i + index]
            )
            for index, source in enumerate((weight_mine, weight_other))
        ]
        for i in range(tiles)
    ]
    for copy in load_blocks + load_weights[0] + load_hidden:
        copy.start()
    for pair in load_weights[1:]:
        for copy in pair:
            copy.start()
    for copy in load_blocks:
        copy.wait()
    departures = []
    for i in range(tiles):
        cols = slice(i * tile, (i + 1) * tile)
        for copy in load_weights[i]:
            copy.wait()
        if i == 0:
            for copy in load_hidden:
                copy.wait()
            head = hidden[1, 0:8, :].astype(F32)
            line = newline[...].reshape(1, -1).astype(F32)
            top = lax.broadcasted_iota(jnp.int32, (8, 1), 0) == 0
            hidden[1, 0:8, :] = jnp.where(top, line, head).astype(BF16)
        for index in range(2):
            mixed = jnp.dot(blocks[index], weights[i, 0], preferred_element_type=F32)
            mixed = mixed + jnp.dot(blocks[2 + index], weights[i, 1], preferred_element_type=F32)
            out[i, index * half : (index + 1) * half, :] = (
                hidden[index, :, cols].astype(F32) + mixed
            ).astype(BF16)
        departures.append(
            pltpu.make_async_copy(out.at[i], out_hbm.at[:, pl.ds(i * tile, tile)], out_sems.at[i])
        )
        departures[-1].start()
    for copy in departures:
        copy.wait()


def output(pieces, weight_mine, weight_other, crops, text, newline):
    section, columns = text.shape
    half = section // 2
    tiles = 4
    tile = columns // tiles
    inner = weight_mine.shape[0]
    whole = pl.BlockSpec(memory_space=pl.ANY)
    return pl.pallas_call(
        output_body,
        in_specs=[whole] * 8 + [pl.BlockSpec(memory_space=pltpu.VMEM)],
        out_specs=whole,
        out_shape=jax.ShapeDtypeStruct((section, columns), BF16),
        scratch_shapes=[
            pltpu.VMEM((4, half, inner), BF16),
            pltpu.VMEM((tiles, 2, inner, tile), BF16),
            pltpu.VMEM((2, half, columns), BF16),
            pltpu.VMEM((tiles, section, tile), BF16),
            pltpu.SemaphoreType.DMA((6 + 2 * tiles,)),
            pltpu.SemaphoreType.DMA((tiles,)),
        ],
        name="output",
    )(*pieces, weight_mine, weight_other, crops, text, newline)


def per_device_halves(
    text_embed, crop_feats, crop_dest, vision_gain, proj_weight, newline, norm_gain, xz_weight,
    dt_weight, bc_weight, conv_x, conv_bc, dt_bias, a_log, skip, out_gain, out_weight,
):
    my_chip = lax.axis_index("tensor")
    my_segment = lax.axis_index("segment")
    segment_count = lax.axis_size("segment")
    text = text_embed[0]
    section, columns = text.shape
    half = section // 2
    width = columns * lax.axis_size("tensor")
    feats = crop_feats[0, 0, 0]
    feats_other = swapped(feats, "dp", 1)
    text_other = swapped(text[half:], "dp", 1)
    crops, rows, first = enter(
        crop_dest, feats, feats_other, vision_gain, proj_weight, text, text_other, newline,
        norm_gain, xz_weight, bc_weight, dt_weight.T,
    )
    later = (conv_x, out_gain, dt_bias, a_log, skip, out_weight, first, rows)
    conv_x, out_gain, dt_bias, a_log, skip, out_weight, first, rows = lax.optimization_barrier(later)
    first = lax.psum_scatter(first, "tensor", scatter_dimension=0, tiled=False)
    second = gates(rows, xz_weight)
    weight_other = swapped(out_weight, "dp", 1)
    own = jnp.concatenate(
        [conv_x.astype(F32), out_gain.astype(F32)[None]]
        + [jnp.broadcast_to(value[:, None], (1, 128)) for value in (dt_bias, a_log, skip)],
        0,
    )
    params = lax.all_gather(own, "tensor", axis=1, tiled=True)
    second, params = lax.optimization_barrier((second, params))
    second = lax.psum_scatter(second, "tensor", scatter_dimension=0, tiled=False)
    route = [(i, i + 1) for i in range(0, 4 * segment_count, 2)]
    route += [(i, i + 3) for i in range(1, 4 * segment_count - 4, 2)]
    before = lax.ppermute(first[half - 8 :], ("segment", "tensor"), route)
    streams, maps, meta, state = scan(width, first, before, params, conv_bc)
    local = inside(streams, maps, meta, params)
    partner = swapped(state, "tensor", 1).astype(F32)
    state = state.astype(F32)
    late = my_chip % 2 == 1
    early_state = jnp.where(late, partner, state)[:128]
    late_state = jnp.where(late, state, partner)[:128]
    early_decay = jnp.where(late, partner, state)[128:129]
    late_decay = jnp.where(late, state, partner)[128:129]
    whole = jnp.concatenate(
        [
            late_decay * early_state + late_state,
            jnp.broadcast_to(early_decay * late_decay, (16, 512)),
        ],
        0,
    ).astype(BF16)
    others = [None] + [swapped(whole, "segment", bits) for bits in range(1, segment_count)]
    prior = jnp.zeros((128, 512), F32)
    for source in range(segment_count - 1):
        bits = my_segment ^ source
        piece = others[1]
        for index in range(2, segment_count):
            piece = jnp.where(bits == index, others[index], piece)
        piece = piece.astype(F32)
        prior = jnp.where(source < my_segment, piece[128:129] * prior + piece[:128], prior)
    prior = jnp.where(late, early_decay * prior + early_state, prior)
    normed = gate(second, local, maps, meta, prior, params)
    near, far, here = (
        lax.ppermute(
            normed, ("dp", "tensor"), [(i, (i if i % 4 < 2 else i ^ 4) ^ bits) for i in range(8)]
        )
        for bits in (1, 2, 0)
    )
    pieces = (here, near, far, swapped(far, "tensor", 1))
    return output(pieces, out_weight, weight_other, crops, text, newline)[None]


def per_device(*args):
    text_embed, crop_feats = args[0], args[1]
    sizes = tuple(lax.axis_size(axis) for axis in ("segment", "dp", "tensor"))
    heads_dev = args[12].shape[0]
    head_width = args[15].shape[0] // heads_dev
    state_size = args[9].shape[1] // 2
    fits = (
        sizes == (4, 2, 4)
        and heads_dev == 1
        and (head_width, state_size) == (128, 128)
        and crop_feats.shape[2:4] == (1, 256)
        and text_embed.shape[1] == 512
    )
    return (per_device_halves if fits else per_device_any)(*args)


def solution(mesh):
    return jax.shard_map(
        per_device,
        mesh=mesh,
        in_specs=(
            P("dp", "segment", "tensor"),
            P("segment", "dp", None, None, None),
            P("segment", None, None),
            P(),
            P(None, "tensor"),
            P("tensor"),
            P("tensor"),
            P("tensor", "dp"),
            P("tensor", "dp"),
            P("tensor", "dp"),
            P(None, ("dp", "tensor")),
            P(None, "dp"),
            P(("dp", "tensor")),
            P(("dp", "tensor")),
            P(("dp", "tensor")),
            P(("dp", "tensor")),
            P("dp", "tensor"),
        ),
        out_specs=P("dp", "segment", "tensor"),
        check_vma=False,
    )
```

```python
import jax
import jax.numpy as jnp
from jax import lax
from jax.experimental import pallas as pl
from jax.experimental.pallas import tpu as pltpu
from jax.sharding import PartitionSpec as P

EPS = 1e-05
F32 = jnp.float32
BF16 = jnp.bfloat16
HIGHEST = lax.Precision.HIGHEST


def passed_along(block, axis, distance):
    devices = range(lax.axis_size(axis))
    route = [(i - distance, i) for i in devices if i - distance in devices]
    return lax.ppermute(block, axis, route)


def swapped(block, axis, bits):
    return lax.ppermute(block, axis, [(i, i ^ bits) for i in range(lax.axis_size(axis))])


def per_device_any(
    text_embed,
    crop_feats,
    crop_dest,
    vision_gain,
    proj_weight,
    newline,
    norm_gain,
    xz_weight,
    dt_weight,
    bc_weight,
    conv_x,
    conv_bc,
    dt_bias,
    a_log,
    skip,
    out_gain,
    out_weight,
):
    highest = lax.Precision.HIGHEST
    eps = 1e-05
    dp_count = lax.axis_size("dp")
    tp_count = lax.axis_size("tensor")
    segment_count = lax.axis_size("segment")
    my_rank = lax.axis_index("dp")
    section = text_embed.shape[1]
    columns = text_embed.shape[2]
    crop_count = crop_feats.shape[2]
    crop_rows = crop_feats.shape[3]
    crop_span = crop_rows + 1
    heads_dev = dt_bias.shape[0]
    head_width = out_gain.shape[0] // heads_dev
    state_size = bc_weight.shape[1] // 2
    feats = crop_feats[0, 0].astype(jnp.float32)
    vision = (
        feats
        * lax.rsqrt(jnp.mean(feats * feats, -1, keepdims=True) + eps)
        * vision_gain.astype(jnp.float32)
    ).astype(jnp.bfloat16)
    encoded = jnp.dot(
        vision.reshape(crop_count * crop_rows, -1), proj_weight, preferred_element_type=jnp.float32
    )
    encoded = encoded.astype(jnp.bfloat16).reshape(crop_count, crop_rows, columns)
    table = crop_dest[0]
    sources = jnp.arange(dp_count, dtype=jnp.int32)
    mine = jnp.sum(jnp.where(sources[:, None] == my_rank, table, 0), axis=0)
    chosen = mine[None, :] == sources[:, None]
    outgoing = jnp.einsum(
        "dc,crq->drq", chosen.astype(jnp.bfloat16), encoded, preferred_element_type=jnp.float32
    ).astype(jnp.bfloat16)
    incoming = lax.all_to_all(outgoing, "dp", split_axis=0, concat_axis=0, tiled=True)
    sent_rows = incoming.shape[1]
    valid = jnp.any(table == my_rank, axis=1).astype(jnp.int32)
    order = jnp.cumsum(valid) - valid
    counted = jnp.sum(valid)
    positions = jnp.arange(section, dtype=jnp.int32)
    block = positions // crop_span
    within = positions % crop_span
    slot_ids = jnp.arange(section // crop_span + 1, dtype=jnp.int32)
    matched = (valid[None, :] == 1) & (order[None, :] == slot_ids[:, None])
    slot_source = jnp.sum(jnp.where(matched, sources[None, :], 0), axis=1)
    row_source = jnp.sum(
        jnp.where(block[:, None] == slot_ids[None, :], slot_source[None, :], 0), axis=1
    )
    row_index = row_source * sent_rows + jnp.minimum(within, sent_rows - 1)
    picked = jnp.take(incoming.reshape(dp_count * sent_rows, columns), row_index, axis=0)
    image = block < counted
    text = text_embed[0]
    crop_pos = image & (within < crop_rows)
    line_pos = image & (within == crop_rows)
    hidden = jnp.where(
        crop_pos[:, None], picked, jnp.where(line_pos[:, None], newline[None, :], text)
    )
    wide = hidden.astype(jnp.float32)
    row_total = lax.psum(jnp.sum(wide * wide, -1), "tensor")
    normed = (
        wide
        * lax.rsqrt(row_total / (columns * tp_count) + eps)[:, None]
        * norm_gain.astype(jnp.float32)
    ).astype(jnp.bfloat16)
    pair_cols = xz_weight.shape[1]
    step_cols = dt_weight.shape[1]
    piece = lax.all_gather(normed, "dp", axis=0, tiled=True)
    terms = jnp.concatenate(
        [
            jnp.dot(piece, xz_weight, preferred_element_type=jnp.float32),
            jnp.dot(piece, dt_weight, preferred_element_type=jnp.float32),
            jnp.dot(piece, bc_weight, preferred_element_type=jnp.float32),
        ],
        axis=1,
    )
    pair_mine, step_mine = (
        lax.psum_scatter(
            terms[:, :pair_cols].astype(jnp.bfloat16), "tensor", scatter_dimension=1, tiled=True
        ).astype(jnp.float32),
        lax.psum_scatter(
            terms[:, pair_cols : pair_cols + step_cols].astype(jnp.bfloat16),
            "tensor",
            scatter_dimension=1,
            tiled=True,
        ).astype(jnp.float32),
    )
    map_terms = terms[:, pair_cols + step_cols :]
    maps_all = lax.psum(map_terms.astype(jnp.bfloat16), "tensor").astype(jnp.float32)
    pairs = pair_mine.reshape(dp_count, section, heads_dev, 2, head_width)
    values = pairs[:, :, :, 0, :].reshape(dp_count, section, heads_dev * head_width)
    gates = pairs[:, :, :, 1, :]
    fresh = jnp.concatenate([values, maps_all.reshape(dp_count, section, 2 * state_size)], axis=2)
    kernel = jnp.concatenate([conv_x, conv_bc], axis=1).astype(jnp.float32)
    taps = kernel.shape[0]
    edge = passed_along(fresh[:, section - (taps - 1) :, :], "segment", 1)
    padded = jnp.concatenate([edge, fresh], axis=1)
    filtered = kernel[0] * padded[:, 0:section]
    for offset in range(1, taps):
        filtered = filtered + kernel[offset] * padded[:, offset : offset + section]
    activated = jax.nn.silu(filtered)
    inner_cols = heads_dev * head_width
    streams = activated[..., :inner_cols].reshape(dp_count, section, heads_dev, head_width)
    b_rows = activated[..., inner_cols : inner_cols + state_size]
    c_rows = activated[..., inner_cols + state_size :]
    step = jax.nn.softplus(step_mine.reshape(dp_count, section, heads_dev) + dt_bias)
    cumulative = jnp.cumsum(-jnp.exp(a_log) * step, axis=1)
    scores = jnp.einsum("nls,nms->nlm", c_rows, b_rows, precision=highest)
    mask = (positions[:, None] >= positions[None, :])[None, :, :, None]
    gaps = cumulative[:, :, None, :] - cumulative[:, None, :, :]
    weights = (
        jnp.where(mask, jnp.exp(jnp.where(mask, gaps, 0.0)), 0.0)
        * scores[..., None]
        * step[:, None, :, :]
    )
    inside = jnp.einsum("nlmh,nmhp->nlhp", weights, streams, precision=highest)
    final = cumulative[:, -1, :]
    carry_weight = jnp.exp(final[:, None, :] - cumulative) * step
    local_state = jnp.einsum("nlh,nls,nlhp->nhsp", carry_weight, b_rows, streams, precision=highest)
    decay = jnp.exp(final)
    prior = jnp.zeros_like(local_state)
    for turn in range(segment_count - 1):
        prior = passed_along(
            (decay[:, :, None, None] * prior + local_state).astype(jnp.bfloat16), "segment", 1
        ).astype(jnp.float32)
    across = jnp.exp(cumulative)[..., None] * jnp.einsum(
        "nls,nhsp->nlhp", c_rows, prior, precision=highest
    )
    outputs = inside + across + skip[None, None, :, None] * streams
    gated = outputs * jax.nn.silu(gates)
    group_total = lax.psum(jnp.sum(gated * gated, axis=(2, 3)), "tensor")
    scale = lax.rsqrt(group_total / (inner_cols * tp_count) + eps)
    normed_out = (
        gated * scale[..., None, None] * out_gain.astype(jnp.float32).reshape(heads_dev, head_width)
    ).astype(jnp.bfloat16)
    normed_out = normed_out.reshape(dp_count * section, inner_cols)
    term = jnp.dot(
        lax.all_gather(normed_out, "tensor", axis=1, tiled=True),
        out_weight,
        preferred_element_type=jnp.float32,
    )
    mixed = lax.psum_scatter(
        term.astype(jnp.bfloat16), "dp", scatter_dimension=0, tiled=True
    ).astype(jnp.float32)
    return (wide + mixed).astype(jnp.bfloat16)[None]


def contract(a, b, dims, precision=None):
    return lax.dot_general(
        a, b, (dims, ((), ())), precision=precision, preferred_element_type=F32
    )


def eye(n):
    return (
        lax.broadcasted_iota(jnp.int32, (n, n), 0) == lax.broadcasted_iota(jnp.int32, (n, n), 1)
    ).astype(F32)


def columns_of(rows):
    return contract(eye(rows.shape[1]), rows, ((1,), (1,)), HIGHEST)


def silu(a):
    return a / (1.0 + jnp.exp(-a))


def enter_body(
    table, dt_bias, a_log, skip, feats_mine, feats_other, vision_gain, proj, text, text_other,
    newline, gain, xz, bc, dt, conv_x, out_gain,
    crops_out, rows_out, first_out, keep_out, send_out,
    feats, normed, proj_tiles, tails, weights, crops, rows, first, maps, sems, out_sems,
):
    half = tails.shape[1]
    tiles, _, tile = proj_tiles.shape
    columns = rows.shape[1]
    load_feats = [
        pltpu.make_async_copy(feats_mine, feats.at[0], sems.at[0]),
        pltpu.make_async_copy(feats_other, feats.at[1], sems.at[1]),
    ]
    load_proj = [
        pltpu.make_async_copy(proj.at[:, pl.ds(i * tile, tile)], proj_tiles.at[i], sems.at[2 + i])
        for i in range(tiles)
    ]
    load_tails = [
        pltpu.make_async_copy(text.at[pl.ds(half, half), :], tails.at[0], sems.at[2 + tiles]),
        pltpu.make_async_copy(text_other.at[pl.ds(half, half), :], tails.at[1], sems.at[3 + tiles]),
    ]
    load_weights = [
        pltpu.make_async_copy(
            xz.at[:, pl.ds(i * 256, 128)],
            weights.at[i // 2, :, pl.ds(i % 2 * 128, 128)],
            sems.at[4 + tiles + i],
        )
        for i in range(4)
    ]
    load_weights.append(pltpu.make_async_copy(bc, weights.at[2], sems.at[8 + tiles]))
    for copy in load_feats + load_proj[:2] + load_tails + load_proj[2:] + load_weights:
        copy.start()
    gain_row = gain[...].reshape(1, -1)
    rank = lax.axis_index("dp")
    stays = table[0, 0, rank] == rank
    load_feats[0].wait()
    load_feats[1].wait()
    for index in range(2):
        block = jnp.where(stays, feats[index], feats[1 - index]).astype(F32)
        scale = lax.rsqrt(jnp.mean(block * block, -1, keepdims=True) + EPS)
        normed[index * half : (index + 1) * half, :] = (
            block * scale * vision_gain[...].reshape(1, -1).astype(F32)
        ).astype(BF16)
    ones = jnp.ones((8, 128), BF16)

    def folded(block):
        total = jnp.zeros((block.shape[0], 128), F32)
        for start in range(0, block.shape[1], 128):
            piece = block[:, start : start + 128].astype(F32)
            total = total + piece * piece
        return total

    squares = [None] * 4
    for i in range(tiles):
        load_proj[i].wait()
        cols = slice(i * tile, (i + 1) * tile)
        result = jnp.dot(normed[...], proj_tiles[i], preferred_element_type=F32).astype(BF16)
        crops[:, cols] = result
        scaled = result * gain_row[:, cols]
        rows[0:half, cols] = scaled[:half]
        rows[2 * half : 3 * half, cols] = scaled[half:]
        for index in range(2):
            more = folded(result[index * half : (index + 1) * half])
            squares[2 * index] = more if i == 0 else squares[2 * index] + more
        if i < 2:
            load_tails[i].wait()
            head = tails[i, 0:8, :].astype(F32)
            line = newline[...].reshape(1, -1).astype(F32)
            top = lax.broadcasted_iota(jnp.int32, (8, 1), 0) == 0
            tails[i, 0:8, :] = jnp.where(top, line, head).astype(BF16)
            main = tails[i]
            base = (2 * i + 1) * half
            rows[base : base + half, :] = main * gain_row
            squares[2 * i + 1] = folded(main)
    departures = [
        pltpu.make_async_copy(crops, crops_out, out_sems.at[0]),
        pltpu.make_async_copy(rows, rows_out, out_sems.at[1]),
    ]
    for copy in departures:
        copy.start()
    for copy in load_weights:
        copy.wait()
    chip = lax.axis_index("tensor")
    lane = lax.broadcasted_iota(jnp.int32, (1, 128), 1)
    own = [conv_x[...].astype(F32), out_gain[...].reshape(1, 128).astype(F32)]
    for value in (dt_bias[0], a_log[0], skip[0]):
        whole = jnp.full((1, 128), value, F32)
        high = whole.astype(BF16).astype(F32)
        middle = (whole - high).astype(BF16).astype(F32)
        low = whole - high - middle
        pieces = jnp.where(lane < 32, high, jnp.where(lane < 64, middle, low))
        own.append(jnp.where(lane < 96, pieces, 0.0))
    own = jnp.concatenate(own, 0)
    slots = jnp.concatenate([jnp.where(chip == slot, own, 0.0) for slot in range(4)], 1)
    for part in range(4):
        main = rows[part * half : (part + 1) * half, :]
        maps[part] = jnp.dot(main, weights[2], preferred_element_type=F32).astype(BF16)
        goes = pltpu.make_async_copy(maps.at[part], send_out.at[part // 2], out_sems.at[6 + part])
        remains = pltpu.make_async_copy(
            maps.at[part], keep_out.at[part // 2], out_sems.at[6 + part]
        )
        here = chip % 2 == part % 2
        pl.when(here)(remains.start)
        pl.when(jnp.logical_not(here))(goes.start)
        departures.append(goes)
    for part in range(4):
        main = rows[part * half : (part + 1) * half, :]
        for i in range(2):
            first[part, 0:half, i * 256 : i * 256 + 256] = jnp.dot(
                main, weights[i], preferred_element_type=F32
            ).astype(BF16)
        steps = contract(dt[...], main, ((1,), (1,)))
        sums = contract(ones, squares[part].astype(BF16), ((1,), (1,)))
        sums = jnp.concatenate([steps[0:4], sums[0:4]], 0)
        sums = jnp.concatenate([sums, jnp.zeros((8, 512 - half), F32)], 1)
        first[part, half : half + 16, :] = jnp.concatenate([sums, slots], 0).astype(BF16)
        departures.append(
            pltpu.make_async_copy(first.at[part], first_out.at[part], out_sems.at[2 + part])
        )
        departures[-1].start()
    for copy in departures:
        copy.wait()


def enter(
    table, dt_bias, a_log, skip, feats_mine, feats_other, vision_gain, proj, text, text_other,
    newline, gain, xz, bc, dt, conv_x, out_gain,
):
    half, vision = feats_mine.shape
    columns = text.shape[1]
    tiles = 4
    whole = pl.BlockSpec(memory_space=pl.ANY)
    near = pl.BlockSpec(memory_space=pltpu.VMEM)
    return pl.pallas_call(
        enter_body,
        in_specs=[pl.BlockSpec(memory_space=pltpu.SMEM)] * 4
        + [whole, whole, near, whole, whole, whole]
        + [near, near, whole, whole, near, near, near],
        out_specs=[whole] * 5,
        out_shape=[
            jax.ShapeDtypeStruct((2 * half, columns), BF16),
            jax.ShapeDtypeStruct((4 * half, columns), BF16),
            jax.ShapeDtypeStruct((4, half + 16, 512), BF16),
            jax.ShapeDtypeStruct((2, half, 256), BF16),
            jax.ShapeDtypeStruct((2, half, 256), BF16),
        ],
        scratch_shapes=[
            pltpu.VMEM((2, half, vision), BF16),
            pltpu.VMEM((2 * half, vision), BF16),
            pltpu.VMEM((tiles, vision, columns // tiles), BF16),
            pltpu.VMEM((2, half, columns), BF16),
            pltpu.VMEM((3, columns, 256), BF16),
            pltpu.VMEM((2 * half, columns), BF16),
            pltpu.VMEM((4 * half, columns), BF16),
            pltpu.VMEM((4, half + 16, 512), BF16),
            pltpu.VMEM((4, half, 256), BF16),
            pltpu.SemaphoreType.DMA((9 + tiles,)),
            pltpu.SemaphoreType.DMA((10,)),
        ],
        name="enter",
    )(
        table, dt_bias, a_log, skip, feats_mine, feats_other, vision_gain, proj, text, text_other,
        newline, gain, xz, bc, dt, conv_x, out_gain,
    )


def gates_body(rows, weight, out):
    for head in range(4):
        out[0, :, 128 * head : 128 * head + 128] = jnp.dot(
            rows[...],
            weight[:, 256 * head + 128 : 256 * head + 256],
            preferred_element_type=F32,
        ).astype(BF16)


def gates(rows, weight):
    half, columns = rows.shape[0] // 4, rows.shape[1]
    return pl.pallas_call(
        gates_body,
        grid=(4,),
        in_specs=[
            pl.BlockSpec((half, columns), lambda i: (i, 0)),
            pl.BlockSpec(weight.shape, lambda i: (0, 0)),
        ],
        out_specs=pl.BlockSpec((1, half, 512), lambda i: (i, 0, 0)),
        out_shape=jax.ShapeDtypeStruct((4, half, 512), BF16),
        name="gates",
    )(rows, weight)


def filtered(main, edge, taps):
    rows = main.shape[0]
    padded = jnp.concatenate([edge, main], 0)
    count = taps.shape[0]
    total = taps[count - 1 : count] * main
    for back in range(1, count):
        total = total + taps[count - 1 - back : count - back] * padded[8 - back : 8 - back + rows]
    return total


def scan_body(
    width, first, kept, received, before, taps_maps, streams, maps, meta, state, params
):
    half = first.shape[0] - 16
    slots = first[half : half + 16, :].astype(F32)[8:16]
    params[...] = slots
    sums = first[half : half + 16, 0:half].astype(F32)[0:8]
    scale = lax.rsqrt(sums[4:5] / width + EPS)
    sums_before = before[8:16, half - 128 : half].astype(F32)
    scale_before = lax.rsqrt(sums_before[4:5] / width + EPS)
    head = lax.broadcasted_iota(jnp.int32, (8, 512), 1) // 128
    owner = (head == lax.broadcasted_iota(jnp.int32, (8, 512), 0)).astype(F32)
    scalars = slots[5:8]
    bias = jnp.sum(owner * scalars[0:1], 1, keepdims=True) * (1.0 / 32)
    rate = jnp.sum(owner * scalars[1:2], 1, keepdims=True) * (1.0 / 32)
    raw = sums * scale + bias
    step = jnp.maximum(raw, 0.0) + jnp.log1p(jnp.exp(-jnp.abs(raw)))
    decays = -jnp.exp(rate) * step
    upper = (
        lax.broadcasted_iota(jnp.int32, (half, half), 0)
        <= lax.broadcasted_iota(jnp.int32, (half, half), 1)
    ).astype(F32)
    cumulative = contract(decays, upper, ((1,), (0,)), HIGHEST)
    final = cumulative[:, half - 1 : half]
    carry = jnp.exp(final - cumulative) * step
    scale_main = columns_of(jnp.broadcast_to(scale, (8, half)))[:, 0:1]
    scale_edge = columns_of(jnp.broadcast_to(scale_before, (8, 128)))[120:128, 0:1]
    taps_x = slots[0:4]
    edge = before[0:8, :].astype(F32) * scale_edge
    x = silu(filtered(first[0:half, :].astype(F32) * scale_main, edge[:, 0:512], taps_x))
    both = silu(
        filtered(
            (kept[...].astype(F32) + received[...].astype(F32)) * scale_main,
            edge[:, 512:768],
            taps_maps[...].astype(F32),
        )
    ).astype(BF16)
    carried = contract(columns_of(carry), owner, ((1,), (0,)), HIGHEST)
    state[0:128, :] = contract(both[:, 0:128], (x * carried).astype(BF16), ((0,), (0,))).astype(BF16)
    total = jnp.sum(jnp.exp(final) * owner, 0, keepdims=True)
    state[128:144, :] = jnp.broadcast_to(total, (16, 512)).astype(BF16)
    streams[...] = x.astype(BF16)
    maps[...] = both
    meta[0:8, :] = cumulative
    meta[8:16, :] = step
    meta[16:24, :] = jnp.broadcast_to(scale, (8, half))


def scan(width, first, kept, received, before, taps_maps):
    half = kept.shape[0]
    return pl.pallas_call(
        lambda *refs: scan_body(width, *refs),
        out_shape=[
            jax.ShapeDtypeStruct((half, 512), BF16),
            jax.ShapeDtypeStruct((half, 256), BF16),
            jax.ShapeDtypeStruct((24, half), F32),
            jax.ShapeDtypeStruct((144, 512), BF16),
            jax.ShapeDtypeStruct((8, 512), F32),
        ],
        name="scan",
    )(first, kept, received, before, taps_maps)


def inside_body(streams, maps, meta, params, out):
    half = streams.shape[0]
    cumulative = meta[0:8, :]
    step = meta[8:16, :]
    cum_cols = columns_of(cumulative)
    scores = contract(maps[:, 128:256], maps[:, 0:128], ((1,), (1,)))
    lower = lax.broadcasted_iota(jnp.int32, (half, half), 0) >= lax.broadcasted_iota(
        jnp.int32, (half, half), 1
    )
    scores = jnp.where(lower, scores, 0.0)
    for head in range(4):
        cols = slice(128 * head, 128 * head + 128)
        x = streams[:, cols]
        gaps = cum_cols[:, head : head + 1] - cumulative[head : head + 1]
        weights = jnp.exp(jnp.where(lower, gaps, 0.0)) * scores * step[head : head + 1]
        y = jnp.dot(weights.astype(BF16), x, preferred_element_type=F32)
        through = jnp.sum(params[7:8, cols], 1, keepdims=True) * (1.0 / 32)
        out[:, cols] = y + through * x.astype(F32)


def inside(streams, maps, meta, params):
    return pl.pallas_call(
        inside_body,
        out_shape=jax.ShapeDtypeStruct(streams.shape, F32),
        name="inside",
    )(streams, maps, meta, params)


def gate_body(second, local, maps, meta, prior, params, out):
    half = local.shape[0]
    scale = columns_of(meta[16:24, :])[:, 0:1]
    entry = jnp.exp(columns_of(meta[0:8, :]))
    across = jnp.dot(maps[:, 128:256], prior[...].astype(BF16), preferred_element_type=F32)
    gated = []
    squares = jnp.zeros((half, 1), F32)
    for head in range(4):
        cols = slice(128 * head, 128 * head + 128)
        y = local[:, cols] + entry[:, head : head + 1] * across[:, cols]
        value = y * silu(second[:, cols].astype(F32) * scale)
        squares = squares + jnp.sum(value * value, -1, keepdims=True)
        gated.append(value)
    norm = lax.rsqrt(squares / 512 + EPS)
    for head in range(4):
        cols = slice(128 * head, 128 * head + 128)
        out[:, cols] = (gated[head] * norm * params[4:5, cols]).astype(BF16)


def gate(second, local, maps, meta, prior, params):
    return pl.pallas_call(
        gate_body,
        out_shape=jax.ShapeDtypeStruct(local.shape, BF16),
        name="gate",
    )(second, local, maps, meta, prior, params)


def per_device_halves(
    text_embed, crop_feats, crop_dest, vision_gain, proj_weight, newline, norm_gain, xz_weight,
    dt_weight, bc_weight, conv_x, conv_bc, dt_bias, a_log, skip, out_gain, out_weight,
):
    my_chip = lax.axis_index("tensor")
    my_segment = lax.axis_index("segment")
    segment_count = lax.axis_size("segment")
    text = text_embed[0]
    section, columns = text.shape
    half = section // 2
    width = columns * lax.axis_size("tensor")
    feats = crop_feats[0, 0, 0]
    feats_other = swapped(feats, "dp", 1)
    text_other = swapped(text, "dp", 1)
    crops, rows, first, keep, send = enter(
        crop_dest.transpose(0, 2, 1), dt_bias, a_log, skip, feats, feats_other, vision_gain,
        proj_weight, text, text_other, newline, norm_gain, xz_weight, bc_weight, dt_weight.T,
        conv_x, out_gain,
    )
    out_weight, newline, rows, first = lax.optimization_barrier((out_weight, newline, rows, first))
    first = lax.psum_scatter(first, "tensor", scatter_dimension=0, tiled=False)
    pair = keep.astype(F32) + swapped(send, "tensor", 1).astype(F32)
    lower = my_chip < 2
    received = swapped(jnp.where(lower, pair[1], pair[0]).astype(BF16), "tensor", 2)
    kept = jnp.where(lower, pair[0], pair[1]).astype(BF16)
    second = gates(rows, xz_weight)
    weight_other = swapped(out_weight, "dp", 1)
    weights = (
        jnp.where(lower, out_weight, weight_other), jnp.where(lower, weight_other, out_weight)
    )
    late = my_chip % 2 == 1
    head = crops[:half]
    tail = jnp.where(jnp.arange(half)[:, None] == 0, newline[None], text[half:])
    hidden = (jnp.where(late, tail, head), jnp.where(late, head, tail))
    second, weights, hidden = lax.optimization_barrier((second, weights, hidden))
    second = lax.psum_scatter(second, "tensor", scatter_dimension=0, tiled=False)
    route = [(i, i + 1) for i in range(0, 4 * segment_count, 2)]
    route += [(i, i + 3) for i in range(1, 4 * segment_count - 4, 2)]
    ends = (kept[half - 8 :].astype(F32) + received[half - 8 :].astype(F32)).astype(BF16)
    before = jnp.concatenate([first[half - 8 : half + 8], jnp.pad(ends, ((0, 8), (0, 0)))], 1)
    before = lax.ppermute(before, ("segment", "tensor"), route)
    streams, maps, meta, state, params = scan(width, first, kept, received, before, conv_bc)
    local = inside(streams, maps, meta, params)
    partner = swapped(state, "tensor", 1).astype(F32)
    state = state.astype(F32)
    early_state = jnp.where(late, partner, state)[:128]
    late_state = jnp.where(late, state, partner)[:128]
    early_decay = jnp.where(late, partner, state)[128:129]
    late_decay = jnp.where(late, state, partner)[128:129]
    whole = jnp.concatenate(
        [
            late_decay * early_state + late_state,
            jnp.broadcast_to(early_decay * late_decay, (16, 512)),
        ],
        0,
    ).astype(BF16)
    others = [None] + [swapped(whole, "segment", bits) for bits in range(1, segment_count)]
    prior = jnp.zeros((128, 512), F32)
    for source in range(segment_count - 1):
        bits = my_segment ^ source
        piece = others[1]
        for index in range(2, segment_count):
            piece = jnp.where(bits == index, others[index], piece)
        piece = piece.astype(F32)
        prior = jnp.where(source < my_segment, piece[128:129] * prior + piece[:128], prior)
    prior = jnp.where(late, early_decay * prior + early_state, prior)
    normed = gate(second, local, maps, meta, prior, params)
    near, far, here = (
        lax.ppermute(
            normed, ("dp", "tensor"), [(i, (i if i % 4 < 2 else i ^ 4) ^ bits) for i in range(8)]
        )
        for bits in (1, 2, 0)
    )
    both = swapped(far, "tensor", 1)
    out = jnp.zeros((section, columns), BF16)
    for index, pair in enumerate(((here, far), (near, both))):
        mixed = jnp.dot(pair[0], weights[0], preferred_element_type=F32)
        mixed = mixed + jnp.dot(pair[1], weights[1], preferred_element_type=F32)
        block = (hidden[index].astype(F32) + mixed).astype(BF16)
        start = jnp.where(late, half, 0) if index == 0 else jnp.where(late, 0, half)
        out = lax.dynamic_update_slice(out, block, (start, 0))
    return out[None]


def per_device(*args):
    text_embed, crop_feats = args[0], args[1]
    sizes = tuple(lax.axis_size(axis) for axis in ("segment", "dp", "tensor"))
    heads_dev = args[12].shape[0]
    head_width = args[15].shape[0] // heads_dev
    state_size = args[9].shape[1] // 2
    fits = (
        sizes == (4, 2, 4)
        and heads_dev == 1
        and (head_width, state_size) == (128, 128)
        and crop_feats.shape[2:4] == (1, 256)
        and text_embed.shape[1] == 512
    )
    return (per_device_halves if fits else per_device_any)(*args)


def solution(mesh):
    return jax.shard_map(
        per_device,
        mesh=mesh,
        in_specs=(
            P("dp", "segment", "tensor"),
            P("segment", "dp", None, None, None),
            P("segment", None, None),
            P(),
            P(None, "tensor"),
            P("tensor"),
            P("tensor"),
            P("tensor", "dp"),
            P("tensor", "dp"),
            P("tensor", "dp"),
            P(None, ("dp", "tensor")),
            P(None, "dp"),
            P(("dp", "tensor")),
            P(("dp", "tensor")),
            P(("dp", "tensor")),
            P(("dp", "tensor")),
            P("dp", "tensor"),
        ),
        out_specs=P("dp", "segment", "tensor"),
        check_vma=False,
    )
```

```python
import jax
import jax.numpy as jnp
from jax import lax
from jax.experimental import pallas as pl
from jax.experimental.pallas import tpu as pltpu
from jax.sharding import PartitionSpec as P

EPS = 1e-05
F32 = jnp.float32
BF16 = jnp.bfloat16
HIGHEST = lax.Precision.HIGHEST


def passed_along(block, axis, distance):
    devices = range(lax.axis_size(axis))
    route = [(i - distance, i) for i in devices if i - distance in devices]
    return lax.ppermute(block, axis, route)


def swapped(block, axis, bits):
    return lax.ppermute(block, axis, [(i, i ^ bits) for i in range(lax.axis_size(axis))])


def per_device_any(
    text_embed,
    crop_feats,
    crop_dest,
    vision_gain,
    proj_weight,
    newline,
    norm_gain,
    xz_weight,
    dt_weight,
    bc_weight,
    conv_x,
    conv_bc,
    dt_bias,
    a_log,
    skip,
    out_gain,
    out_weight,
):
    highest = lax.Precision.HIGHEST
    eps = 1e-05
    dp_count = lax.axis_size("dp")
    tp_count = lax.axis_size("tensor")
    segment_count = lax.axis_size("segment")
    my_rank = lax.axis_index("dp")
    section = text_embed.shape[1]
    columns = text_embed.shape[2]
    crop_count = crop_feats.shape[2]
    crop_rows = crop_feats.shape[3]
    crop_span = crop_rows + 1
    heads_dev = dt_bias.shape[0]
    head_width = out_gain.shape[0] // heads_dev
    state_size = bc_weight.shape[1] // 2
    feats = crop_feats[0, 0].astype(jnp.float32)
    vision = (
        feats
        * lax.rsqrt(jnp.mean(feats * feats, -1, keepdims=True) + eps)
        * vision_gain.astype(jnp.float32)
    ).astype(jnp.bfloat16)
    encoded = jnp.dot(
        vision.reshape(crop_count * crop_rows, -1), proj_weight, preferred_element_type=jnp.float32
    )
    encoded = encoded.astype(jnp.bfloat16).reshape(crop_count, crop_rows, columns)
    table = crop_dest[0]
    sources = jnp.arange(dp_count, dtype=jnp.int32)
    mine = jnp.sum(jnp.where(sources[:, None] == my_rank, table, 0), axis=0)
    chosen = mine[None, :] == sources[:, None]
    outgoing = jnp.einsum(
        "dc,crq->drq", chosen.astype(jnp.bfloat16), encoded, preferred_element_type=jnp.float32
    ).astype(jnp.bfloat16)
    incoming = lax.all_to_all(outgoing, "dp", split_axis=0, concat_axis=0, tiled=True)
    sent_rows = incoming.shape[1]
    valid = jnp.any(table == my_rank, axis=1).astype(jnp.int32)
    order = jnp.cumsum(valid) - valid
    counted = jnp.sum(valid)
    positions = jnp.arange(section, dtype=jnp.int32)
    block = positions // crop_span
    within = positions % crop_span
    slot_ids = jnp.arange(section // crop_span + 1, dtype=jnp.int32)
    matched = (valid[None, :] == 1) & (order[None, :] == slot_ids[:, None])
    slot_source = jnp.sum(jnp.where(matched, sources[None, :], 0), axis=1)
    row_source = jnp.sum(
        jnp.where(block[:, None] == slot_ids[None, :], slot_source[None, :], 0), axis=1
    )
    row_index = row_source * sent_rows + jnp.minimum(within, sent_rows - 1)
    picked = jnp.take(incoming.reshape(dp_count * sent_rows, columns), row_index, axis=0)
    image = block < counted
    text = text_embed[0]
    crop_pos = image & (within < crop_rows)
    line_pos = image & (within == crop_rows)
    hidden = jnp.where(
        crop_pos[:, None], picked, jnp.where(line_pos[:, None], newline[None, :], text)
    )
    wide = hidden.astype(jnp.float32)
    row_total = lax.psum(jnp.sum(wide * wide, -1), "tensor")
    normed = (
        wide
        * lax.rsqrt(row_total / (columns * tp_count) + eps)[:, None]
        * norm_gain.astype(jnp.float32)
    ).astype(jnp.bfloat16)
    pair_cols = xz_weight.shape[1]
    step_cols = dt_weight.shape[1]
    piece = lax.all_gather(normed, "dp", axis=0, tiled=True)
    terms = jnp.concatenate(
        [
            jnp.dot(piece, xz_weight, preferred_element_type=jnp.float32),
            jnp.dot(piece, dt_weight, preferred_element_type=jnp.float32),
            jnp.dot(piece, bc_weight, preferred_element_type=jnp.float32),
        ],
        axis=1,
    )
    pair_mine, step_mine = (
        lax.psum_scatter(
            terms[:, :pair_cols].astype(jnp.bfloat16), "tensor", scatter_dimension=1, tiled=True
        ).astype(jnp.float32),
        lax.psum_scatter(
            terms[:, pair_cols : pair_cols + step_cols].astype(jnp.bfloat16),
            "tensor",
            scatter_dimension=1,
            tiled=True,
        ).astype(jnp.float32),
    )
    map_terms = terms[:, pair_cols + step_cols :]
    maps_all = lax.psum(map_terms.astype(jnp.bfloat16), "tensor").astype(jnp.float32)
    pairs = pair_mine.reshape(dp_count, section, heads_dev, 2, head_width)
    values = pairs[:, :, :, 0, :].reshape(dp_count, section, heads_dev * head_width)
    gates = pairs[:, :, :, 1, :]
    fresh = jnp.concatenate([values, maps_all.reshape(dp_count, section, 2 * state_size)], axis=2)
    kernel = jnp.concatenate([conv_x, conv_bc], axis=1).astype(jnp.float32)
    taps = kernel.shape[0]
    edge = passed_along(fresh[:, section - (taps - 1) :, :], "segment", 1)
    padded = jnp.concatenate([edge, fresh], axis=1)
    filtered = kernel[0] * padded[:, 0:section]
    for offset in range(1, taps):
        filtered = filtered + kernel[offset] * padded[:, offset : offset + section]
    activated = jax.nn.silu(filtered)
    inner_cols = heads_dev * head_width
    streams = activated[..., :inner_cols].reshape(dp_count, section, heads_dev, head_width)
    b_rows = activated[..., inner_cols : inner_cols + state_size]
    c_rows = activated[..., inner_cols + state_size :]
    step = jax.nn.softplus(step_mine.reshape(dp_count, section, heads_dev) + dt_bias)
    cumulative = jnp.cumsum(-jnp.exp(a_log) * step, axis=1)
    scores = jnp.einsum("nls,nms->nlm", c_rows, b_rows, precision=highest)
    mask = (positions[:, None] >= positions[None, :])[None, :, :, None]
    gaps = cumulative[:, :, None, :] - cumulative[:, None, :, :]
    weights = (
        jnp.where(mask, jnp.exp(jnp.where(mask, gaps, 0.0)), 0.0)
        * scores[..., None]
        * step[:, None, :, :]
    )
    inside = jnp.einsum("nlmh,nmhp->nlhp", weights, streams, precision=highest)
    final = cumulative[:, -1, :]
    carry_weight = jnp.exp(final[:, None, :] - cumulative) * step
    local_state = jnp.einsum("nlh,nls,nlhp->nhsp", carry_weight, b_rows, streams, precision=highest)
    decay = jnp.exp(final)
    prior = jnp.zeros_like(local_state)
    for turn in range(segment_count - 1):
        prior = passed_along(
            (decay[:, :, None, None] * prior + local_state).astype(jnp.bfloat16), "segment", 1
        ).astype(jnp.float32)
    across = jnp.exp(cumulative)[..., None] * jnp.einsum(
        "nls,nhsp->nlhp", c_rows, prior, precision=highest
    )
    outputs = inside + across + skip[None, None, :, None] * streams
    gated = outputs * jax.nn.silu(gates)
    group_total = lax.psum(jnp.sum(gated * gated, axis=(2, 3)), "tensor")
    scale = lax.rsqrt(group_total / (inner_cols * tp_count) + eps)
    normed_out = (
        gated * scale[..., None, None] * out_gain.astype(jnp.float32).reshape(heads_dev, head_width)
    ).astype(jnp.bfloat16)
    normed_out = normed_out.reshape(dp_count * section, inner_cols)
    term = jnp.dot(
        lax.all_gather(normed_out, "tensor", axis=1, tiled=True),
        out_weight,
        preferred_element_type=jnp.float32,
    )
    mixed = lax.psum_scatter(
        term.astype(jnp.bfloat16), "dp", scatter_dimension=0, tiled=True
    ).astype(jnp.float32)
    return (wide + mixed).astype(jnp.bfloat16)[None]


def contract(a, b, dims, precision=None):
    return lax.dot_general(
        a, b, (dims, ((), ())), precision=precision, preferred_element_type=F32
    )


def eye(n):
    return (
        lax.broadcasted_iota(jnp.int32, (n, n), 0) == lax.broadcasted_iota(jnp.int32, (n, n), 1)
    ).astype(F32)


def columns_of(rows):
    return contract(eye(rows.shape[1]), rows, ((1,), (1,)), HIGHEST)


def silu(a):
    return a / (1.0 + jnp.exp(-a))


def enter_body(
    table, dt_bias, a_log, skip, feats_mine, feats_other, vision_gain, proj, text, text_other,
    newline, gain, xz, bc, dt, conv_x, out_gain,
    crops_out, rows_out, keep_x_out, send_x_out, keep_out, send_out,
    feats, normed, proj_tiles, tails, weights, crops, rows, first, maps, sems, out_sems,
):
    half = tails.shape[1]
    tiles, _, tile = proj_tiles.shape
    columns = rows.shape[1]
    load_feats = [
        pltpu.make_async_copy(feats_mine, feats.at[0], sems.at[0]),
        pltpu.make_async_copy(feats_other, feats.at[1], sems.at[1]),
    ]
    load_proj = [
        pltpu.make_async_copy(proj.at[:, pl.ds(i * tile, tile)], proj_tiles.at[i], sems.at[2 + i])
        for i in range(tiles)
    ]
    load_tails = [
        pltpu.make_async_copy(text.at[pl.ds(half, half), :], tails.at[0], sems.at[2 + tiles]),
        pltpu.make_async_copy(text_other.at[pl.ds(half, half), :], tails.at[1], sems.at[3 + tiles]),
    ]
    load_weights = [
        pltpu.make_async_copy(
            xz.at[:, pl.ds(i * 256, 128)],
            weights.at[i // 2, :, pl.ds(i % 2 * 128, 128)],
            sems.at[4 + tiles + i],
        )
        for i in range(4)
    ]
    load_weights.append(pltpu.make_async_copy(bc, weights.at[2], sems.at[8 + tiles]))
    for copy in load_feats + load_proj[:2] + load_tails + load_proj[2:] + load_weights:
        copy.start()
    gain_row = gain[...].reshape(1, -1)
    rank = lax.axis_index("dp")
    stays = table[0, 0, rank] == rank
    load_feats[0].wait()
    load_feats[1].wait()
    for index in range(2):
        block = jnp.where(stays, feats[index], feats[1 - index]).astype(F32)
        scale = lax.rsqrt(jnp.mean(block * block, -1, keepdims=True) + EPS)
        normed[index * half : (index + 1) * half, :] = (
            block * scale * vision_gain[...].reshape(1, -1).astype(F32)
        ).astype(BF16)
    ones = jnp.ones((8, 128), BF16)

    def folded(block):
        total = jnp.zeros((block.shape[0], 128), F32)
        for start in range(0, block.shape[1], 128):
            piece = block[:, start : start + 128].astype(F32)
            total = total + piece * piece
        return total

    squares = [None] * 4
    for i in range(tiles):
        load_proj[i].wait()
        cols = slice(i * tile, (i + 1) * tile)
        result = jnp.dot(normed[...], proj_tiles[i], preferred_element_type=F32).astype(BF16)
        crops[:, cols] = result
        scaled = result * gain_row[:, cols]
        rows[0:half, cols] = scaled[:half]
        rows[2 * half : 3 * half, cols] = scaled[half:]
        for index in range(2):
            more = folded(result[index * half : (index + 1) * half])
            squares[2 * index] = more if i == 0 else squares[2 * index] + more
        if i < 2:
            load_tails[i].wait()
            head = tails[i, 0:8, :].astype(F32)
            line = newline[...].reshape(1, -1).astype(F32)
            top = lax.broadcasted_iota(jnp.int32, (8, 1), 0) == 0
            tails[i, 0:8, :] = jnp.where(top, line, head).astype(BF16)
            main = tails[i]
            base = (2 * i + 1) * half
            rows[base : base + half, :] = main * gain_row
            squares[2 * i + 1] = folded(main)
    departures = [
        pltpu.make_async_copy(crops, crops_out, out_sems.at[0]),
        pltpu.make_async_copy(rows, rows_out, out_sems.at[1]),
    ]
    for copy in departures:
        copy.start()
    for copy in load_weights:
        copy.wait()
    chip = lax.axis_index("tensor")
    lane = lax.broadcasted_iota(jnp.int32, (1, 128), 1)
    own = [conv_x[...].astype(F32), out_gain[...].reshape(1, 128).astype(F32)]
    for value in (dt_bias[0], a_log[0], skip[0]):
        whole = jnp.full((1, 128), value, F32)
        high = whole.astype(BF16).astype(F32)
        middle = (whole - high).astype(BF16).astype(F32)
        low = whole - high - middle
        pieces = jnp.where(lane < 32, high, jnp.where(lane < 64, middle, low))
        own.append(jnp.where(lane < 96, pieces, 0.0))
    own = jnp.concatenate(own, 0)
    slots = jnp.concatenate([jnp.where(chip == slot, own, 0.0) for slot in range(4)], 1)

    def parted(source, keep, send, part, sem):
        goes = pltpu.make_async_copy(source.at[part], send.at[part // 2], sem)
        remains = pltpu.make_async_copy(source.at[part], keep.at[part // 2], sem)
        here = chip % 2 == part % 2
        pl.when(here)(remains.start)
        pl.when(jnp.logical_not(here))(goes.start)
        departures.append(goes)

    for part in range(4):
        main = rows[part * half : (part + 1) * half, :]
        maps[part] = jnp.dot(main, weights[2], preferred_element_type=F32).astype(BF16)
        parted(maps, keep_out, send_out, part, out_sems.at[6 + part])
    for part in range(4):
        main = rows[part * half : (part + 1) * half, :]
        for i in range(2):
            first[part, 0:half, i * 256 : i * 256 + 256] = jnp.dot(
                main, weights[i], preferred_element_type=F32
            ).astype(BF16)
        steps = contract(dt[...], main, ((1,), (1,)))
        sums = contract(ones, squares[part].astype(BF16), ((1,), (1,)))
        sums = jnp.concatenate([steps[0:4], sums[0:4]], 0)
        sums = jnp.concatenate([sums, jnp.zeros((8, 512 - half), F32)], 1)
        first[part, half : half + 16, :] = jnp.concatenate([sums, slots], 0).astype(BF16)
        parted(first, keep_x_out, send_x_out, part, out_sems.at[2 + part])
    for copy in departures:
        copy.wait()


def enter(
    table, dt_bias, a_log, skip, feats_mine, feats_other, vision_gain, proj, text, text_other,
    newline, gain, xz, bc, dt, conv_x, out_gain,
):
    half, vision = feats_mine.shape
    columns = text.shape[1]
    tiles = 4
    whole = pl.BlockSpec(memory_space=pl.ANY)
    near = pl.BlockSpec(memory_space=pltpu.VMEM)
    return pl.pallas_call(
        enter_body,
        in_specs=[pl.BlockSpec(memory_space=pltpu.SMEM)] * 4
        + [whole, whole, near, whole, whole, whole]
        + [near, near, whole, whole, near, near, near],
        out_specs=[whole] * 6,
        out_shape=[
            jax.ShapeDtypeStruct((2 * half, columns), BF16),
            jax.ShapeDtypeStruct((4 * half, columns), BF16),
            jax.ShapeDtypeStruct((2, half + 16, 512), BF16),
            jax.ShapeDtypeStruct((2, half + 16, 512), BF16),
            jax.ShapeDtypeStruct((2, half, 256), BF16),
            jax.ShapeDtypeStruct((2, half, 256), BF16),
        ],
        scratch_shapes=[
            pltpu.VMEM((2, half, vision), BF16),
            pltpu.VMEM((2 * half, vision), BF16),
            pltpu.VMEM((tiles, vision, columns // tiles), BF16),
            pltpu.VMEM((2, half, columns), BF16),
            pltpu.VMEM((3, columns, 256), BF16),
            pltpu.VMEM((2 * half, columns), BF16),
            pltpu.VMEM((4 * half, columns), BF16),
            pltpu.VMEM((4, half + 16, 512), BF16),
            pltpu.VMEM((4, half, 256), BF16),
            pltpu.SemaphoreType.DMA((9 + tiles,)),
            pltpu.SemaphoreType.DMA((10,)),
        ],
        name="enter",
    )(
        table, dt_bias, a_log, skip, feats_mine, feats_other, vision_gain, proj, text, text_other,
        newline, gain, xz, bc, dt, conv_x, out_gain,
    )


def gates_body(rows_hbm, xz, keep_out, send_out, rows, weights, results, sems, out_sems):
    half = results.shape[1]
    chip = lax.axis_index("tensor")
    load_weights = [
        pltpu.make_async_copy(
            xz.at[:, pl.ds(i * 256 + 128, 128)],
            weights.at[i // 2, :, pl.ds(i % 2 * 128, 128)],
            sems.at[4 + i],
        )
        for i in range(4)
    ]
    load_rows = [
        pltpu.make_async_copy(rows_hbm.at[pl.ds(part * half, half), :], rows.at[part], sems.at[part])
        for part in range(4)
    ]
    for copy in load_rows[:1] + load_weights + load_rows[1:]:
        copy.start()
    departures = []
    for part in range(4):
        load_rows[part].wait()
        for i in range(2):
            if part == 0:
                load_weights[2 * i].wait()
                load_weights[2 * i + 1].wait()
            results[part, :, 256 * i : 256 * i + 256] = jnp.dot(
                rows[part], weights[i], preferred_element_type=F32
            ).astype(BF16)
        goes = pltpu.make_async_copy(results.at[part], send_out.at[part // 2], out_sems.at[part])
        remains = pltpu.make_async_copy(results.at[part], keep_out.at[part // 2], out_sems.at[part])
        here = chip % 2 == part % 2
        pl.when(here)(remains.start)
        pl.when(jnp.logical_not(here))(goes.start)
        departures.append(goes)
    for copy in departures:
        copy.wait()


def gates(rows, xz):
    half, columns = rows.shape[0] // 4, rows.shape[1]
    whole = pl.BlockSpec(memory_space=pl.ANY)
    return pl.pallas_call(
        gates_body,
        in_specs=[whole, whole],
        out_specs=[whole, whole],
        out_shape=[jax.ShapeDtypeStruct((2, half, 512), BF16)] * 2,
        scratch_shapes=[
            pltpu.VMEM((4, half, columns), BF16),
            pltpu.VMEM((2, columns, 256), BF16),
            pltpu.VMEM((4, half, 512), BF16),
            pltpu.SemaphoreType.DMA((8,)),
            pltpu.SemaphoreType.DMA((4,)),
        ],
        name="gates",
    )(rows, xz)


def filtered(main, edge, taps):
    rows = main.shape[0]
    padded = jnp.concatenate([edge, main], 0)
    count = taps.shape[0]
    total = taps[count - 1 : count] * main
    for back in range(1, count):
        total = total + taps[count - 1 - back : count - back] * padded[8 - back : 8 - back + rows]
    return total


def scan_body(
    width, kept_x, received_x, kept, received, before, taps_maps, streams, maps, meta, state, params
):
    first = kept_x[...].astype(F32) + received_x[...].astype(F32)
    half = first.shape[0] - 16
    slots = first[half + 8 : half + 16]
    params[...] = slots
    sums = first[half : half + 8, 0:half]
    scale = lax.rsqrt(sums[4:5] / width + EPS)
    sums_before = before[8:16, half - 128 : half].astype(F32)
    scale_before = lax.rsqrt(sums_before[4:5] / width + EPS)
    head = lax.broadcasted_iota(jnp.int32, (8, 512), 1) // 128
    owner = (head == lax.broadcasted_iota(jnp.int32, (8, 512), 0)).astype(F32)
    scalars = slots[5:8]
    bias = jnp.sum(owner * scalars[0:1], 1, keepdims=True) * (1.0 / 32)
    rate = jnp.sum(owner * scalars[1:2], 1, keepdims=True) * (1.0 / 32)
    raw = sums * scale + bias
    step = jnp.maximum(raw, 0.0) + jnp.log1p(jnp.exp(-jnp.abs(raw)))
    decays = -jnp.exp(rate) * step
    upper = (
        lax.broadcasted_iota(jnp.int32, (half, half), 0)
        <= lax.broadcasted_iota(jnp.int32, (half, half), 1)
    ).astype(F32)
    cumulative = contract(decays, upper, ((1,), (0,)), HIGHEST)
    final = cumulative[:, half - 1 : half]
    carry = jnp.exp(final - cumulative) * step
    scale_main = columns_of(jnp.broadcast_to(scale, (8, half)))[:, 0:1]
    scale_edge = columns_of(jnp.broadcast_to(scale_before, (8, 128)))[120:128, 0:1]
    taps_x = slots[0:4]
    edge = before[0:8, :].astype(F32) * scale_edge
    x = silu(filtered(first[0:half] * scale_main, edge[:, 0:512], taps_x))
    both = silu(
        filtered(
            (kept[...].astype(F32) + received[...].astype(F32)) * scale_main,
            edge[:, 512:768],
            taps_maps[...].astype(F32),
        )
    ).astype(BF16)
    carried = contract(columns_of(carry), owner, ((1,), (0,)), HIGHEST)
    state[0:128, :] = contract(both[:, 0:128], (x * carried).astype(BF16), ((0,), (0,))).astype(BF16)
    total = jnp.sum(jnp.exp(final) * owner, 0, keepdims=True)
    state[128:144, :] = jnp.broadcast_to(total, (16, 512)).astype(BF16)
    streams[...] = x.astype(BF16)
    maps[...] = both
    meta[0:8, :] = cumulative
    meta[8:16, :] = step
    meta[16:24, :] = jnp.broadcast_to(scale, (8, half))


def scan(width, *operands):
    half = operands[2].shape[0]
    return pl.pallas_call(
        lambda *refs: scan_body(width, *refs),
        out_shape=[
            jax.ShapeDtypeStruct((half, 512), BF16),
            jax.ShapeDtypeStruct((half, 256), BF16),
            jax.ShapeDtypeStruct((24, half), F32),
            jax.ShapeDtypeStruct((144, 512), BF16),
            jax.ShapeDtypeStruct((8, 512), F32),
        ],
        name="scan",
    )(*operands)


def join_body(state, partner, out):
    late = lax.axis_index("tensor") % 2 == 1
    mine, other = state[...].astype(F32), partner[...].astype(F32)
    first, second = jnp.where(late, other, mine), jnp.where(late, mine, other)
    out[0:128, :] = (second[128:129] * first[0:128] + second[0:128]).astype(BF16)
    out[128:144, :] = (first[128:144] * second[128:144]).astype(BF16)


def join(state, partner):
    return pl.pallas_call(
        join_body, out_shape=jax.ShapeDtypeStruct(state.shape, BF16), name="join"
    )(state, partner)


def inside_body(streams, maps, meta, params, out):
    half = streams.shape[0]
    cumulative = meta[0:8, :]
    step = meta[8:16, :]
    cum_cols = columns_of(cumulative)
    scores = contract(maps[:, 128:256], maps[:, 0:128], ((1,), (1,)))
    lower = lax.broadcasted_iota(jnp.int32, (half, half), 0) >= lax.broadcasted_iota(
        jnp.int32, (half, half), 1
    )
    scores = jnp.where(lower, scores, 0.0)
    for head in range(4):
        cols = slice(128 * head, 128 * head + 128)
        x = streams[:, cols]
        gaps = cum_cols[:, head : head + 1] - cumulative[head : head + 1]
        weights = jnp.exp(jnp.where(lower, gaps, 0.0)) * scores * step[head : head + 1]
        y = jnp.dot(weights.astype(BF16), x, preferred_element_type=F32)
        through = jnp.sum(params[7:8, cols], 1, keepdims=True) * (1.0 / 32)
        out[:, cols] = y + through * x.astype(F32)


def inside(streams, maps, meta, params):
    return pl.pallas_call(
        inside_body,
        out_shape=jax.ShapeDtypeStruct(streams.shape, F32),
        name="inside",
    )(streams, maps, meta, params)


def gate_body(kept, received, local, maps, meta, params, partner, *others_and_out):
    *others, out = others_and_out
    half = local.shape[0]
    section = lax.axis_index("segment")
    late = lax.axis_index("tensor") % 2 == 1
    prior = jnp.zeros((128, 512), F32)
    for source in range(len(others)):
        bits = jnp.bitwise_xor(section, source)
        piece = others[0][...]
        for index in range(1, len(others)):
            piece = jnp.where(bits == index + 1, others[index][...], piece)
        piece = piece.astype(F32)
        prior = jnp.where(source < section, piece[128:129] * prior + piece[0:128], prior)
    before = partner[...].astype(F32)
    prior = jnp.where(late, before[128:129] * prior + before[0:128], prior)
    scale = columns_of(meta[16:24, :])[:, 0:1]
    entry = jnp.exp(columns_of(meta[0:8, :]))
    across = jnp.dot(maps[:, 128:256], prior.astype(BF16), preferred_element_type=F32)
    gated = []
    squares = jnp.zeros((half, 1), F32)
    for head in range(4):
        cols = slice(128 * head, 128 * head + 128)
        y = local[:, cols] + entry[:, head : head + 1] * across[:, cols]
        gates = kept[:, cols].astype(F32) + received[:, cols].astype(F32)
        value = y * silu(gates * scale)
        squares = squares + jnp.sum(value * value, -1, keepdims=True)
        gated.append(value)
    norm = lax.rsqrt(squares / 512 + EPS)
    for head in range(4):
        cols = slice(128 * head, 128 * head + 128)
        out[:, cols] = (gated[head] * norm * params[4:5, cols]).astype(BF16)


def gate(local, *operands):
    return pl.pallas_call(
        gate_body, out_shape=jax.ShapeDtypeStruct(local.shape, BF16), name="gate"
    )(*operands[:2], local, *operands[2:])


def per_device_halves(
    text_embed, crop_feats, crop_dest, vision_gain, proj_weight, newline, norm_gain, xz_weight,
    dt_weight, bc_weight, conv_x, conv_bc, dt_bias, a_log, skip, out_gain, out_weight,
):
    my_chip = lax.axis_index("tensor")
    segment_count = lax.axis_size("segment")
    text = text_embed[0]
    section, columns = text.shape
    half = section // 2
    width = columns * lax.axis_size("tensor")
    feats = crop_feats[0, 0, 0]
    feats_other = swapped(feats, "dp", 1)
    text_other = swapped(text, "dp", 1)
    crops, rows, keep_x, send_x, keep, send = enter(
        crop_dest.transpose(0, 2, 1), dt_bias, a_log, skip, feats, feats_other, vision_gain,
        proj_weight, text, text_other, newline, norm_gain, xz_weight, bc_weight, dt_weight.T,
        conv_x, out_gain,
    )
    out_weight, newline, rows = lax.optimization_barrier((out_weight, newline, rows))
    lower = my_chip < 2

    def added(keep, arrived):
        pair = keep.astype(F32) + arrived.astype(F32)
        leaves = jnp.where(lower, pair[1], pair[0]).astype(BF16)
        return leaves, jnp.where(lower, pair[0], pair[1]).astype(BF16)

    keep_gates, send_gates = gates(rows, xz_weight)
    leaves, kept = added(keep, swapped(send, "tensor", 1))
    leaves, kept, send_x, send_gates, out_weight = lax.optimization_barrier(
        (leaves, kept, send_x, send_gates, out_weight)
    )
    received = swapped(leaves, "tensor", 2)
    leaves_x, kept_x = added(keep_x, swapped(send_x, "tensor", 1))
    leaves_x, kept_x, send_gates, received = lax.optimization_barrier(
        (leaves_x, kept_x, send_gates, received)
    )
    received_x = swapped(leaves_x, "tensor", 2)
    arrived_gates = swapped(send_gates, "tensor", 1)
    weight_other = swapped(out_weight, "dp", 1)
    weights = (
        jnp.where(lower, out_weight, weight_other), jnp.where(lower, weight_other, out_weight)
    )
    late = my_chip % 2 == 1
    head = crops[:half]
    tail = jnp.where(jnp.arange(half)[:, None] == 0, newline[None], text[half:])
    hidden = (jnp.where(late, tail, head), jnp.where(late, head, tail))
    kept_x, received_x, weights, hidden = lax.optimization_barrier(
        (kept_x, received_x, weights, hidden)
    )
    route = [(i, i + 1) for i in range(0, 4 * segment_count, 2)]
    route += [(i, i + 3) for i in range(1, 4 * segment_count - 4, 2)]
    ends = (kept[half - 8 :].astype(F32) + received[half - 8 :].astype(F32)).astype(BF16)
    before = slice(half - 8, half + 8)
    before = (kept_x[before].astype(F32) + received_x[before].astype(F32)).astype(BF16)
    before = jnp.concatenate([before, jnp.pad(ends, ((0, 8), (0, 0)))], 1)
    before = lax.ppermute(before, ("segment", "tensor"), route)
    streams, maps, meta, state, params = scan(
        width, kept_x, received_x, kept, received, before, conv_bc
    )
    meta, keep_gates = lax.optimization_barrier((meta, keep_gates))
    local = inside(streams, maps, meta, params)
    partner = swapped(state, "tensor", 1)
    whole = join(state, partner)
    whole, local = lax.optimization_barrier((whole, local))
    others = [swapped(whole, "segment", bits) for bits in range(1, segment_count)]
    leaves, kept = added(keep_gates, arrived_gates)
    received = swapped(leaves, "tensor", 2)
    normed = gate(local, kept, received, maps, meta, params, partner, *others)
    near, far, here = (
        lax.ppermute(
            normed, ("dp", "tensor"), [(i, (i if i % 4 < 2 else i ^ 4) ^ bits) for i in range(8)]
        )
        for bits in (1, 2, 0)
    )
    both = swapped(far, "tensor", 1)
    out = jnp.zeros((section, columns), BF16)
    for index, pair in enumerate(((here, far), (near, both))):
        mixed = jnp.dot(pair[0], weights[0], preferred_element_type=F32)
        mixed = mixed + jnp.dot(pair[1], weights[1], preferred_element_type=F32)
        block = (hidden[index].astype(F32) + mixed).astype(BF16)
        start = jnp.where(late, half, 0) if index == 0 else jnp.where(late, 0, half)
        out = lax.dynamic_update_slice(out, block, (start, 0))
    return out[None]


def per_device(*args):
    text_embed, crop_feats = args[0], args[1]
    sizes = tuple(lax.axis_size(axis) for axis in ("segment", "dp", "tensor"))
    heads_dev = args[12].shape[0]
    head_width = args[15].shape[0] // heads_dev
    state_size = args[9].shape[1] // 2
    fits = (
        sizes == (4, 2, 4)
        and heads_dev == 1
        and (head_width, state_size) == (128, 128)
        and crop_feats.shape[2:4] == (1, 256)
        and text_embed.shape[1] == 512
    )
    return (per_device_halves if fits else per_device_any)(*args)


def solution(mesh):
    return jax.shard_map(
        per_device,
        mesh=mesh,
        in_specs=(
            P("dp", "segment", "tensor"),
            P("segment", "dp", None, None, None),
            P("segment", None, None),
            P(),
            P(None, "tensor"),
            P("tensor"),
            P("tensor"),
            P("tensor", "dp"),
            P("tensor", "dp"),
            P("tensor", "dp"),
            P(None, ("dp", "tensor")),
            P(None, "dp"),
            P(("dp", "tensor")),
            P(("dp", "tensor")),
            P(("dp", "tensor")),
            P(("dp", "tensor")),
            P("dp", "tensor"),
        ),
        out_specs=P("dp", "segment", "tensor"),
        check_vma=False,
    )
```

```python
import jax
import jax.numpy as jnp
from jax import lax
from jax.experimental import pallas as pl
from jax.experimental.pallas import tpu as pltpu
from jax.sharding import PartitionSpec as P

EPS = 1e-05
F32 = jnp.float32
BF16 = jnp.bfloat16
HIGHEST = lax.Precision.HIGHEST


def passed_along(block, axis, distance):
    devices = range(lax.axis_size(axis))
    route = [(i - distance, i) for i in devices if i - distance in devices]
    return lax.ppermute(block, axis, route)


def swapped(block, axis, bits):
    return lax.ppermute(block, axis, [(i, i ^ bits) for i in range(lax.axis_size(axis))])


def per_device_any(
    text_embed,
    crop_feats,
    crop_dest,
    vision_gain,
    proj_weight,
    newline,
    norm_gain,
    xz_weight,
    dt_weight,
    bc_weight,
    conv_x,
    conv_bc,
    dt_bias,
    a_log,
    skip,
    out_gain,
    out_weight,
):
    highest = lax.Precision.HIGHEST
    eps = 1e-05
    dp_count = lax.axis_size("dp")
    tp_count = lax.axis_size("tensor")
    segment_count = lax.axis_size("segment")
    my_rank = lax.axis_index("dp")
    section = text_embed.shape[1]
    columns = text_embed.shape[2]
    crop_count = crop_feats.shape[2]
    crop_rows = crop_feats.shape[3]
    crop_span = crop_rows + 1
    heads_dev = dt_bias.shape[0]
    head_width = out_gain.shape[0] // heads_dev
    state_size = bc_weight.shape[1] // 2
    feats = crop_feats[0, 0].astype(jnp.float32)
    vision = (
        feats
        * lax.rsqrt(jnp.mean(feats * feats, -1, keepdims=True) + eps)
        * vision_gain.astype(jnp.float32)
    ).astype(jnp.bfloat16)
    encoded = jnp.dot(
        vision.reshape(crop_count * crop_rows, -1), proj_weight, preferred_element_type=jnp.float32
    )
    encoded = encoded.astype(jnp.bfloat16).reshape(crop_count, crop_rows, columns)
    table = crop_dest[0]
    sources = jnp.arange(dp_count, dtype=jnp.int32)
    mine = jnp.sum(jnp.where(sources[:, None] == my_rank, table, 0), axis=0)
    chosen = mine[None, :] == sources[:, None]
    outgoing = jnp.einsum(
        "dc,crq->drq", chosen.astype(jnp.bfloat16), encoded, preferred_element_type=jnp.float32
    ).astype(jnp.bfloat16)
    incoming = lax.all_to_all(outgoing, "dp", split_axis=0, concat_axis=0, tiled=True)
    sent_rows = incoming.shape[1]
    valid = jnp.any(table == my_rank, axis=1).astype(jnp.int32)
    order = jnp.cumsum(valid) - valid
    counted = jnp.sum(valid)
    positions = jnp.arange(section, dtype=jnp.int32)
    block = positions // crop_span
    within = positions % crop_span
    slot_ids = jnp.arange(section // crop_span + 1, dtype=jnp.int32)
    matched = (valid[None, :] == 1) & (order[None, :] == slot_ids[:, None])
    slot_source = jnp.sum(jnp.where(matched, sources[None, :], 0), axis=1)
    row_source = jnp.sum(
        jnp.where(block[:, None] == slot_ids[None, :], slot_source[None, :], 0), axis=1
    )
    row_index = row_source * sent_rows + jnp.minimum(within, sent_rows - 1)
    picked = jnp.take(incoming.reshape(dp_count * sent_rows, columns), row_index, axis=0)
    image = block < counted
    text = text_embed[0]
    crop_pos = image & (within < crop_rows)
    line_pos = image & (within == crop_rows)
    hidden = jnp.where(
        crop_pos[:, None], picked, jnp.where(line_pos[:, None], newline[None, :], text)
    )
    wide = hidden.astype(jnp.float32)
    row_total = lax.psum(jnp.sum(wide * wide, -1), "tensor")
    normed = (
        wide
        * lax.rsqrt(row_total / (columns * tp_count) + eps)[:, None]
        * norm_gain.astype(jnp.float32)
    ).astype(jnp.bfloat16)
    pair_cols = xz_weight.shape[1]
    step_cols = dt_weight.shape[1]
    piece = lax.all_gather(normed, "dp", axis=0, tiled=True)
    terms = jnp.concatenate(
        [
            jnp.dot(piece, xz_weight, preferred_element_type=jnp.float32),
            jnp.dot(piece, dt_weight, preferred_element_type=jnp.float32),
            jnp.dot(piece, bc_weight, preferred_element_type=jnp.float32),
        ],
        axis=1,
    )
    pair_mine, step_mine = (
        lax.psum_scatter(
            terms[:, :pair_cols].astype(jnp.bfloat16), "tensor", scatter_dimension=1, tiled=True
        ).astype(jnp.float32),
        lax.psum_scatter(
            terms[:, pair_cols : pair_cols + step_cols].astype(jnp.bfloat16),
            "tensor",
            scatter_dimension=1,
            tiled=True,
        ).astype(jnp.float32),
    )
    map_terms = terms[:, pair_cols + step_cols :]
    maps_all = lax.psum(map_terms.astype(jnp.bfloat16), "tensor").astype(jnp.float32)
    pairs = pair_mine.reshape(dp_count, section, heads_dev, 2, head_width)
    values = pairs[:, :, :, 0, :].reshape(dp_count, section, heads_dev * head_width)
    gates = pairs[:, :, :, 1, :]
    fresh = jnp.concatenate([values, maps_all.reshape(dp_count, section, 2 * state_size)], axis=2)
    kernel = jnp.concatenate([conv_x, conv_bc], axis=1).astype(jnp.float32)
    taps = kernel.shape[0]
    edge = passed_along(fresh[:, section - (taps - 1) :, :], "segment", 1)
    padded = jnp.concatenate([edge, fresh], axis=1)
    filtered = kernel[0] * padded[:, 0:section]
    for offset in range(1, taps):
        filtered = filtered + kernel[offset] * padded[:, offset : offset + section]
    activated = jax.nn.silu(filtered)
    inner_cols = heads_dev * head_width
    streams = activated[..., :inner_cols].reshape(dp_count, section, heads_dev, head_width)
    b_rows = activated[..., inner_cols : inner_cols + state_size]
    c_rows = activated[..., inner_cols + state_size :]
    step = jax.nn.softplus(step_mine.reshape(dp_count, section, heads_dev) + dt_bias)
    cumulative = jnp.cumsum(-jnp.exp(a_log) * step, axis=1)
    scores = jnp.einsum("nls,nms->nlm", c_rows, b_rows, precision=highest)
    mask = (positions[:, None] >= positions[None, :])[None, :, :, None]
    gaps = cumulative[:, :, None, :] - cumulative[:, None, :, :]
    weights = (
        jnp.where(mask, jnp.exp(jnp.where(mask, gaps, 0.0)), 0.0)
        * scores[..., None]
        * step[:, None, :, :]
    )
    inside = jnp.einsum("nlmh,nmhp->nlhp", weights, streams, precision=highest)
    final = cumulative[:, -1, :]
    carry_weight = jnp.exp(final[:, None, :] - cumulative) * step
    local_state = jnp.einsum("nlh,nls,nlhp->nhsp", carry_weight, b_rows, streams, precision=highest)
    decay = jnp.exp(final)
    prior = jnp.zeros_like(local_state)
    for turn in range(segment_count - 1):
        prior = passed_along(
            (decay[:, :, None, None] * prior + local_state).astype(jnp.bfloat16), "segment", 1
        ).astype(jnp.float32)
    across = jnp.exp(cumulative)[..., None] * jnp.einsum(
        "nls,nhsp->nlhp", c_rows, prior, precision=highest
    )
    outputs = inside + across + skip[None, None, :, None] * streams
    gated = outputs * jax.nn.silu(gates)
    group_total = lax.psum(jnp.sum(gated * gated, axis=(2, 3)), "tensor")
    scale = lax.rsqrt(group_total / (inner_cols * tp_count) + eps)
    normed_out = (
        gated * scale[..., None, None] * out_gain.astype(jnp.float32).reshape(heads_dev, head_width)
    ).astype(jnp.bfloat16)
    normed_out = normed_out.reshape(dp_count * section, inner_cols)
    term = jnp.dot(
        lax.all_gather(normed_out, "tensor", axis=1, tiled=True),
        out_weight,
        preferred_element_type=jnp.float32,
    )
    mixed = lax.psum_scatter(
        term.astype(jnp.bfloat16), "dp", scatter_dimension=0, tiled=True
    ).astype(jnp.float32)
    return (wide + mixed).astype(jnp.bfloat16)[None]


def contract(a, b, dims, precision=None):
    return lax.dot_general(
        a, b, (dims, ((), ())), precision=precision, preferred_element_type=F32
    )


def eye(n):
    return (
        lax.broadcasted_iota(jnp.int32, (n, n), 0) == lax.broadcasted_iota(jnp.int32, (n, n), 1)
    ).astype(F32)


def columns_of(rows):
    return contract(eye(rows.shape[1]), rows, ((1,), (1,)), HIGHEST)


def silu(a):
    return a / (1.0 + jnp.exp(-a))


def enter_body(
    table, dt_bias, a_log, skip, feats_mine, feats_other, vision_gain, proj, text, text_other,
    newline, gain, xz, bc, dt, conv_x, out_gain,
    crops_out, rows_out, keep_x_out, send_x_out, keep_out, send_out,
    feats, normed, proj_tiles, tails, weights, crops, rows, first, maps, sems, out_sems,
):
    half = tails.shape[1]
    tiles, _, tile = proj_tiles.shape
    columns = rows.shape[1]
    load_feats = [
        pltpu.make_async_copy(feats_mine, feats.at[0], sems.at[0]),
        pltpu.make_async_copy(feats_other, feats.at[1], sems.at[1]),
    ]
    load_proj = [
        pltpu.make_async_copy(proj.at[:, pl.ds(i * tile, tile)], proj_tiles.at[i], sems.at[2 + i])
        for i in range(tiles)
    ]
    load_tails = [
        pltpu.make_async_copy(text.at[pl.ds(half, half), :], tails.at[0], sems.at[2 + tiles]),
        pltpu.make_async_copy(text_other.at[pl.ds(half, half), :], tails.at[1], sems.at[3 + tiles]),
    ]
    load_weights = [
        pltpu.make_async_copy(
            xz.at[:, pl.ds(i * 256, 128)],
            weights.at[i // 2, :, pl.ds(i % 2 * 128, 128)],
            sems.at[4 + tiles + i],
        )
        for i in range(4)
    ]
    load_weights.append(pltpu.make_async_copy(bc, weights.at[2], sems.at[8 + tiles]))
    for copy in load_feats + load_proj[:2] + load_tails + load_proj[2:] + load_weights:
        copy.start()
    gain_row = gain[...].reshape(1, -1)
    rank = lax.axis_index("dp")
    stays = table[0, 0, rank] == rank
    load_feats[0].wait()
    load_feats[1].wait()
    for index in range(2):
        block = jnp.where(stays, feats[index], feats[1 - index]).astype(F32)
        scale = lax.rsqrt(jnp.mean(block * block, -1, keepdims=True) + EPS)
        normed[index * half : (index + 1) * half, :] = (
            block * scale * vision_gain[...].reshape(1, -1).astype(F32)
        ).astype(BF16)
    ones = jnp.ones((8, 128), BF16)

    def folded(block):
        total = jnp.zeros((block.shape[0], 128), F32)
        for start in range(0, block.shape[1], 128):
            piece = block[:, start : start + 128].astype(F32)
            total = total + piece * piece
        return total

    squares = [None] * 4
    for i in range(tiles):
        load_proj[i].wait()
        cols = slice(i * tile, (i + 1) * tile)
        result = jnp.dot(normed[...], proj_tiles[i], preferred_element_type=F32).astype(BF16)
        crops[:, cols] = result
        scaled = result * gain_row[:, cols]
        rows[0:half, cols] = scaled[:half]
        rows[2 * half : 3 * half, cols] = scaled[half:]
        for index in range(2):
            more = folded(result[index * half : (index + 1) * half])
            squares[2 * index] = more if i == 0 else squares[2 * index] + more
        if i < 2:
            load_tails[i].wait()
            head = tails[i, 0:8, :].astype(F32)
            line = newline[...].reshape(1, -1).astype(F32)
            top = lax.broadcasted_iota(jnp.int32, (8, 1), 0) == 0
            tails[i, 0:8, :] = jnp.where(top, line, head).astype(BF16)
            main = tails[i]
            base = (2 * i + 1) * half
            rows[base : base + half, :] = main * gain_row
            squares[2 * i + 1] = folded(main)
    departures = [
        pltpu.make_async_copy(crops, crops_out, out_sems.at[0]),
        pltpu.make_async_copy(rows, rows_out, out_sems.at[1]),
    ]
    for copy in departures:
        copy.start()
    for copy in load_weights:
        copy.wait()
    chip = lax.axis_index("tensor")
    lane = lax.broadcasted_iota(jnp.int32, (1, 128), 1)
    own = [conv_x[...].astype(F32), out_gain[...].reshape(1, 128).astype(F32)]
    for value in (dt_bias[0], a_log[0], skip[0]):
        whole = jnp.full((1, 128), value, F32)
        high = whole.astype(BF16).astype(F32)
        middle = (whole - high).astype(BF16).astype(F32)
        low = whole - high - middle
        pieces = jnp.where(lane < 32, high, jnp.where(lane < 64, middle, low))
        own.append(jnp.where(lane < 96, pieces, 0.0))
    own = jnp.concatenate(own, 0)
    slots = jnp.concatenate([jnp.where(chip == slot, own, 0.0) for slot in range(4)], 1)

    def parted(source, keep, send, part, sem):
        goes = pltpu.make_async_copy(source.at[part], send.at[part // 2], sem)
        remains = pltpu.make_async_copy(source.at[part], keep.at[part // 2], sem)
        here = chip % 2 == part % 2
        pl.when(here)(remains.start)
        pl.when(jnp.logical_not(here))(goes.start)
        departures.append(goes)

    for part in range(4):
        main = rows[part * half : (part + 1) * half, :]
        maps[part] = jnp.dot(main, weights[2], preferred_element_type=F32).astype(BF16)
        parted(maps, keep_out, send_out, part, out_sems.at[6 + part])
    for part in range(4):
        main = rows[part * half : (part + 1) * half, :]
        for i in range(2):
            first[part, 0:half, i * 256 : i * 256 + 256] = jnp.dot(
                main, weights[i], preferred_element_type=F32
            ).astype(BF16)
        steps = contract(dt[...], main, ((1,), (1,)))
        sums = contract(ones, squares[part].astype(BF16), ((1,), (1,)))
        sums = jnp.concatenate([steps[0:4], sums[0:4]], 0)
        sums = jnp.concatenate([sums, jnp.zeros((8, 512 - half), F32)], 1)
        first[part, half : half + 16, :] = jnp.concatenate([sums, slots], 0).astype(BF16)
        parted(first, keep_x_out, send_x_out, part, out_sems.at[2 + part])
    for copy in departures:
        copy.wait()


def enter(
    table, dt_bias, a_log, skip, feats_mine, feats_other, vision_gain, proj, text, text_other,
    newline, gain, xz, bc, dt, conv_x, out_gain,
):
    half, vision = feats_mine.shape
    columns = text.shape[1]
    tiles = 4
    whole = pl.BlockSpec(memory_space=pl.ANY)
    near = pl.BlockSpec(memory_space=pltpu.VMEM)
    return pl.pallas_call(
        enter_body,
        in_specs=[pl.BlockSpec(memory_space=pltpu.SMEM)] * 4
        + [whole, whole, near, whole, whole, whole]
        + [near, near, whole, whole, near, near, near],
        out_specs=[whole] * 6,
        out_shape=[
            jax.ShapeDtypeStruct((2 * half, columns), BF16),
            jax.ShapeDtypeStruct((4 * half, columns), BF16),
            jax.ShapeDtypeStruct((2, half + 16, 512), BF16),
            jax.ShapeDtypeStruct((2, half + 16, 512), BF16),
            jax.ShapeDtypeStruct((2, half, 256), BF16),
            jax.ShapeDtypeStruct((2, half, 256), BF16),
        ],
        scratch_shapes=[
            pltpu.VMEM((2, half, vision), BF16),
            pltpu.VMEM((2 * half, vision), BF16),
            pltpu.VMEM((tiles, vision, columns // tiles), BF16),
            pltpu.VMEM((2, half, columns), BF16),
            pltpu.VMEM((3, columns, 256), BF16),
            pltpu.VMEM((2 * half, columns), BF16),
            pltpu.VMEM((4 * half, columns), BF16),
            pltpu.VMEM((4, half + 16, 512), BF16),
            pltpu.VMEM((4, half, 256), BF16),
            pltpu.SemaphoreType.DMA((9 + tiles,)),
            pltpu.SemaphoreType.DMA((10,)),
        ],
        name="enter",
    )(
        table, dt_bias, a_log, skip, feats_mine, feats_other, vision_gain, proj, text, text_other,
        newline, gain, xz, bc, dt, conv_x, out_gain,
    )


def gates_body(rows_hbm, xz, keep_out, send_out, rows, weights, results, sems, out_sems):
    half = results.shape[1]
    chip = lax.axis_index("tensor")
    load_weights = [
        pltpu.make_async_copy(
            xz.at[:, pl.ds(i * 256 + 128, 128)],
            weights.at[i // 2, :, pl.ds(i % 2 * 128, 128)],
            sems.at[4 + i],
        )
        for i in range(4)
    ]
    load_rows = [
        pltpu.make_async_copy(rows_hbm.at[pl.ds(part * half, half), :], rows.at[part], sems.at[part])
        for part in range(4)
    ]
    for copy in load_rows[:1] + load_weights + load_rows[1:]:
        copy.start()
    departures = []
    for part in range(4):
        load_rows[part].wait()
        for i in range(2):
            if part == 0:
                load_weights[2 * i].wait()
                load_weights[2 * i + 1].wait()
            results[part, :, 256 * i : 256 * i + 256] = jnp.dot(
                rows[part], weights[i], preferred_element_type=F32
            ).astype(BF16)
        goes = pltpu.make_async_copy(results.at[part], send_out.at[part // 2], out_sems.at[part])
        remains = pltpu.make_async_copy(results.at[part], keep_out.at[part // 2], out_sems.at[part])
        here = chip % 2 == part % 2
        pl.when(here)(remains.start)
        pl.when(jnp.logical_not(here))(goes.start)
        departures.append(goes)
    for copy in departures:
        copy.wait()


def gates(rows, xz):
    half, columns = rows.shape[0] // 4, rows.shape[1]
    whole = pl.BlockSpec(memory_space=pl.ANY)
    return pl.pallas_call(
        gates_body,
        in_specs=[whole, whole],
        out_specs=[whole, whole],
        out_shape=[jax.ShapeDtypeStruct((2, half, 512), BF16)] * 2,
        scratch_shapes=[
            pltpu.VMEM((4, half, columns), BF16),
            pltpu.VMEM((2, columns, 256), BF16),
            pltpu.VMEM((4, half, 512), BF16),
            pltpu.SemaphoreType.DMA((8,)),
            pltpu.SemaphoreType.DMA((4,)),
        ],
        name="gates",
    )(rows, xz)


def filtered(main, edge, taps):
    rows = main.shape[0]
    padded = jnp.concatenate([edge, main], 0)
    count = taps.shape[0]
    total = taps[count - 1 : count] * main
    for back in range(1, count):
        total = total + taps[count - 1 - back : count - back] * padded[8 - back : 8 - back + rows]
    return total


def scan_body(
    width, kept_x, received_x, kept, received, before, taps_maps, streams, maps, meta, cols, state, params
):
    first = kept_x[...].astype(F32) + received_x[...].astype(F32)
    half = first.shape[0] - 16
    slots = first[half + 8 : half + 16]
    params[...] = slots
    sums = first[half : half + 8, 0:half]
    scale = lax.rsqrt(sums[4:5] / width + EPS)
    sums_before = before[8:16, half - 128 : half].astype(F32)
    scale_before = lax.rsqrt(sums_before[4:5] / width + EPS)
    head = lax.broadcasted_iota(jnp.int32, (8, 512), 1) // 128
    owner = (head == lax.broadcasted_iota(jnp.int32, (8, 512), 0)).astype(F32)
    scalars = slots[5:8]
    bias = jnp.sum(owner * scalars[0:1], 1, keepdims=True) * (1.0 / 32)
    rate = jnp.sum(owner * scalars[1:2], 1, keepdims=True) * (1.0 / 32)
    raw = sums * scale + bias
    step = jnp.maximum(raw, 0.0) + jnp.log1p(jnp.exp(-jnp.abs(raw)))
    decays = -jnp.exp(rate) * step
    upper = (
        lax.broadcasted_iota(jnp.int32, (half, half), 0)
        <= lax.broadcasted_iota(jnp.int32, (half, half), 1)
    ).astype(F32)
    cumulative = contract(decays, upper, ((1,), (0,)), HIGHEST)
    final = cumulative[:, half - 1 : half]
    carry = jnp.exp(final - cumulative) * step
    wide = jnp.concatenate([scale_before, jnp.zeros((1, half - 128), F32)], 1)
    columns = columns_of(
        jnp.concatenate(
            [cumulative, carry] + [jnp.broadcast_to(row, (8, half)) for row in (scale, wide)], 0
        )
    )
    cols[...] = columns
    scale_main = columns[:, 16:17]
    scale_edge = columns[120:128, 24:25]
    taps_x = slots[0:4]
    edge = before[0:8, :].astype(F32) * scale_edge
    x = silu(filtered(first[0:half] * scale_main, edge[:, 0:512], taps_x))
    both = silu(
        filtered(
            (kept[...].astype(F32) + received[...].astype(F32)) * scale_main,
            edge[:, 512:768],
            taps_maps[...].astype(F32),
        )
    ).astype(BF16)
    carried = jnp.concatenate(
        [jnp.broadcast_to(columns[:, 8 + h : 9 + h], (half, 128)) for h in range(4)], 1
    )
    state[0:128, :] = contract(both[:, 0:128], (x * carried).astype(BF16), ((0,), (0,))).astype(BF16)
    total = jnp.sum(jnp.exp(final) * owner, 0, keepdims=True)
    state[128:144, :] = jnp.broadcast_to(total, (16, 512)).astype(BF16)
    streams[...] = x.astype(BF16)
    maps[...] = both
    meta[0:8, :] = cumulative
    meta[8:16, :] = step


def scan(width, *operands):
    half = operands[2].shape[0]
    return pl.pallas_call(
        lambda *refs: scan_body(width, *refs),
        out_shape=[
            jax.ShapeDtypeStruct((half, 512), BF16),
            jax.ShapeDtypeStruct((half, 256), BF16),
            jax.ShapeDtypeStruct((16, half), F32),
            jax.ShapeDtypeStruct((half, 32), F32),
            jax.ShapeDtypeStruct((144, 512), BF16),
            jax.ShapeDtypeStruct((8, 512), F32),
        ],
        name="scan",
    )(*operands)


def join(state, partner):
    late = lax.axis_index("tensor") % 2 == 1
    first = jnp.where(late, partner, state).astype(F32)
    second = jnp.where(late, state, partner).astype(F32)
    decay = lax.broadcasted_iota(jnp.int32, state.shape, 0) >= 128
    return jnp.where(decay, first * second, second[128:129] * first + second).astype(BF16)


def inside_body(streams, maps, meta, cols, params, out):
    half = streams.shape[0]
    cumulative = meta[0:8, :]
    step = meta[8:16, :]
    cum_cols = cols[:, 0:8]
    scores = contract(maps[:, 128:256], maps[:, 0:128], ((1,), (1,)))
    lower = lax.broadcasted_iota(jnp.int32, (half, half), 0) >= lax.broadcasted_iota(
        jnp.int32, (half, half), 1
    )
    scores = jnp.where(lower, scores, 0.0)
    for head in range(4):
        lanes = slice(128 * head, 128 * head + 128)
        x = streams[:, lanes]
        gaps = cum_cols[:, head : head + 1] - cumulative[head : head + 1]
        weights = jnp.exp(jnp.where(lower, gaps, 0.0)) * scores * step[head : head + 1]
        y = jnp.dot(weights.astype(BF16), x, preferred_element_type=F32)
        through = jnp.sum(params[7:8, lanes], 1, keepdims=True) * (1.0 / 32)
        out[:, lanes] = y + through * x.astype(F32)


def inside(streams, maps, meta, cols, params):
    return pl.pallas_call(
        inside_body,
        out_shape=jax.ShapeDtypeStruct(streams.shape, F32),
        name="inside",
    )(streams, maps, meta, cols, params)


def gate_body(kept, received, local, maps, cols, params, partner, *others_and_out):
    *others, out = others_and_out
    half = local.shape[0]
    section = lax.axis_index("segment")
    late = lax.axis_index("tensor") % 2 == 1
    prior = jnp.zeros((128, 512), F32)
    for source in range(len(others)):
        bits = jnp.bitwise_xor(section, source)
        piece = others[0][...]
        for index in range(1, len(others)):
            piece = jnp.where(bits == index + 1, others[index][...], piece)
        piece = piece.astype(F32)
        prior = jnp.where(source < section, piece[128:129] * prior + piece[0:128], prior)
    before = partner[...].astype(F32)
    prior = jnp.where(late, before[128:129] * prior + before[0:128], prior)
    scale = cols[:, 16:17]
    entry = jnp.exp(cols[:, 0:8])
    across = jnp.dot(maps[:, 128:256], prior.astype(BF16), preferred_element_type=F32)
    gated = []
    squares = jnp.zeros((half, 1), F32)
    for head in range(4):
        lanes = slice(128 * head, 128 * head + 128)
        y = local[:, lanes] + entry[:, head : head + 1] * across[:, lanes]
        gates = kept[:, lanes].astype(F32) + received[:, lanes].astype(F32)
        value = y * silu(gates * scale)
        squares = squares + jnp.sum(value * value, -1, keepdims=True)
        gated.append(value)
    norm = lax.rsqrt(squares / 512 + EPS)
    for head in range(4):
        lanes = slice(128 * head, 128 * head + 128)
        out[:, lanes] = (gated[head] * norm * params[4:5, lanes]).astype(BF16)


def gate(local, *operands):
    return pl.pallas_call(
        gate_body, out_shape=jax.ShapeDtypeStruct(local.shape, BF16), name="gate"
    )(*operands[:2], local, *operands[2:])


def per_device_halves(
    text_embed, crop_feats, crop_dest, vision_gain, proj_weight, newline, norm_gain, xz_weight,
    dt_weight, bc_weight, conv_x, conv_bc, dt_bias, a_log, skip, out_gain, out_weight,
):
    my_chip = lax.axis_index("tensor")
    segment_count = lax.axis_size("segment")
    text = text_embed[0]
    section, columns = text.shape
    half = section // 2
    width = columns * lax.axis_size("tensor")
    feats = crop_feats[0, 0, 0]
    feats_other = swapped(feats, "dp", 1)
    text_other = swapped(text, "dp", 1)
    crops, rows, keep_x, send_x, keep, send = enter(
        crop_dest.transpose(0, 2, 1), dt_bias, a_log, skip, feats, feats_other, vision_gain,
        proj_weight, text, text_other, newline, norm_gain, xz_weight, bc_weight, dt_weight.T,
        conv_x, out_gain,
    )
    out_weight, newline, rows = lax.optimization_barrier((out_weight, newline, rows))
    lower = my_chip < 2

    def added(keep, arrived):
        pair = keep.astype(F32) + arrived.astype(F32)
        leaves = jnp.where(lower, pair[1], pair[0]).astype(BF16)
        return leaves, jnp.where(lower, pair[0], pair[1]).astype(BF16)

    keep_gates, send_gates = gates(rows, xz_weight)
    leaves, kept = added(keep, swapped(send, "tensor", 1))
    leaves, kept, send_x, send_gates, out_weight = lax.optimization_barrier(
        (leaves, kept, send_x, send_gates, out_weight)
    )
    received = swapped(leaves, "tensor", 2)
    leaves_x, kept_x = added(keep_x, swapped(send_x, "tensor", 1))
    leaves_x, kept_x, send_gates, received = lax.optimization_barrier(
        (leaves_x, kept_x, send_gates, received)
    )
    received_x = swapped(leaves_x, "tensor", 2)
    arrived_gates = swapped(send_gates, "tensor", 1)
    weight_other = swapped(out_weight, "dp", 1)
    weights = (
        jnp.where(lower, out_weight, weight_other), jnp.where(lower, weight_other, out_weight)
    )
    late = my_chip % 2 == 1
    head = crops[:half]
    tail = jnp.where(jnp.arange(half)[:, None] == 0, newline[None], text[half:])
    hidden = (jnp.where(late, tail, head), jnp.where(late, head, tail))
    kept_x, received_x, weights, hidden = lax.optimization_barrier(
        (kept_x, received_x, weights, hidden)
    )
    route = [(i, i + 1) for i in range(0, 4 * segment_count, 2)]
    route += [(i, i + 3) for i in range(1, 4 * segment_count - 4, 2)]
    ends = (kept[half - 8 :].astype(F32) + received[half - 8 :].astype(F32)).astype(BF16)
    before = slice(half - 8, half + 8)
    before = (kept_x[before].astype(F32) + received_x[before].astype(F32)).astype(BF16)
    before = jnp.concatenate([before, jnp.pad(ends, ((0, 8), (0, 0)))], 1)
    before = lax.ppermute(before, ("segment", "tensor"), route)
    streams, maps, meta, as_columns, state, params = scan(
        width, kept_x, received_x, kept, received, before, conv_bc
    )
    meta, keep_gates = lax.optimization_barrier((meta, keep_gates))
    local = inside(streams, maps, meta, as_columns, params)
    partner = swapped(state, "tensor", 1)
    whole = join(state, partner)
    whole, local = lax.optimization_barrier((whole, local))
    others = [swapped(whole, "segment", bits) for bits in range(1, segment_count)]
    leaves, kept = added(keep_gates, arrived_gates)
    received = swapped(leaves, "tensor", 2)
    normed = gate(local, kept, received, maps, as_columns, params, partner, *others)
    near, far, here = (
        lax.ppermute(
            normed, ("dp", "tensor"), [(i, (i if i % 4 < 2 else i ^ 4) ^ bits) for i in range(8)]
        )
        for bits in (1, 2, 0)
    )
    both = swapped(far, "tensor", 1)
    out = jnp.zeros((section, columns), BF16)
    for index, pair in enumerate(((here, far), (near, both))):
        mixed = jnp.dot(pair[0], weights[0], preferred_element_type=F32)
        mixed = mixed + jnp.dot(pair[1], weights[1], preferred_element_type=F32)
        block = (hidden[index].astype(F32) + mixed).astype(BF16)
        start = jnp.where(late, half, 0) if index == 0 else jnp.where(late, 0, half)
        out = lax.dynamic_update_slice(out, block, (start, 0))
    return out[None]


def per_device(*args):
    text_embed, crop_feats = args[0], args[1]
    sizes = tuple(lax.axis_size(axis) for axis in ("segment", "dp", "tensor"))
    heads_dev = args[12].shape[0]
    head_width = args[15].shape[0] // heads_dev
    state_size = args[9].shape[1] // 2
    fits = (
        sizes == (4, 2, 4)
        and heads_dev == 1
        and (head_width, state_size) == (128, 128)
        and crop_feats.shape[2:4] == (1, 256)
        and text_embed.shape[1] == 512
    )
    return (per_device_halves if fits else per_device_any)(*args)


def solution(mesh):
    return jax.shard_map(
        per_device,
        mesh=mesh,
        in_specs=(
            P("dp", "segment", "tensor"),
            P("segment", "dp", None, None, None),
            P("segment", None, None),
            P(),
            P(None, "tensor"),
            P("tensor"),
            P("tensor"),
            P("tensor", "dp"),
            P("tensor", "dp"),
            P("tensor", "dp"),
            P(None, ("dp", "tensor")),
            P(None, "dp"),
            P(("dp", "tensor")),
            P(("dp", "tensor")),
            P(("dp", "tensor")),
            P(("dp", "tensor")),
            P("dp", "tensor"),
        ),
        out_specs=P("dp", "segment", "tensor"),
        check_vma=False,
    )
```

```python
import jax
import jax.numpy as jnp
from jax import lax
from jax.experimental import pallas as pl
from jax.experimental.pallas import tpu as pltpu
from jax.sharding import PartitionSpec as P

EPS = 1e-05
F32 = jnp.float32
BF16 = jnp.bfloat16
HIGHEST = lax.Precision.HIGHEST


def passed_along(block, axis, distance):
    devices = range(lax.axis_size(axis))
    route = [(i - distance, i) for i in devices if i - distance in devices]
    return lax.ppermute(block, axis, route)


def swapped(block, axis, bits):
    return lax.ppermute(block, axis, [(i, i ^ bits) for i in range(lax.axis_size(axis))])


def per_device_any(
    text_embed,
    crop_feats,
    crop_dest,
    vision_gain,
    proj_weight,
    newline,
    norm_gain,
    xz_weight,
    dt_weight,
    bc_weight,
    conv_x,
    conv_bc,
    dt_bias,
    a_log,
    skip,
    out_gain,
    out_weight,
):
    highest = lax.Precision.HIGHEST
    eps = 1e-05
    dp_count = lax.axis_size("dp")
    tp_count = lax.axis_size("tensor")
    segment_count = lax.axis_size("segment")
    my_rank = lax.axis_index("dp")
    section = text_embed.shape[1]
    columns = text_embed.shape[2]
    crop_count = crop_feats.shape[2]
    crop_rows = crop_feats.shape[3]
    crop_span = crop_rows + 1
    heads_dev = dt_bias.shape[0]
    head_width = out_gain.shape[0] // heads_dev
    state_size = bc_weight.shape[1] // 2
    feats = crop_feats[0, 0].astype(jnp.float32)
    vision = (
        feats
        * lax.rsqrt(jnp.mean(feats * feats, -1, keepdims=True) + eps)
        * vision_gain.astype(jnp.float32)
    ).astype(jnp.bfloat16)
    encoded = jnp.dot(
        vision.reshape(crop_count * crop_rows, -1), proj_weight, preferred_element_type=jnp.float32
    )
    encoded = encoded.astype(jnp.bfloat16).reshape(crop_count, crop_rows, columns)
    table = crop_dest[0]
    sources = jnp.arange(dp_count, dtype=jnp.int32)
    mine = jnp.sum(jnp.where(sources[:, None] == my_rank, table, 0), axis=0)
    chosen = mine[None, :] == sources[:, None]
    outgoing = jnp.einsum(
        "dc,crq->drq", chosen.astype(jnp.bfloat16), encoded, preferred_element_type=jnp.float32
    ).astype(jnp.bfloat16)
    incoming = lax.all_to_all(outgoing, "dp", split_axis=0, concat_axis=0, tiled=True)
    sent_rows = incoming.shape[1]
    valid = jnp.any(table == my_rank, axis=1).astype(jnp.int32)
    order = jnp.cumsum(valid) - valid
    counted = jnp.sum(valid)
    positions = jnp.arange(section, dtype=jnp.int32)
    block = positions // crop_span
    within = positions % crop_span
    slot_ids = jnp.arange(section // crop_span + 1, dtype=jnp.int32)
    matched = (valid[None, :] == 1) & (order[None, :] == slot_ids[:, None])
    slot_source = jnp.sum(jnp.where(matched, sources[None, :], 0), axis=1)
    row_source = jnp.sum(
        jnp.where(block[:, None] == slot_ids[None, :], slot_source[None, :], 0), axis=1
    )
    row_index = row_source * sent_rows + jnp.minimum(within, sent_rows - 1)
    picked = jnp.take(incoming.reshape(dp_count * sent_rows, columns), row_index, axis=0)
    image = block < counted
    text = text_embed[0]
    crop_pos = image & (within < crop_rows)
    line_pos = image & (within == crop_rows)
    hidden = jnp.where(
        crop_pos[:, None], picked, jnp.where(line_pos[:, None], newline[None, :], text)
    )
    wide = hidden.astype(jnp.float32)
    row_total = lax.psum(jnp.sum(wide * wide, -1), "tensor")
    normed = (
        wide
        * lax.rsqrt(row_total / (columns * tp_count) + eps)[:, None]
        * norm_gain.astype(jnp.float32)
    ).astype(jnp.bfloat16)
    pair_cols = xz_weight.shape[1]
    step_cols = dt_weight.shape[1]
    piece = lax.all_gather(normed, "dp", axis=0, tiled=True)
    terms = jnp.concatenate(
        [
            jnp.dot(piece, xz_weight, preferred_element_type=jnp.float32),
            jnp.dot(piece, dt_weight, preferred_element_type=jnp.float32),
            jnp.dot(piece, bc_weight, preferred_element_type=jnp.float32),
        ],
        axis=1,
    )
    pair_mine, step_mine = (
        lax.psum_scatter(
            terms[:, :pair_cols].astype(jnp.bfloat16), "tensor", scatter_dimension=1, tiled=True
        ).astype(jnp.float32),
        lax.psum_scatter(
            terms[:, pair_cols : pair_cols + step_cols].astype(jnp.bfloat16),
            "tensor",
            scatter_dimension=1,
            tiled=True,
        ).astype(jnp.float32),
    )
    map_terms = terms[:, pair_cols + step_cols :]
    maps_all = lax.psum(map_terms.astype(jnp.bfloat16), "tensor").astype(jnp.float32)
    pairs = pair_mine.reshape(dp_count, section, heads_dev, 2, head_width)
    values = pairs[:, :, :, 0, :].reshape(dp_count, section, heads_dev * head_width)
    gates = pairs[:, :, :, 1, :]
    fresh = jnp.concatenate([values, maps_all.reshape(dp_count, section, 2 * state_size)], axis=2)
    kernel = jnp.concatenate([conv_x, conv_bc], axis=1).astype(jnp.float32)
    taps = kernel.shape[0]
    edge = passed_along(fresh[:, section - (taps - 1) :, :], "segment", 1)
    padded = jnp.concatenate([edge, fresh], axis=1)
    filtered = kernel[0] * padded[:, 0:section]
    for offset in range(1, taps):
        filtered = filtered + kernel[offset] * padded[:, offset : offset + section]
    activated = jax.nn.silu(filtered)
    inner_cols = heads_dev * head_width
    streams = activated[..., :inner_cols].reshape(dp_count, section, heads_dev, head_width)
    b_rows = activated[..., inner_cols : inner_cols + state_size]
    c_rows = activated[..., inner_cols + state_size :]
    step = jax.nn.softplus(step_mine.reshape(dp_count, section, heads_dev) + dt_bias)
    cumulative = jnp.cumsum(-jnp.exp(a_log) * step, axis=1)
    scores = jnp.einsum("nls,nms->nlm", c_rows, b_rows, precision=highest)
    mask = (positions[:, None] >= positions[None, :])[None, :, :, None]
    gaps = cumulative[:, :, None, :] - cumulative[:, None, :, :]
    weights = (
        jnp.where(mask, jnp.exp(jnp.where(mask, gaps, 0.0)), 0.0)
        * scores[..., None]
        * step[:, None, :, :]
    )
    inside = jnp.einsum("nlmh,nmhp->nlhp", weights, streams, precision=highest)
    final = cumulative[:, -1, :]
    carry_weight = jnp.exp(final[:, None, :] - cumulative) * step
    local_state = jnp.einsum("nlh,nls,nlhp->nhsp", carry_weight, b_rows, streams, precision=highest)
    decay = jnp.exp(final)
    prior = jnp.zeros_like(local_state)
    for turn in range(segment_count - 1):
        prior = passed_along(
            (decay[:, :, None, None] * prior + local_state).astype(jnp.bfloat16), "segment", 1
        ).astype(jnp.float32)
    across = jnp.exp(cumulative)[..., None] * jnp.einsum(
        "nls,nhsp->nlhp", c_rows, prior, precision=highest
    )
    outputs = inside + across + skip[None, None, :, None] * streams
    gated = outputs * jax.nn.silu(gates)
    group_total = lax.psum(jnp.sum(gated * gated, axis=(2, 3)), "tensor")
    scale = lax.rsqrt(group_total / (inner_cols * tp_count) + eps)
    normed_out = (
        gated * scale[..., None, None] * out_gain.astype(jnp.float32).reshape(heads_dev, head_width)
    ).astype(jnp.bfloat16)
    normed_out = normed_out.reshape(dp_count * section, inner_cols)
    term = jnp.dot(
        lax.all_gather(normed_out, "tensor", axis=1, tiled=True),
        out_weight,
        preferred_element_type=jnp.float32,
    )
    mixed = lax.psum_scatter(
        term.astype(jnp.bfloat16), "dp", scatter_dimension=0, tiled=True
    ).astype(jnp.float32)
    return (wide + mixed).astype(jnp.bfloat16)[None]


def contract(a, b, dims, precision=None):
    return lax.dot_general(
        a, b, (dims, ((), ())), precision=precision, preferred_element_type=F32
    )


def eye(n):
    return (
        lax.broadcasted_iota(jnp.int32, (n, n), 0) == lax.broadcasted_iota(jnp.int32, (n, n), 1)
    ).astype(F32)


def columns_of(rows):
    return contract(eye(rows.shape[1]), rows, ((1,), (1,)), HIGHEST)


def silu(a):
    return a / (1.0 + jnp.exp(-a))


def enter_body(
    table, dt_bias, a_log, skip, feats_mine, feats_other, vision_gain, proj, text, text_other,
    newline, gain, xz, bc, dt, conv_x, out_gain,
    crops_out, rows_out, keep_x_out, send_x_out, keep_out, send_out,
    feats, normed, proj_tiles, tails, weights, crops, rows, first, maps, sems, out_sems,
):
    half = tails.shape[1]
    tiles, _, tile = proj_tiles.shape
    columns = rows.shape[1]
    load_feats = [
        pltpu.make_async_copy(feats_mine, feats.at[0], sems.at[0]),
        pltpu.make_async_copy(feats_other, feats.at[1], sems.at[1]),
    ]
    load_proj = [
        pltpu.make_async_copy(proj.at[:, pl.ds(i * tile, tile)], proj_tiles.at[i], sems.at[2 + i])
        for i in range(tiles)
    ]
    load_tails = [
        pltpu.make_async_copy(text.at[pl.ds(half, half), :], tails.at[0], sems.at[2 + tiles]),
        pltpu.make_async_copy(text_other, tails.at[1], sems.at[3 + tiles]),
    ]
    load_weights = [
        pltpu.make_async_copy(
            xz.at[:, pl.ds(i * 256, 128)],
            weights.at[i // 2, :, pl.ds(i % 2 * 128, 128)],
            sems.at[4 + tiles + i],
        )
        for i in range(4)
    ]
    load_weights.append(pltpu.make_async_copy(bc, weights.at[2], sems.at[8 + tiles]))
    for copy in load_feats + load_proj[:2] + load_tails + load_proj[2:] + load_weights:
        copy.start()
    gain_row = gain[...].reshape(1, -1)
    rank = lax.axis_index("dp")
    stays = table[0, 0, rank] == rank
    load_feats[0].wait()
    load_feats[1].wait()
    for index in range(2):
        block = jnp.where(stays, feats[index], feats[1 - index]).astype(F32)
        scale = lax.rsqrt(jnp.mean(block * block, -1, keepdims=True) + EPS)
        normed[index * half : (index + 1) * half, :] = (
            block * scale * vision_gain[...].reshape(1, -1).astype(F32)
        ).astype(BF16)
    ones = jnp.ones((8, 128), BF16)

    def folded(block):
        total = jnp.zeros((block.shape[0], 128), F32)
        for start in range(0, block.shape[1], 128):
            piece = block[:, start : start + 128].astype(F32)
            total = total + piece * piece
        return total

    squares = [None] * 4
    for i in range(tiles):
        load_proj[i].wait()
        cols = slice(i * tile, (i + 1) * tile)
        result = jnp.dot(normed[...], proj_tiles[i], preferred_element_type=F32).astype(BF16)
        crops[:, cols] = result
        scaled = result * gain_row[:, cols]
        rows[0:half, cols] = scaled[:half]
        rows[2 * half : 3 * half, cols] = scaled[half:]
        for index in range(2):
            more = folded(result[index * half : (index + 1) * half])
            squares[2 * index] = more if i == 0 else squares[2 * index] + more
        if i < 2:
            load_tails[i].wait()
            head = tails[i, 0:8, :].astype(F32)
            line = newline[...].reshape(1, -1).astype(F32)
            top = lax.broadcasted_iota(jnp.int32, (8, 1), 0) == 0
            tails[i, 0:8, :] = jnp.where(top, line, head).astype(BF16)
            main = tails[i]
            base = (2 * i + 1) * half
            rows[base : base + half, :] = main * gain_row
            squares[2 * i + 1] = folded(main)
    departures = [
        pltpu.make_async_copy(crops, crops_out, out_sems.at[0]),
        pltpu.make_async_copy(rows, rows_out, out_sems.at[1]),
    ]
    for copy in departures:
        copy.start()
    for copy in load_weights:
        copy.wait()
    chip = lax.axis_index("tensor")
    lane = lax.broadcasted_iota(jnp.int32, (1, 128), 1)
    own = [conv_x[...].astype(F32), out_gain[...].reshape(1, 128).astype(F32)]
    for value in (dt_bias[0], a_log[0], skip[0]):
        whole = jnp.full((1, 128), value, F32)
        high = whole.astype(BF16).astype(F32)
        middle = (whole - high).astype(BF16).astype(F32)
        low = whole - high - middle
        pieces = jnp.where(lane < 32, high, jnp.where(lane < 64, middle, low))
        own.append(jnp.where(lane < 96, pieces, 0.0))
    own = jnp.concatenate(own, 0)
    slots = jnp.concatenate([jnp.where(chip == slot, own, 0.0) for slot in range(4)], 1)

    def parted(source, keep, send, part, sem):
        goes = pltpu.make_async_copy(source.at[part], send.at[part // 2], sem)
        remains = pltpu.make_async_copy(source.at[part], keep.at[part // 2], sem)
        here = chip % 2 == part % 2
        pl.when(here)(remains.start)
        pl.when(jnp.logical_not(here))(goes.start)
        departures.append(goes)

    for part in range(4):
        main = rows[part * half : (part + 1) * half, :]
        maps[part] = jnp.dot(main, weights[2], preferred_element_type=F32).astype(BF16)
        parted(maps, keep_out, send_out, part, out_sems.at[6 + part])
    for part in range(4):
        main = rows[part * half : (part + 1) * half, :]
        for i in range(2):
            first[part, 0:half, i * 256 : i * 256 + 256] = jnp.dot(
                main, weights[i], preferred_element_type=F32
            ).astype(BF16)
        steps = contract(dt[...], main, ((1,), (1,)))
        sums = contract(ones, squares[part].astype(BF16), ((1,), (1,)))
        sums = jnp.concatenate([steps[0:4], sums[0:4]], 0)
        sums = jnp.concatenate([sums, jnp.zeros((8, 512 - half), F32)], 1)
        first[part, half : half + 16, :] = jnp.concatenate([sums, slots], 0).astype(BF16)
        parted(first, keep_x_out, send_x_out, part, out_sems.at[2 + part])
    for copy in departures:
        copy.wait()


def enter(
    table, dt_bias, a_log, skip, feats_mine, feats_other, vision_gain, proj, text, text_other,
    newline, gain, xz, bc, dt, conv_x, out_gain,
):
    half, vision = feats_mine.shape
    columns = text.shape[1]
    tiles = 4
    whole = pl.BlockSpec(memory_space=pl.ANY)
    near = pl.BlockSpec(memory_space=pltpu.VMEM)
    return pl.pallas_call(
        enter_body,
        in_specs=[pl.BlockSpec(memory_space=pltpu.SMEM)] * 4
        + [whole, whole, near, whole, whole, whole]
        + [near, near, whole, whole, near, near, near],
        out_specs=[whole] * 6,
        out_shape=[
            jax.ShapeDtypeStruct((2 * half, columns), BF16),
            jax.ShapeDtypeStruct((4 * half, columns), BF16),
            jax.ShapeDtypeStruct((2, half + 16, 512), BF16),
            jax.ShapeDtypeStruct((2, half + 16, 512), BF16),
            jax.ShapeDtypeStruct((2, half, 256), BF16),
            jax.ShapeDtypeStruct((2, half, 256), BF16),
        ],
        scratch_shapes=[
            pltpu.VMEM((2, half, vision), BF16),
            pltpu.VMEM((2 * half, vision), BF16),
            pltpu.VMEM((tiles, vision, columns // tiles), BF16),
            pltpu.VMEM((2, half, columns), BF16),
            pltpu.VMEM((3, columns, 256), BF16),
            pltpu.VMEM((2 * half, columns), BF16),
            pltpu.VMEM((4 * half, columns), BF16),
            pltpu.VMEM((4, half + 16, 512), BF16),
            pltpu.VMEM((4, half, 256), BF16),
            pltpu.SemaphoreType.DMA((9 + tiles,)),
            pltpu.SemaphoreType.DMA((10,)),
        ],
        name="enter",
    )(
        table, dt_bias, a_log, skip, feats_mine, feats_other, vision_gain, proj, text, text_other,
        newline, gain, xz, bc, dt, conv_x, out_gain,
    )


def gates_body(rows_hbm, xz, keep_out, send_out, rows, weights, results, sems, out_sems):
    half = results.shape[1]
    chip = lax.axis_index("tensor")
    load_weights = [
        pltpu.make_async_copy(
            xz.at[:, pl.ds(i * 256 + 128, 128)],
            weights.at[i // 2, :, pl.ds(i % 2 * 128, 128)],
            sems.at[4 + i],
        )
        for i in range(4)
    ]
    load_rows = [
        pltpu.make_async_copy(rows_hbm.at[pl.ds(part * half, half), :], rows.at[part], sems.at[part])
        for part in range(4)
    ]
    for copy in load_rows[:1] + load_weights + load_rows[1:]:
        copy.start()
    departures = []
    for part in range(4):
        load_rows[part].wait()
        for i in range(2):
            if part == 0:
                load_weights[2 * i].wait()
                load_weights[2 * i + 1].wait()
            results[part, :, 256 * i : 256 * i + 256] = jnp.dot(
                rows[part], weights[i], preferred_element_type=F32
            ).astype(BF16)
        goes = pltpu.make_async_copy(results.at[part], send_out.at[part // 2], out_sems.at[part])
        remains = pltpu.make_async_copy(results.at[part], keep_out.at[part // 2], out_sems.at[part])
        here = chip % 2 == part % 2
        pl.when(here)(remains.start)
        pl.when(jnp.logical_not(here))(goes.start)
        departures.append(goes)
    for copy in departures:
        copy.wait()


def gates(rows, xz):
    half, columns = rows.shape[0] // 4, rows.shape[1]
    whole = pl.BlockSpec(memory_space=pl.ANY)
    return pl.pallas_call(
        gates_body,
        in_specs=[whole, whole],
        out_specs=[whole, whole],
        out_shape=[jax.ShapeDtypeStruct((2, half, 512), BF16)] * 2,
        scratch_shapes=[
            pltpu.VMEM((4, half, columns), BF16),
            pltpu.VMEM((2, columns, 256), BF16),
            pltpu.VMEM((4, half, 512), BF16),
            pltpu.SemaphoreType.DMA((8,)),
            pltpu.SemaphoreType.DMA((4,)),
        ],
        name="gates",
    )(rows, xz)


def filtered(main, edge, taps):
    rows = main.shape[0]
    padded = jnp.concatenate([edge, main], 0)
    count = taps.shape[0]
    total = taps[count - 1 : count] * main
    for back in range(1, count):
        total = total + taps[count - 1 - back : count - back] * padded[8 - back : 8 - back + rows]
    return total


def scan_body(
    width, kept_x, received_x, kept, received, before, taps_maps, streams, maps, meta, cols, state, params
):
    first = kept_x[...].astype(F32) + received_x[...].astype(F32)
    half = first.shape[0] - 16
    slots = first[half + 8 : half + 16]
    params[...] = slots
    sums = first[half : half + 8, 0:half]
    scale = lax.rsqrt(sums[4:5] / width + EPS)
    sums_before = before[8:16, half - 128 : half].astype(F32)
    scale_before = lax.rsqrt(sums_before[4:5] / width + EPS)
    head = lax.broadcasted_iota(jnp.int32, (8, 512), 1) // 128
    owner = (head == lax.broadcasted_iota(jnp.int32, (8, 512), 0)).astype(F32)
    scalars = slots[5:8]
    bias = jnp.sum(owner * scalars[0:1], 1, keepdims=True) * (1.0 / 32)
    rate = jnp.sum(owner * scalars[1:2], 1, keepdims=True) * (1.0 / 32)
    raw = sums * scale + bias
    step = jnp.maximum(raw, 0.0) + jnp.log1p(jnp.exp(-jnp.abs(raw)))
    decays = -jnp.exp(rate) * step
    upper = (
        lax.broadcasted_iota(jnp.int32, (half, half), 0)
        <= lax.broadcasted_iota(jnp.int32, (half, half), 1)
    ).astype(F32)
    cumulative = contract(decays, upper, ((1,), (0,)), HIGHEST)
    final = cumulative[:, half - 1 : half]
    carry = jnp.exp(final - cumulative) * step
    wide = jnp.concatenate([scale_before, jnp.zeros((1, half - 128), F32)], 1)
    columns = columns_of(
        jnp.concatenate(
            [cumulative, carry] + [jnp.broadcast_to(row, (8, half)) for row in (scale, wide)], 0
        )
    )
    cols[...] = columns
    scale_main = columns[:, 16:17]
    scale_edge = columns[120:128, 24:25]
    taps_x = slots[0:4]
    edge = before[0:8, :].astype(F32) * scale_edge
    x = silu(filtered(first[0:half] * scale_main, edge[:, 0:512], taps_x))
    both = silu(
        filtered(
            (kept[...].astype(F32) + received[...].astype(F32)) * scale_main,
            edge[:, 512:768],
            taps_maps[...].astype(F32),
        )
    ).astype(BF16)
    carried = jnp.concatenate(
        [jnp.broadcast_to(columns[:, 8 + h : 9 + h], (half, 128)) for h in range(4)], 1
    )
    state[0:128, :] = contract(both[:, 0:128], (x * carried).astype(BF16), ((0,), (0,))).astype(BF16)
    total = jnp.sum(jnp.exp(final) * owner, 0, keepdims=True)
    state[128:144, :] = jnp.broadcast_to(total, (16, 512)).astype(BF16)
    streams[...] = x.astype(BF16)
    maps[...] = both
    meta[0:8, :] = cumulative
    meta[8:16, :] = step


def scan(width, *operands):
    half = operands[2].shape[0]
    return pl.pallas_call(
        lambda *refs: scan_body(width, *refs),
        out_shape=[
            jax.ShapeDtypeStruct((half, 512), BF16),
            jax.ShapeDtypeStruct((half, 256), BF16),
            jax.ShapeDtypeStruct((16, half), F32),
            jax.ShapeDtypeStruct((half, 32), F32),
            jax.ShapeDtypeStruct((144, 512), BF16),
            jax.ShapeDtypeStruct((8, 512), F32),
        ],
        name="scan",
    )(*operands)


def join(state, partner):
    late = lax.axis_index("tensor") % 2 == 1
    first = jnp.where(late, partner, state).astype(F32)
    second = jnp.where(late, state, partner).astype(F32)
    decay = lax.broadcasted_iota(jnp.int32, state.shape, 0) >= 128
    return jnp.where(decay, first * second, second[128:129] * first + second).astype(BF16)


def inside_body(streams, maps, meta, cols, params, out):
    half = streams.shape[0]
    cumulative = meta[0:8, :]
    step = meta[8:16, :]
    cum_cols = cols[:, 0:8]
    scores = contract(maps[:, 128:256], maps[:, 0:128], ((1,), (1,)))
    lower = lax.broadcasted_iota(jnp.int32, (half, half), 0) >= lax.broadcasted_iota(
        jnp.int32, (half, half), 1
    )
    scores = jnp.where(lower, scores, 0.0)
    for head in range(4):
        lanes = slice(128 * head, 128 * head + 128)
        x = streams[:, lanes]
        gaps = cum_cols[:, head : head + 1] - cumulative[head : head + 1]
        weights = jnp.exp(jnp.where(lower, gaps, 0.0)) * scores * step[head : head + 1]
        y = jnp.dot(weights.astype(BF16), x, preferred_element_type=F32)
        through = jnp.sum(params[7:8, lanes], 1, keepdims=True) * (1.0 / 32)
        out[:, lanes] = y + through * x.astype(F32)


def inside(streams, maps, meta, cols, params):
    return pl.pallas_call(
        inside_body,
        out_shape=jax.ShapeDtypeStruct(streams.shape, F32),
        name="inside",
    )(streams, maps, meta, cols, params)


def gate_body(kept, received, local, maps, cols, params, partner, *others_and_out):
    *others, out = others_and_out
    half = local.shape[0]
    section = lax.axis_index("segment")
    late = lax.axis_index("tensor") % 2 == 1
    prior = jnp.zeros((128, 512), F32)
    for source in range(len(others)):
        bits = jnp.bitwise_xor(section, source)
        piece = others[0][...]
        for index in range(1, len(others)):
            piece = jnp.where(bits == index + 1, others[index][...], piece)
        piece = piece.astype(F32)
        prior = jnp.where(source < section, piece[128:129] * prior + piece[0:128], prior)
    before = partner[...].astype(F32)
    prior = jnp.where(late, before[128:129] * prior + before[0:128], prior)
    scale = cols[:, 16:17]
    entry = jnp.exp(cols[:, 0:8])
    across = jnp.dot(maps[:, 128:256], prior.astype(BF16), preferred_element_type=F32)
    gated = []
    squares = jnp.zeros((half, 1), F32)
    for head in range(4):
        lanes = slice(128 * head, 128 * head + 128)
        y = local[:, lanes] + entry[:, head : head + 1] * across[:, lanes]
        gates = kept[:, lanes].astype(F32) + received[:, lanes].astype(F32)
        value = y * silu(gates * scale)
        squares = squares + jnp.sum(value * value, -1, keepdims=True)
        gated.append(value)
    norm = lax.rsqrt(squares / 512 + EPS)
    for head in range(4):
        lanes = slice(128 * head, 128 * head + 128)
        out[:, lanes] = (gated[head] * norm * params[4:5, lanes]).astype(BF16)


def gate(local, *operands):
    return pl.pallas_call(
        gate_body, out_shape=jax.ShapeDtypeStruct(local.shape, BF16), name="gate"
    )(*operands[:2], local, *operands[2:])


def per_device_halves(
    text_embed, crop_feats, crop_dest, vision_gain, proj_weight, newline, norm_gain, xz_weight,
    dt_weight, bc_weight, conv_x, conv_bc, dt_bias, a_log, skip, out_gain, out_weight,
):
    my_chip = lax.axis_index("tensor")
    segment_count = lax.axis_size("segment")
    text = text_embed[0]
    section, columns = text.shape
    half = section // 2
    width = columns * lax.axis_size("tensor")
    feats = crop_feats[0, 0, 0]
    feats_other = swapped(feats, "dp", 1)
    text_other = swapped(text[half:], "dp", 1)
    crops, rows, keep_x, send_x, keep, send = enter(
        crop_dest.transpose(0, 2, 1), dt_bias, a_log, skip, feats, feats_other, vision_gain,
        proj_weight, text, text_other, newline, norm_gain, xz_weight, bc_weight, dt_weight.T,
        conv_x, out_gain,
    )
    out_weight, newline, rows = lax.optimization_barrier((out_weight, newline, rows))
    lower = my_chip < 2

    def added(keep, arrived):
        pair = keep.astype(F32) + arrived.astype(F32)
        leaves = jnp.where(lower, pair[1], pair[0]).astype(BF16)
        return leaves, jnp.where(lower, pair[0], pair[1]).astype(BF16)

    keep_gates, send_gates = gates(rows, xz_weight)
    leaves, kept = added(keep, swapped(send, "tensor", 1))
    leaves, kept, send_gates = lax.optimization_barrier((leaves, kept, send_gates))
    received = swapped(leaves, "tensor", 2)
    leaves_x, kept_x = added(keep_x, swapped(send_x, "tensor", 1))
    leaves_x, kept_x, send_gates, received, out_weight, newline = lax.optimization_barrier(
        (leaves_x, kept_x, send_gates, received, out_weight, newline)
    )
    received_x = swapped(leaves_x, "tensor", 2)
    arrived_gates = swapped(send_gates, "tensor", 1)
    weight_other = swapped(out_weight, "dp", 1)
    weights = (
        jnp.where(lower, out_weight, weight_other), jnp.where(lower, weight_other, out_weight)
    )
    late = my_chip % 2 == 1
    head = crops[:half]
    tail = jnp.where(jnp.arange(half)[:, None] == 0, newline[None], text[half:])
    hidden = (jnp.where(late, tail, head), jnp.where(late, head, tail))
    kept_x, received_x, weights, hidden = lax.optimization_barrier(
        (kept_x, received_x, weights, hidden)
    )
    route = [(i, i + 1) for i in range(0, 4 * segment_count, 2)]
    route += [(i, i + 3) for i in range(1, 4 * segment_count - 4, 2)]
    ends = (kept[half - 8 :].astype(F32) + received[half - 8 :].astype(F32)).astype(BF16)
    before = slice(half - 8, half + 8)
    before = (kept_x[before].astype(F32) + received_x[before].astype(F32)).astype(BF16)
    before = jnp.concatenate([before, jnp.pad(ends, ((0, 8), (0, 0)))], 1)
    before = lax.ppermute(before, ("segment", "tensor"), route)
    streams, maps, meta, as_columns, state, params = scan(
        width, kept_x, received_x, kept, received, before, conv_bc
    )
    meta, keep_gates = lax.optimization_barrier((meta, keep_gates))
    local = inside(streams, maps, meta, as_columns, params)
    partner = swapped(state, "tensor", 1)
    whole = join(state, partner)
    whole, local = lax.optimization_barrier((whole, local))
    others = [swapped(whole, "segment", bits) for bits in range(1, segment_count)]
    leaves, kept = added(keep_gates, arrived_gates)
    received = swapped(leaves, "tensor", 2)
    normed = gate(local, kept, received, maps, as_columns, params, partner, *others)
    near, far, here = (
        lax.ppermute(
            normed, ("dp", "tensor"), [(i, (i if i % 4 < 2 else i ^ 4) ^ bits) for i in range(8)]
        )
        for bits in (1, 2, 0)
    )
    both = swapped(far, "tensor", 1)
    out = jnp.zeros((section, columns), BF16)
    for index, pair in enumerate(((here, far), (near, both))):
        mixed = jnp.dot(pair[0], weights[0], preferred_element_type=F32)
        mixed = mixed + jnp.dot(pair[1], weights[1], preferred_element_type=F32)
        block = (hidden[index].astype(F32) + mixed).astype(BF16)
        start = jnp.where(late, half, 0) if index == 0 else jnp.where(late, 0, half)
        out = lax.dynamic_update_slice(out, block, (start, 0))
    return out[None]


def per_device(*args):
    text_embed, crop_feats = args[0], args[1]
    sizes = tuple(lax.axis_size(axis) for axis in ("segment", "dp", "tensor"))
    heads_dev = args[12].shape[0]
    head_width = args[15].shape[0] // heads_dev
    state_size = args[9].shape[1] // 2
    fits = (
        sizes == (4, 2, 4)
        and heads_dev == 1
        and (head_width, state_size) == (128, 128)
        and crop_feats.shape[2:4] == (1, 256)
        and text_embed.shape[1] == 512
    )
    return (per_device_halves if fits else per_device_any)(*args)


def solution(mesh):
    return jax.shard_map(
        per_device,
        mesh=mesh,
        in_specs=(
            P("dp", "segment", "tensor"),
            P("segment", "dp", None, None, None),
            P("segment", None, None),
            P(),
            P(None, "tensor"),
            P("tensor"),
            P("tensor"),
            P("tensor", "dp"),
            P("tensor", "dp"),
            P("tensor", "dp"),
            P(None, ("dp", "tensor")),
            P(None, "dp"),
            P(("dp", "tensor")),
            P(("dp", "tensor")),
            P(("dp", "tensor")),
            P(("dp", "tensor")),
            P("dp", "tensor"),
        ),
        out_specs=P("dp", "segment", "tensor"),
        check_vma=False,
    )
```

```python
import jax
import jax.numpy as jnp
from jax import lax
from jax.experimental import pallas as pl
from jax.experimental.pallas import tpu as pltpu
from jax.sharding import PartitionSpec as P

EPS = 1e-05
F32 = jnp.float32
BF16 = jnp.bfloat16
HIGHEST = lax.Precision.HIGHEST


def passed_along(block, axis, distance):
    devices = range(lax.axis_size(axis))
    route = [(i - distance, i) for i in devices if i - distance in devices]
    return lax.ppermute(block, axis, route)


def swapped(block, axis, bits):
    return lax.ppermute(block, axis, [(i, i ^ bits) for i in range(lax.axis_size(axis))])


def per_device_any(
    text_embed,
    crop_feats,
    crop_dest,
    vision_gain,
    proj_weight,
    newline,
    norm_gain,
    xz_weight,
    dt_weight,
    bc_weight,
    conv_x,
    conv_bc,
    dt_bias,
    a_log,
    skip,
    out_gain,
    out_weight,
):
    highest = lax.Precision.HIGHEST
    eps = 1e-05
    dp_count = lax.axis_size("dp")
    tp_count = lax.axis_size("tensor")
    segment_count = lax.axis_size("segment")
    my_rank = lax.axis_index("dp")
    section = text_embed.shape[1]
    columns = text_embed.shape[2]
    crop_count = crop_feats.shape[2]
    crop_rows = crop_feats.shape[3]
    crop_span = crop_rows + 1
    heads_dev = dt_bias.shape[0]
    head_width = out_gain.shape[0] // heads_dev
    state_size = bc_weight.shape[1] // 2
    feats = crop_feats[0, 0].astype(jnp.float32)
    vision = (
        feats
        * lax.rsqrt(jnp.mean(feats * feats, -1, keepdims=True) + eps)
        * vision_gain.astype(jnp.float32)
    ).astype(jnp.bfloat16)
    encoded = jnp.dot(
        vision.reshape(crop_count * crop_rows, -1), proj_weight, preferred_element_type=jnp.float32
    )
    encoded = encoded.astype(jnp.bfloat16).reshape(crop_count, crop_rows, columns)
    table = crop_dest[0]
    sources = jnp.arange(dp_count, dtype=jnp.int32)
    mine = jnp.sum(jnp.where(sources[:, None] == my_rank, table, 0), axis=0)
    chosen = mine[None, :] == sources[:, None]
    outgoing = jnp.einsum(
        "dc,crq->drq", chosen.astype(jnp.bfloat16), encoded, preferred_element_type=jnp.float32
    ).astype(jnp.bfloat16)
    incoming = lax.all_to_all(outgoing, "dp", split_axis=0, concat_axis=0, tiled=True)
    sent_rows = incoming.shape[1]
    valid = jnp.any(table == my_rank, axis=1).astype(jnp.int32)
    order = jnp.cumsum(valid) - valid
    counted = jnp.sum(valid)
    positions = jnp.arange(section, dtype=jnp.int32)
    block = positions // crop_span
    within = positions % crop_span
    slot_ids = jnp.arange(section // crop_span + 1, dtype=jnp.int32)
    matched = (valid[None, :] == 1) & (order[None, :] == slot_ids[:, None])
    slot_source = jnp.sum(jnp.where(matched, sources[None, :], 0), axis=1)
    row_source = jnp.sum(
        jnp.where(block[:, None] == slot_ids[None, :], slot_source[None, :], 0), axis=1
    )
    row_index = row_source * sent_rows + jnp.minimum(within, sent_rows - 1)
    picked = jnp.take(incoming.reshape(dp_count * sent_rows, columns), row_index, axis=0)
    image = block < counted
    text = text_embed[0]
    crop_pos = image & (within < crop_rows)
    line_pos = image & (within == crop_rows)
    hidden = jnp.where(
        crop_pos[:, None], picked, jnp.where(line_pos[:, None], newline[None, :], text)
    )
    wide = hidden.astype(jnp.float32)
    row_total = lax.psum(jnp.sum(wide * wide, -1), "tensor")
    normed = (
        wide
        * lax.rsqrt(row_total / (columns * tp_count) + eps)[:, None]
        * norm_gain.astype(jnp.float32)
    ).astype(jnp.bfloat16)
    pair_cols = xz_weight.shape[1]
    step_cols = dt_weight.shape[1]
    piece = lax.all_gather(normed, "dp", axis=0, tiled=True)
    terms = jnp.concatenate(
        [
            jnp.dot(piece, xz_weight, preferred_element_type=jnp.float32),
            jnp.dot(piece, dt_weight, preferred_element_type=jnp.float32),
            jnp.dot(piece, bc_weight, preferred_element_type=jnp.float32),
        ],
        axis=1,
    )
    pair_mine, step_mine = (
        lax.psum_scatter(
            terms[:, :pair_cols].astype(jnp.bfloat16), "tensor", scatter_dimension=1, tiled=True
        ).astype(jnp.float32),
        lax.psum_scatter(
            terms[:, pair_cols : pair_cols + step_cols].astype(jnp.bfloat16),
            "tensor",
            scatter_dimension=1,
            tiled=True,
        ).astype(jnp.float32),
    )
    map_terms = terms[:, pair_cols + step_cols :]
    maps_all = lax.psum(map_terms.astype(jnp.bfloat16), "tensor").astype(jnp.float32)
    pairs = pair_mine.reshape(dp_count, section, heads_dev, 2, head_width)
    values = pairs[:, :, :, 0, :].reshape(dp_count, section, heads_dev * head_width)
    gates = pairs[:, :, :, 1, :]
    fresh = jnp.concatenate([values, maps_all.reshape(dp_count, section, 2 * state_size)], axis=2)
    kernel = jnp.concatenate([conv_x, conv_bc], axis=1).astype(jnp.float32)
    taps = kernel.shape[0]
    edge = passed_along(fresh[:, section - (taps - 1) :, :], "segment", 1)
    padded = jnp.concatenate([edge, fresh], axis=1)
    filtered = kernel[0] * padded[:, 0:section]
    for offset in range(1, taps):
        filtered = filtered + kernel[offset] * padded[:, offset : offset + section]
    activated = jax.nn.silu(filtered)
    inner_cols = heads_dev * head_width
    streams = activated[..., :inner_cols].reshape(dp_count, section, heads_dev, head_width)
    b_rows = activated[..., inner_cols : inner_cols + state_size]
    c_rows = activated[..., inner_cols + state_size :]
    step = jax.nn.softplus(step_mine.reshape(dp_count, section, heads_dev) + dt_bias)
    cumulative = jnp.cumsum(-jnp.exp(a_log) * step, axis=1)
    scores = jnp.einsum("nls,nms->nlm", c_rows, b_rows, precision=highest)
    mask = (positions[:, None] >= positions[None, :])[None, :, :, None]
    gaps = cumulative[:, :, None, :] - cumulative[:, None, :, :]
    weights = (
        jnp.where(mask, jnp.exp(jnp.where(mask, gaps, 0.0)), 0.0)
        * scores[..., None]
        * step[:, None, :, :]
    )
    inside = jnp.einsum("nlmh,nmhp->nlhp", weights, streams, precision=highest)
    final = cumulative[:, -1, :]
    carry_weight = jnp.exp(final[:, None, :] - cumulative) * step
    local_state = jnp.einsum("nlh,nls,nlhp->nhsp", carry_weight, b_rows, streams, precision=highest)
    decay = jnp.exp(final)
    prior = jnp.zeros_like(local_state)
    for turn in range(segment_count - 1):
        prior = passed_along(
            (decay[:, :, None, None] * prior + local_state).astype(jnp.bfloat16), "segment", 1
        ).astype(jnp.float32)
    across = jnp.exp(cumulative)[..., None] * jnp.einsum(
        "nls,nhsp->nlhp", c_rows, prior, precision=highest
    )
    outputs = inside + across + skip[None, None, :, None] * streams
    gated = outputs * jax.nn.silu(gates)
    group_total = lax.psum(jnp.sum(gated * gated, axis=(2, 3)), "tensor")
    scale = lax.rsqrt(group_total / (inner_cols * tp_count) + eps)
    normed_out = (
        gated * scale[..., None, None] * out_gain.astype(jnp.float32).reshape(heads_dev, head_width)
    ).astype(jnp.bfloat16)
    normed_out = normed_out.reshape(dp_count * section, inner_cols)
    term = jnp.dot(
        lax.all_gather(normed_out, "tensor", axis=1, tiled=True),
        out_weight,
        preferred_element_type=jnp.float32,
    )
    mixed = lax.psum_scatter(
        term.astype(jnp.bfloat16), "dp", scatter_dimension=0, tiled=True
    ).astype(jnp.float32)
    return (wide + mixed).astype(jnp.bfloat16)[None]


def contract(a, b, dims, precision=None):
    return lax.dot_general(
        a, b, (dims, ((), ())), precision=precision, preferred_element_type=F32
    )


def eye(n):
    return (
        lax.broadcasted_iota(jnp.int32, (n, n), 0) == lax.broadcasted_iota(jnp.int32, (n, n), 1)
    ).astype(F32)


def columns_of(rows):
    return contract(eye(rows.shape[1]), rows, ((1,), (1,)), HIGHEST)


def silu(a):
    return a / (1.0 + jnp.exp(-a))


def enter_body(
    table, dt_bias, a_log, skip, feats_mine, feats_other, vision_gain, proj, text, text_other,
    newline, gain, xz, bc, dt, conv_x, out_gain,
    crops_out, rows_out, keep_x_out, send_x_out, keep_out, send_out,
    feats, normed, proj_tiles, tails, weights, crops, rows, first, maps, sems, out_sems,
):
    half = tails.shape[1]
    tiles, _, tile = proj_tiles.shape
    columns = rows.shape[1]
    load_feats = [
        pltpu.make_async_copy(feats_mine, feats.at[0], sems.at[0]),
        pltpu.make_async_copy(feats_other, feats.at[1], sems.at[1]),
    ]
    load_proj = [
        pltpu.make_async_copy(proj.at[:, pl.ds(i * tile, tile)], proj_tiles.at[i], sems.at[2 + i])
        for i in range(tiles)
    ]
    load_tails = [
        pltpu.make_async_copy(text.at[pl.ds(half, half), :], tails.at[0], sems.at[2 + tiles]),
        pltpu.make_async_copy(text_other, tails.at[1], sems.at[3 + tiles]),
    ]
    load_weights = [
        pltpu.make_async_copy(
            xz.at[:, pl.ds(i * 256, 128)],
            weights.at[i // 2, :, pl.ds(i % 2 * 128, 128)],
            sems.at[4 + tiles + i],
        )
        for i in range(4)
    ]
    load_weights.append(pltpu.make_async_copy(bc, weights.at[2], sems.at[8 + tiles]))
    for copy in load_feats + load_proj[:2] + load_tails + load_proj[2:] + load_weights:
        copy.start()
    gain_row = gain[...].reshape(1, -1)
    rank = lax.axis_index("dp")
    stays = table[0, 0, rank] == rank
    load_feats[0].wait()
    load_feats[1].wait()
    for index in range(2):
        block = jnp.where(stays, feats[index], feats[1 - index]).astype(F32)
        scale = lax.rsqrt(jnp.mean(block * block, -1, keepdims=True) + EPS)
        normed[index * half : (index + 1) * half, :] = (
            block * scale * vision_gain[...].reshape(1, -1).astype(F32)
        ).astype(BF16)
    ones = jnp.ones((8, 128), BF16)

    def folded(block):
        total = jnp.zeros((block.shape[0], 128), F32)
        for start in range(0, block.shape[1], 128):
            piece = block[:, start : start + 128].astype(F32)
            total = total + piece * piece
        return total

    squares = [None] * 4
    for i in range(tiles):
        load_proj[i].wait()
        cols = slice(i * tile, (i + 1) * tile)
        result = jnp.dot(normed[...], proj_tiles[i], preferred_element_type=F32).astype(BF16)
        crops[:, cols] = result
        scaled = result * gain_row[:, cols]
        rows[0:half, cols] = scaled[:half]
        rows[2 * half : 3 * half, cols] = scaled[half:]
        for index in range(2):
            more = folded(result[index * half : (index + 1) * half])
            squares[2 * index] = more if i == 0 else squares[2 * index] + more
        if i < 2:
            load_tails[i].wait()
            head = tails[i, 0:8, :].astype(F32)
            line = newline[...].reshape(1, -1).astype(F32)
            top = lax.broadcasted_iota(jnp.int32, (8, 1), 0) == 0
            tails[i, 0:8, :] = jnp.where(top, line, head).astype(BF16)
            main = tails[i]
            base = (2 * i + 1) * half
            rows[base : base + half, :] = main * gain_row
            squares[2 * i + 1] = folded(main)
    departures = [
        pltpu.make_async_copy(crops, crops_out, out_sems.at[0]),
        pltpu.make_async_copy(rows, rows_out, out_sems.at[1]),
    ]
    for copy in departures:
        copy.start()
    for copy in load_weights:
        copy.wait()
    chip = lax.axis_index("tensor")
    lane = lax.broadcasted_iota(jnp.int32, (1, 128), 1)
    own = [conv_x[...].astype(F32), out_gain[...].reshape(1, 128).astype(F32)]
    for value in (dt_bias[0], a_log[0], skip[0]):
        whole = jnp.full((1, 128), value, F32)
        high = whole.astype(BF16).astype(F32)
        middle = (whole - high).astype(BF16).astype(F32)
        low = whole - high - middle
        pieces = jnp.where(lane < 32, high, jnp.where(lane < 64, middle, low))
        own.append(jnp.where(lane < 96, pieces, 0.0))
    own = jnp.concatenate(own, 0)
    slots = jnp.concatenate([jnp.where(chip == slot, own, 0.0) for slot in range(4)], 1)

    def parted(source, keep, send, part, sem):
        goes = pltpu.make_async_copy(source.at[part], send.at[part // 2], sem)
        remains = pltpu.make_async_copy(source.at[part], keep.at[part // 2], sem)
        here = chip % 2 == part % 2
        pl.when(here)(remains.start)
        pl.when(jnp.logical_not(here))(goes.start)
        departures.append(goes)

    for part in range(4):
        main = rows[part * half : (part + 1) * half, :]
        maps[part] = jnp.dot(main, weights[2], preferred_element_type=F32).astype(BF16)
        parted(maps, keep_out, send_out, part, out_sems.at[6 + part])
    for part in range(4):
        main = rows[part * half : (part + 1) * half, :]
        for i in range(2):
            first[part, 0:half, i * 256 : i * 256 + 256] = jnp.dot(
                main, weights[i], preferred_element_type=F32
            ).astype(BF16)
        steps = contract(dt[...], main, ((1,), (1,)))
        sums = contract(ones, squares[part].astype(BF16), ((1,), (1,)))
        sums = jnp.concatenate([steps[0:4], sums[0:4]], 0)
        sums = jnp.concatenate([sums, jnp.zeros((8, 512 - half), F32)], 1)
        first[part, half : half + 16, :] = jnp.concatenate([sums, slots], 0).astype(BF16)
        parted(first, keep_x_out, send_x_out, part, out_sems.at[2 + part])
    for copy in departures:
        copy.wait()


def enter(
    table, dt_bias, a_log, skip, feats_mine, feats_other, vision_gain, proj, text, text_other,
    newline, gain, xz, bc, dt, conv_x, out_gain,
):
    half, vision = feats_mine.shape
    columns = text.shape[1]
    tiles = 4
    whole = pl.BlockSpec(memory_space=pl.ANY)
    near = pl.BlockSpec(memory_space=pltpu.VMEM)
    return pl.pallas_call(
        enter_body,
        in_specs=[pl.BlockSpec(memory_space=pltpu.SMEM)] * 4
        + [whole, whole, near, whole, whole, whole]
        + [near, near, whole, whole, near, near, near],
        out_specs=[whole] * 6,
        out_shape=[
            jax.ShapeDtypeStruct((2 * half, columns), BF16),
            jax.ShapeDtypeStruct((4 * half, columns), BF16),
            jax.ShapeDtypeStruct((2, half + 16, 512), BF16),
            jax.ShapeDtypeStruct((2, half + 16, 512), BF16),
            jax.ShapeDtypeStruct((2, half, 256), BF16),
            jax.ShapeDtypeStruct((2, half, 256), BF16),
        ],
        scratch_shapes=[
            pltpu.VMEM((2, half, vision), BF16),
            pltpu.VMEM((2 * half, vision), BF16),
            pltpu.VMEM((tiles, vision, columns // tiles), BF16),
            pltpu.VMEM((2, half, columns), BF16),
            pltpu.VMEM((3, columns, 256), BF16),
            pltpu.VMEM((2 * half, columns), BF16),
            pltpu.VMEM((4 * half, columns), BF16),
            pltpu.VMEM((4, half + 16, 512), BF16),
            pltpu.VMEM((4, half, 256), BF16),
            pltpu.SemaphoreType.DMA((9 + tiles,)),
            pltpu.SemaphoreType.DMA((10,)),
        ],
        name="enter",
    )(
        table, dt_bias, a_log, skip, feats_mine, feats_other, vision_gain, proj, text, text_other,
        newline, gain, xz, bc, dt, conv_x, out_gain,
    )


def gates_body(rows_hbm, xz, keep_out, send_out, rows, weights, results, sems, out_sems):
    half = results.shape[1]
    chip = lax.axis_index("tensor")
    load_weights = [
        pltpu.make_async_copy(
            xz.at[:, pl.ds(i * 256 + 128, 128)],
            weights.at[i // 2, :, pl.ds(i % 2 * 128, 128)],
            sems.at[4 + i],
        )
        for i in range(4)
    ]
    load_rows = [
        pltpu.make_async_copy(rows_hbm.at[pl.ds(part * half, half), :], rows.at[part], sems.at[part])
        for part in range(4)
    ]
    for copy in load_rows[:1] + load_weights + load_rows[1:]:
        copy.start()
    departures = []
    for part in range(4):
        load_rows[part].wait()
        for i in range(2):
            if part == 0:
                load_weights[2 * i].wait()
                load_weights[2 * i + 1].wait()
            results[part, :, 256 * i : 256 * i + 256] = jnp.dot(
                rows[part], weights[i], preferred_element_type=F32
            ).astype(BF16)
        goes = pltpu.make_async_copy(results.at[part], send_out.at[part // 2], out_sems.at[part])
        remains = pltpu.make_async_copy(results.at[part], keep_out.at[part // 2], out_sems.at[part])
        here = chip % 2 == part % 2
        pl.when(here)(remains.start)
        pl.when(jnp.logical_not(here))(goes.start)
        departures.append(goes)
    for copy in departures:
        copy.wait()


def gates(rows, xz):
    half, columns = rows.shape[0] // 4, rows.shape[1]
    whole = pl.BlockSpec(memory_space=pl.ANY)
    return pl.pallas_call(
        gates_body,
        in_specs=[whole, whole],
        out_specs=[whole, whole],
        out_shape=[jax.ShapeDtypeStruct((2, half, 512), BF16)] * 2,
        scratch_shapes=[
            pltpu.VMEM((4, half, columns), BF16),
            pltpu.VMEM((2, columns, 256), BF16),
            pltpu.VMEM((4, half, 512), BF16),
            pltpu.SemaphoreType.DMA((8,)),
            pltpu.SemaphoreType.DMA((4,)),
        ],
        name="gates",
    )(rows, xz)


def filtered(main, edge, taps):
    rows = main.shape[0]
    padded = jnp.concatenate([edge, main], 0)
    count = taps.shape[0]
    total = taps[count - 1 : count] * main
    for back in range(1, count):
        total = total + taps[count - 1 - back : count - back] * padded[8 - back : 8 - back + rows]
    return total


def scan_body(
    width, kept_x, received_x, kept, received, before, taps_maps, streams, maps, meta, cols, state, params
):
    first = kept_x[...].astype(F32) + received_x[...].astype(F32)
    half = first.shape[0] - 16
    slots = first[half + 8 : half + 16]
    params[...] = slots
    sums = first[half : half + 8, 0:half]
    scale = lax.rsqrt(sums[4:5] / width + EPS)
    sums_before = before[8:16, half - 128 : half].astype(F32)
    scale_before = lax.rsqrt(sums_before[4:5] / width + EPS)
    head = lax.broadcasted_iota(jnp.int32, (8, 512), 1) // 128
    owner = (head == lax.broadcasted_iota(jnp.int32, (8, 512), 0)).astype(F32)
    scalars = slots[5:8]
    bias = jnp.sum(owner * scalars[0:1], 1, keepdims=True) * (1.0 / 32)
    rate = jnp.sum(owner * scalars[1:2], 1, keepdims=True) * (1.0 / 32)
    raw = sums * scale + bias
    step = jnp.maximum(raw, 0.0) + jnp.log1p(jnp.exp(-jnp.abs(raw)))
    decays = -jnp.exp(rate) * step
    upper = (
        lax.broadcasted_iota(jnp.int32, (half, half), 0)
        <= lax.broadcasted_iota(jnp.int32, (half, half), 1)
    ).astype(F32)
    cumulative = contract(decays, upper, ((1,), (0,)), HIGHEST)
    final = cumulative[:, half - 1 : half]
    carry = jnp.exp(final - cumulative) * step
    wide = jnp.concatenate([scale_before, jnp.zeros((1, half - 128), F32)], 1)
    columns = columns_of(
        jnp.concatenate(
            [cumulative, carry] + [jnp.broadcast_to(row, (8, half)) for row in (scale, wide)], 0
        )
    )
    cols[...] = columns
    scale_main = columns[:, 16:17]
    scale_edge = columns[120:128, 24:25]
    taps_x = slots[0:4]
    edge = before[0:8, :].astype(F32) * scale_edge
    x = silu(filtered(first[0:half] * scale_main, edge[:, 0:512], taps_x))
    both = silu(
        filtered(
            (kept[...].astype(F32) + received[...].astype(F32)) * scale_main,
            edge[:, 512:768],
            taps_maps[...].astype(F32),
        )
    ).astype(BF16)
    carried = jnp.concatenate(
        [jnp.broadcast_to(columns[:, 8 + h : 9 + h], (half, 128)) for h in range(4)], 1
    )
    state[0:128, :] = contract(both[:, 0:128], (x * carried).astype(BF16), ((0,), (0,))).astype(BF16)
    total = jnp.sum(jnp.exp(final) * owner, 0, keepdims=True)
    state[128:136, :] = jnp.broadcast_to(total, (8, 512)).astype(BF16)
    streams[...] = x.astype(BF16)
    maps[...] = both
    meta[0:8, :] = cumulative
    meta[8:16, :] = step


def scan(width, *operands):
    half = operands[2].shape[0]
    return pl.pallas_call(
        lambda *refs: scan_body(width, *refs),
        out_shape=[
            jax.ShapeDtypeStruct((half, 512), BF16),
            jax.ShapeDtypeStruct((half, 256), BF16),
            jax.ShapeDtypeStruct((16, half), F32),
            jax.ShapeDtypeStruct((half, 32), F32),
            jax.ShapeDtypeStruct((136, 512), BF16),
            jax.ShapeDtypeStruct((8, 512), F32),
        ],
        name="scan",
    )(*operands)


def join(state, partner):
    late = lax.axis_index("tensor") % 2 == 1
    first = jnp.where(late, partner, state).astype(F32)
    second = jnp.where(late, state, partner).astype(F32)
    decay = lax.broadcasted_iota(jnp.int32, state.shape, 0) >= 128
    return jnp.where(decay, first * second, second[128:129] * first + second).astype(BF16)


def inside_body(streams, maps, meta, cols, params, out):
    half = streams.shape[0]
    cumulative = meta[0:8, :]
    step = meta[8:16, :]
    cum_cols = cols[:, 0:8]
    scores = contract(maps[:, 128:256], maps[:, 0:128], ((1,), (1,)))
    lower = lax.broadcasted_iota(jnp.int32, (half, half), 0) >= lax.broadcasted_iota(
        jnp.int32, (half, half), 1
    )
    scores = jnp.where(lower, scores, 0.0)
    for head in range(4):
        lanes = slice(128 * head, 128 * head + 128)
        x = streams[:, lanes]
        gaps = cum_cols[:, head : head + 1] - cumulative[head : head + 1]
        weights = jnp.exp(jnp.where(lower, gaps, 0.0)) * scores * step[head : head + 1]
        y = jnp.dot(weights.astype(BF16), x, preferred_element_type=F32)
        through = jnp.sum(params[7:8, lanes], 1, keepdims=True) * (1.0 / 32)
        out[:, lanes] = y + through * x.astype(F32)


def inside(streams, maps, meta, cols, params):
    return pl.pallas_call(
        inside_body,
        out_shape=jax.ShapeDtypeStruct(streams.shape, F32),
        name="inside",
    )(streams, maps, meta, cols, params)


def gate_body(kept, received, local, maps, cols, params, partner, *others_and_out):
    *others, out = others_and_out
    half = local.shape[0]
    section = lax.axis_index("segment")
    late = lax.axis_index("tensor") % 2 == 1
    prior = jnp.zeros((128, 512), F32)
    for source in range(len(others)):
        bits = jnp.bitwise_xor(section, source)
        piece = others[0][...]
        for index in range(1, len(others)):
            piece = jnp.where(bits == index + 1, others[index][...], piece)
        piece = piece.astype(F32)
        prior = jnp.where(source < section, piece[128:129] * prior + piece[0:128], prior)
    before = partner[...].astype(F32)
    prior = jnp.where(late, before[128:129] * prior + before[0:128], prior)
    scale = cols[:, 16:17]
    entry = jnp.exp(cols[:, 0:8])
    across = jnp.dot(maps[:, 128:256], prior.astype(BF16), preferred_element_type=F32)
    gated = []
    squares = jnp.zeros((half, 1), F32)
    for head in range(4):
        lanes = slice(128 * head, 128 * head + 128)
        y = local[:, lanes] + entry[:, head : head + 1] * across[:, lanes]
        gates = kept[:, lanes].astype(F32) + received[:, lanes].astype(F32)
        value = y * silu(gates * scale)
        squares = squares + jnp.sum(value * value, -1, keepdims=True)
        gated.append(value)
    norm = lax.rsqrt(squares / 512 + EPS)
    for head in range(4):
        lanes = slice(128 * head, 128 * head + 128)
        out[:, lanes] = (gated[head] * norm * params[4:5, lanes]).astype(BF16)


def gate(local, *operands):
    return pl.pallas_call(
        gate_body, out_shape=jax.ShapeDtypeStruct(local.shape, BF16), name="gate"
    )(*operands[:2], local, *operands[2:])


def per_device_halves(
    text_embed, crop_feats, crop_dest, vision_gain, proj_weight, newline, norm_gain, xz_weight,
    dt_weight, bc_weight, conv_x, conv_bc, dt_bias, a_log, skip, out_gain, out_weight,
):
    my_chip = lax.axis_index("tensor")
    segment_count = lax.axis_size("segment")
    text = text_embed[0]
    section, columns = text.shape
    half = section // 2
    width = columns * lax.axis_size("tensor")
    feats = crop_feats[0, 0, 0]
    feats_other = swapped(feats, "dp", 1)
    text_other = swapped(text[half:], "dp", 1)
    crops, rows, keep_x, send_x, keep, send = enter(
        crop_dest.transpose(0, 2, 1), dt_bias, a_log, skip, feats, feats_other, vision_gain,
        proj_weight, text, text_other, newline, norm_gain, xz_weight, bc_weight, dt_weight.T,
        conv_x, out_gain,
    )
    out_weight, newline, rows = lax.optimization_barrier((out_weight, newline, rows))
    lower = my_chip < 2

    def added(keep, arrived):
        pair = keep.astype(F32) + arrived.astype(F32)
        leaves = jnp.where(lower, pair[1], pair[0]).astype(BF16)
        return leaves, jnp.where(lower, pair[0], pair[1]).astype(BF16)

    keep_gates, send_gates = gates(rows, xz_weight)
    leaves, kept = added(keep, swapped(send, "tensor", 1))
    leaves, kept, send_gates = lax.optimization_barrier((leaves, kept, send_gates))
    received = swapped(leaves, "tensor", 2)
    leaves_x, kept_x = added(keep_x, swapped(send_x, "tensor", 1))
    leaves_x, kept_x, send_gates, received, out_weight, newline = lax.optimization_barrier(
        (leaves_x, kept_x, send_gates, received, out_weight, newline)
    )
    received_x = swapped(leaves_x, "tensor", 2)
    arrived_gates = swapped(send_gates, "tensor", 1)
    weight_other = swapped(out_weight, "dp", 1)
    weights = (
        jnp.where(lower, out_weight, weight_other), jnp.where(lower, weight_other, out_weight)
    )
    late = my_chip % 2 == 1
    head = crops[:half]
    tail = jnp.where(jnp.arange(half)[:, None] == 0, newline[None], text[half:])
    hidden = (jnp.where(late, tail, head), jnp.where(late, head, tail))
    kept_x, received_x, weights, hidden = lax.optimization_barrier(
        (kept_x, received_x, weights, hidden)
    )
    route = [(i, i + 1) for i in range(0, 4 * segment_count, 2)]
    route += [(i, i + 3) for i in range(1, 4 * segment_count - 4, 2)]
    ends = (kept[half - 8 :].astype(F32) + received[half - 8 :].astype(F32)).astype(BF16)
    before = slice(half - 8, half + 8)
    before = (kept_x[before].astype(F32) + received_x[before].astype(F32)).astype(BF16)
    before = jnp.concatenate([before, jnp.pad(ends, ((0, 8), (0, 0)))], 1)
    before = lax.ppermute(before, ("segment", "tensor"), route)
    streams, maps, meta, as_columns, state, params = scan(
        width, kept_x, received_x, kept, received, before, conv_bc
    )
    meta, keep_gates = lax.optimization_barrier((meta, keep_gates))
    local = inside(streams, maps, meta, as_columns, params)
    partner = swapped(state, "tensor", 1)
    whole = join(state, partner)
    others = [swapped(whole, "segment", bits) for bits in range(1, segment_count)]
    leaves, kept = added(keep_gates, arrived_gates)
    received = swapped(leaves, "tensor", 2)
    normed = gate(local, kept, received, maps, as_columns, params, partner, *others)
    near, far, here = (
        lax.ppermute(
            normed, ("dp", "tensor"), [(i, (i if i % 4 < 2 else i ^ 4) ^ bits) for i in range(8)]
        )
        for bits in (1, 2, 0)
    )
    both = swapped(far, "tensor", 1)
    out = jnp.zeros((section, columns), BF16)
    for index, pair in enumerate(((here, far), (near, both))):
        mixed = jnp.dot(pair[0], weights[0], preferred_element_type=F32)
        mixed = mixed + jnp.dot(pair[1], weights[1], preferred_element_type=F32)
        block = (hidden[index].astype(F32) + mixed).astype(BF16)
        start = jnp.where(late, half, 0) if index == 0 else jnp.where(late, 0, half)
        out = lax.dynamic_update_slice(out, block, (start, 0))
    return out[None]


def per_device(*args):
    text_embed, crop_feats = args[0], args[1]
    sizes = tuple(lax.axis_size(axis) for axis in ("segment", "dp", "tensor"))
    heads_dev = args[12].shape[0]
    head_width = args[15].shape[0] // heads_dev
    state_size = args[9].shape[1] // 2
    fits = (
        sizes == (4, 2, 4)
        and heads_dev == 1
        and (head_width, state_size) == (128, 128)
        and crop_feats.shape[2:4] == (1, 256)
        and text_embed.shape[1] == 512
    )
    return (per_device_halves if fits else per_device_any)(*args)


def solution(mesh):
    return jax.shard_map(
        per_device,
        mesh=mesh,
        in_specs=(
            P("dp", "segment", "tensor"),
            P("segment", "dp", None, None, None),
            P("segment", None, None),
            P(),
            P(None, "tensor"),
            P("tensor"),
            P("tensor"),
            P("tensor", "dp"),
            P("tensor", "dp"),
            P("tensor", "dp"),
            P(None, ("dp", "tensor")),
            P(None, "dp"),
            P(("dp", "tensor")),
            P(("dp", "tensor")),
            P(("dp", "tensor")),
            P(("dp", "tensor")),
            P("dp", "tensor"),
        ),
        out_specs=P("dp", "segment", "tensor"),
        check_vma=False,
    )
```
